32 devices in a mesh: fsdp: 2 (over x), context: 4 (over y, core), tensor: 4 (over z).
Axes of the slice: x: 2, y: 2, z: 4, core: 2. Of those that a mesh axis runs over, the one named last changes fastest.
Arguments:
- tokens: bfloat16 [4, 2560, 1024], P('fsdp', 'context'), may hold values from -6 to 6
- state: bfloat16 [4, 512, 1024], P('fsdp', 'context'), may hold values from -6 to 6
- parent: int32 [4, 20], P('fsdp'), may hold values from -1 to 11, as said below
- seg_length: int32 [4, 20], P('fsdp', 'context'), may hold values from 64 to 128, as said below
- cell_gate: float32 [1024], replicated, may hold values from 0.7 to 1
- norm1_gain: float32 [1024], replicated, may hold values from 0.5 to 1.5
- norm1_shift: float32 [1024], replicated, may hold values from -1.5 to 1.5
- w_query: bfloat16 [1024, 1024], P('fsdp', 'tensor'), may hold values from -0.1875 to 0.1875
- w_key: bfloat16 [1024, 1024], P('fsdp', 'tensor'), may hold values from -0.1875 to 0.1875
- w_value: bfloat16 [1024, 1024], P('fsdp', 'tensor'), may hold values from -0.1875 to 0.1875
- w_attn_out: bfloat16 [1024, 1024], P('tensor', 'fsdp'), may hold values from -0.75 to 0.75
- rel_bias: float32 [8, 32], P('tensor'), may hold values from -4 to 4
- norm2_gain: float32 [1024], replicated, may hold values from 0.5 to 1.5
- norm2_shift: float32 [1024], replicated, may hold values from -1.5 to 1.5
- w_in: bfloat16 [1024, 4096], P('fsdp', 'tensor'), may hold values from -0.1875 to 0.1875
- w_out: bfloat16 [4096, 1024], P('tensor', 'fsdp'), may hold values from -0.125 to 0.125
- cotangent: bfloat16 [4, 2560, 1024], P('fsdp', 'context'), may hold values from -6 to 6
Outputs:
- output: bfloat16 [4, 2560, 1024], P('fsdp', 'context')
- tokens_grad: bfloat16 [4, 2560, 1024], P('fsdp', 'context')
- state_grad: bfloat16 [4, 512, 1024], P('fsdp', 'context')
- grad_query: float32 [1024, 1024], P('fsdp', 'tensor')
- grad_key: float32 [1024, 1024], P('fsdp', 'tensor')
- grad_value: float32 [1024, 1024], P('fsdp', 'tensor')
- grad_attn_out: float32 [1024, 1024], P('tensor', 'fsdp')
- grad_rel_bias: float32 [8, 32], P('tensor')
- grad_norm1_gain: float32 [1024], replicated
- grad_norm1_shift: float32 [1024], replicated
- grad_norm2_gain: float32 [1024], replicated
- grad_norm2_shift: float32 [1024], replicated
- grad_in: float32 [1024, 4096], P('fsdp', 'tensor')
- grad_out: float32 [4096, 1024], P('tensor', 'fsdp')
- norms: float32 [3], replicated
The draws below stay inside these ranges and needn't reach their ends.
Inputs may be any that keep to these rules, and one draw needn't show every extreme that they name: Segments 0 to 7 form a trunk, each the child of the one before, segment 0 with parent -1; the next 4 segments are each a child of a trunk segment; each remaining segment is a child of one of those branches, 2 to each branch. `seg_length`: A segment's valid tokens are its first ones; every trunk and branch segment has 128; leaves have 128 // 2 or more.
All inputs are finite; a program needn't handle non-finite values.
Results may differ from the reference program's by a relative error of at most 0.022.
Values may be sent and summed in bfloat16 or wider, within the bound.
No kernel may reach another device: no remote copies, remote signals or barrier semaphores. Data moves between devices by JAX's collectives and lax.ppermute only.
A program may use at most 192 MiB of HBM per device.

```python
import math
import jax
import jax.numpy as jnp
from jax import lax

D = 1024
HEADS = 8
FF = 4096
WINDOW = 512
NSTATE = 512
BUCKETS = 32
REACH = 128
SEG = 128
TRUNK_SEG = 8
BRANCHES = 4
LEAVES = 2
NSEG = 20
NLEV = 5
TREES = 4


def draw_parent(key, part):
    keys_pair = jax.random.split(jax.random.fold_in(key, 11), 2)
    attach = jax.random.randint(keys_pair[0], (TREES, BRANCHES), TRUNK_SEG - 4, TRUNK_SEG)
    leaf_total = BRANCHES * LEAVES
    orders = jax.vmap(lambda tree_key: jax.random.permutation(tree_key, leaf_total))(jax.random.split(keys_pair[1], TREES))
    trunk_parent = jnp.broadcast_to(jnp.arange(TRUNK_SEG, dtype=jnp.int32)[None, :] - 1, (TREES, TRUNK_SEG))
    leaf_parent = TRUNK_SEG + orders // LEAVES
    return jnp.concatenate([trunk_parent, attach.astype(jnp.int32), leaf_parent.astype(jnp.int32)], axis=1).astype(jnp.int32)


def draw_seg_length(key, part):
    leaf_total = BRANCHES * LEAVES
    leaf_len = jax.random.randint(jax.random.fold_in(key, 23), (TREES, leaf_total), SEG // 2, SEG + 1)
    full_len = jnp.full((TREES, TRUNK_SEG + BRANCHES), SEG, jnp.int32)
    return jnp.concatenate([full_len, leaf_len.astype(jnp.int32)], axis=1).astype(jnp.int32)


def level_of(key, extent, shards, smallest, top_value):
    loudness, own = 1.0, jax.random.fold_in(key, 6)
    for dim, parts in shards:
        heights = jnp.exp(jax.random.uniform(jax.random.fold_in(own, dim), (parts,), jnp.float32, smallest / len(shards), top_value / len(shards)))
        loudness = loudness * jnp.repeat(heights, extent[dim] // parts).reshape([-1 if axis == dim else 1 for axis in range(len(extent))])
    return loudness


def centred(own_key, extent, spread, reach, cuts=(), held_as=jnp.bfloat16):
    entries = jax.random.normal(own_key, extent, jnp.float32) * spread
    if len(cuts) > 0:
        entries = level_of(own_key, extent, cuts, -0.22, 0.18) * entries
    return jnp.clip(entries, min=-reach, max=reach).astype(held_as)


def setup_inputs(seed: int = 0) -> dict:
    arg_keys = jax.random.split(jax.random.key(seed), 18)
    return {
        "tokens": centred(arg_keys[0], (TREES, NSEG * SEG, D), 1.0, 6.0, ((0, 2), (1, 4))),
        "state": centred(arg_keys[1], (TREES, NSTATE, D), 1.0, 6.0, ((0, 2), (1, 4))),
        "parent": draw_parent(jax.random.fold_in(arg_keys[17], 71), 0),
        "seg_length": draw_seg_length(jax.random.fold_in(arg_keys[17], 71), 0),
        "cell_gate": jnp.clip(jax.random.uniform(arg_keys[4], (D,), jnp.float32, 0.7, 1.0), 0.7, 1.0),
        "norm1_gain": jnp.clip(1.0 + 0.1 * jax.random.normal(arg_keys[5], (D,), jnp.float32), 0.5, 1.5),
        "norm1_shift": centred(arg_keys[6], (D,), 0.3, 1.5, (), jnp.float32),
        "w_query": centred(arg_keys[7], (D, D), D ** -0.5, 0.1875, ((0, 2), (1, 4))),
        "w_key": centred(arg_keys[8], (D, D), D ** -0.5, 0.1875, ((0, 2), (1, 4))),
        "w_value": centred(arg_keys[9], (D, D), D ** -0.5, 0.1875, ((0, 2), (1, 4))),
        "w_attn_out": centred(arg_keys[10], (D, D), (D // 16) ** -0.5, 0.75, ((0, 4), (1, 2))),
        "rel_bias": centred(arg_keys[11], (HEADS, BUCKETS), 1.0, 4.0, ((0, 4),), jnp.float32),
        "norm2_gain": jnp.clip(1.0 + 0.1 * jax.random.normal(arg_keys[12], (D,), jnp.float32), 0.5, 1.5),
        "norm2_shift": centred(arg_keys[13], (D,), 0.3, 1.5, (), jnp.float32),
        "w_in": centred(arg_keys[14], (D, FF), D ** -0.5, 0.1875, ((0, 2), (1, 4))),
        "w_out": centred(arg_keys[15], (FF, D), (FF // 2) ** -0.5, 0.125, ((0, 4), (1, 2))),
        "cotangent": centred(arg_keys[16], (TREES, NSEG * SEG, D), 1.0, 6.0, ((0, 2), (1, 4))),
    }


TOP_PRECISION = lax.Precision.HIGHEST
norm_epsilon = 1e-05
masked_score = -1e+30
gelu_coeff = 0.7978845608028654

@jax.custom_vjp
def low(v):
    return lax.optimization_barrier(v.astype(jnp.bfloat16)).astype(jnp.float32)

@jax.custom_vjp
def reduced_backward(v):
    return v

def low_keep(v):
    return (low(v), None)

def low_pass(kept, grad):
    return (grad,)

def back_keep(v):
    return (v, None)

def back_low(kept, grad):
    return (low(grad),)
low.defvjp(low_keep, low_pass)
reduced_backward.defvjp(back_keep, back_low)

def bucket_edges(bucket_total, far_reach, window):
    exact_count = bucket_total // 2
    boundaries = []
    current = 0
    for distance in range(window):
        if distance < exact_count:
            bucket = distance
        else:
            bucket = exact_count + int(math.log(distance / exact_count) / math.log(far_reach / exact_count) * (bucket_total - exact_count))
            bucket = min(bucket, bucket_total - 1)
        while current < bucket:
            current = current + 1
            boundaries.append(distance)
    return boundaries

def level_tables(levels, segment, window, bucket_total, far_reach):
    boundaries = bucket_edges(bucket_total, far_reach, window)
    lev_index = jnp.arange(levels, dtype=jnp.int32)[:, None, None]
    query_pos = jnp.arange(segment, dtype=jnp.int32)[None, :, None]
    key_pos = jnp.arange(segment, dtype=jnp.int32)[None, None, :]
    distance = lev_index * segment + query_pos - key_pos
    inside = (distance >= 0) & (distance < window)
    bucket = jnp.zeros(distance.shape, jnp.int32)
    for boundary in boundaries:
        bucket = bucket + (distance >= boundary).astype(jnp.int32)
    one_hot = (bucket[None] == jnp.arange(bucket_total, dtype=jnp.int32)[:, None, None, None]).astype(jnp.float32)
    return (inside, one_hot)

def ancestor_index(parents, levels):
    current = jnp.arange(parents.shape[0], dtype=jnp.int32)
    rows = [current]
    for _unused in range(levels - 1):
        current = jnp.where(current >= 0, parents[jnp.maximum(current, 0)], -1).astype(jnp.int32)
        rows.append(current)
    return jnp.stack(rows, axis=1)

def ancestor_limits(lengths, anc_index):
    picked = lengths[jnp.maximum(anc_index, 0)]
    return jnp.where(anc_index >= 0, picked, 0).astype(jnp.float32)

def layer_norm(values, norm_gain, norm_shift):
    row_mean = lax.optimization_barrier(jnp.mean(values, axis=-1, keepdims=True))
    centered = values - row_mean
    variance = lax.optimization_barrier(jnp.mean(centered * centered, axis=-1, keepdims=True))
    return centered * lax.rsqrt(variance + norm_epsilon) * norm_gain + norm_shift

def gelu_tanh(values):
    return 0.5 * values * (1.0 + jnp.tanh(gelu_coeff * (values + 0.044715 * values * values * values)))

def tree_attention(queries, key_rows, value_rows, state_keys, state_values, ancestors, limits, bias_blocks, inside):
    segments = ancestors.shape[0]
    levels = ancestors.shape[1]
    segment = queries.shape[0] // segments
    heads = bias_blocks.shape[0]
    head_dim = queries.shape[1] // heads
    score_factor = head_dim ** (-0.5)
    query_per_head = queries.reshape(segments, segment, heads, head_dim)
    key_anc = jnp.einsum('slj,jke->slke', ancestors, key_rows.reshape(segments, segment, -1), precision=TOP_PRECISION).reshape(segments, levels, segment, heads, head_dim)
    value_ancestor = jnp.einsum('slj,jke->slke', ancestors, value_rows.reshape(segments, segment, -1), precision=TOP_PRECISION).reshape(segments, levels, segment, heads, head_dim)
    state_key_per_head = state_keys.reshape(-1, heads, head_dim)
    state_value_per_head = state_values.reshape(-1, heads, head_dim)
    key_pos = jnp.arange(segment, dtype=jnp.int32)
    allowed = inside.transpose(1, 0, 2)[None, None] & (key_pos[None, None, None, None, :] < limits[:, None, None, :, None])
    raw_win = jnp.einsum('sqhd,slkhd->shqlk', query_per_head, key_anc, precision=TOP_PRECISION) * score_factor + bias_blocks.transpose(0, 2, 1, 3)[None]
    raw_win = reduced_backward(jnp.where(allowed, raw_win, masked_score))
    state_logits = reduced_backward(jnp.einsum('ogjn,xjn->ojgx', query_per_head, state_key_per_head, precision=TOP_PRECISION) * score_factor)
    row_top = jnp.maximum(lax.optimization_barrier(jnp.max(raw_win, axis=(3, 4))), lax.optimization_barrier(jnp.max(state_logits, axis=3)))
    row_total = lax.optimization_barrier(jnp.sum(jnp.exp(raw_win - row_top[..., None, None]), axis=(3, 4))) + lax.optimization_barrier(jnp.sum(jnp.exp(state_logits - row_top[..., None]), axis=3))
    log_total = row_top + jnp.log(row_total)
    window_probability = low(jnp.exp(raw_win - log_total[..., None, None]))
    state_probability = low(jnp.exp(state_logits - log_total[..., None]))
    attention_result = jnp.einsum('wejtv,wtvex->wjex', window_probability, value_ancestor, precision=TOP_PRECISION) + jnp.einsum('utfw,wtr->uftr', state_probability, state_value_per_head, precision=TOP_PRECISION)
    return attention_result.reshape(segments * segment, heads * head_dim)

def reference(tokens, state, parent, seg_length, cell_gate, norm1_gain, norm1_shift, w_query, w_key, w_value, w_attn_out, rel_bias, norm2_gain, norm2_shift, w_in, w_out, cotangent):
    inside, one_hot = level_tables(NLEV, SEG, WINDOW, BUCKETS, REACH)
    anc_index = jax.vmap(lambda parent_row: ancestor_index(parent_row, NLEV))(parent)
    ancestors = (anc_index[..., None] == jnp.arange(NSEG, dtype=jnp.int32)).astype(jnp.float32)
    limits = jax.vmap(ancestor_limits)(seg_length, anc_index)

    def forward(inputs, states, query_w, key_matrix, value_w, attn_w, bias_table, gain_one, shift_one, gain_two, shift_two, in_w, out_w):
        normed = low(layer_norm(inputs, gain_one, shift_one))
        state_normalized = low(layer_norm(states, gain_one, shift_one))
        queries = low(reduced_backward(jnp.einsum('tnd,de->tne', normed, query_w, precision=TOP_PRECISION)))
        key_rows = low(reduced_backward(jnp.einsum('tnd,de->tne', normed, key_matrix, precision=TOP_PRECISION)))
        value_rows = low(reduced_backward(jnp.einsum('tnd,de->tne', normed, value_w, precision=TOP_PRECISION)))
        state_keys = low(reduced_backward(jnp.einsum('tmd,de->tme', state_normalized, key_matrix, precision=TOP_PRECISION)))
        state_values = low(reduced_backward(jnp.einsum('tmd,de->tme', state_normalized, value_w, precision=TOP_PRECISION)))
        bias_blocks = jnp.einsum('hb,blqk->hlqk', bias_table, one_hot, precision=TOP_PRECISION)

        def one_tree(tree_item):
            return tree_attention(tree_item[0], tree_item[1], tree_item[2], tree_item[3], tree_item[4], tree_item[5], tree_item[6], bias_blocks, inside)
        attention_result = lax.map(jax.checkpoint(one_tree), (queries, key_rows, value_rows, state_keys, state_values, ancestors, limits))
        attention_result = low(reduced_backward(attention_result))
        branch = reduced_backward(jnp.einsum('tne,ed->tnd', attention_result, attn_w, precision=TOP_PRECISION))
        gated_branch = cell_gate * branch
        hidden = inputs + gated_branch
        normed_two = low(layer_norm(hidden, gain_two, shift_two))
        up_proj = reduced_backward(jnp.einsum('tnd,df->tnf', normed_two, in_w, precision=TOP_PRECISION))
        activated = low(gelu_tanh(up_proj))
        mlp_out = reduced_backward(jnp.einsum('tnf,fd->tnd', activated, out_w, precision=TOP_PRECISION))
        result = hidden + mlp_out
        cell_count = inputs.size
        squares = jnp.stack([jnp.sum(inputs * inputs), jnp.sum(gated_branch * gated_branch), jnp.sum(mlp_out * mlp_out)])
        return (result, jnp.sqrt(squares / cell_count))
    primals = (tokens.astype(jnp.float32), state.astype(jnp.float32), w_query.astype(jnp.float32), w_key.astype(jnp.float32), w_value.astype(jnp.float32), w_attn_out.astype(jnp.float32), rel_bias, norm1_gain, norm1_shift, norm2_gain, norm2_shift, w_in.astype(jnp.float32), w_out.astype(jnp.float32))
    outcome, pullback = jax.vjp(forward, *primals)
    result, norms = outcome
    grads = pullback((cotangent.astype(jnp.float32), jnp.zeros_like(norms)))
    return (result.astype(jnp.bfloat16), grads[0].astype(jnp.bfloat16), grads[1].astype(jnp.bfloat16), grads[2], grads[3], grads[4], grads[5], grads[6], grads[7], grads[8], grads[9], grads[10], grads[11], grads[12], norms)
```

```python
import functools
import math

import jax
import jax.numpy as jnp
from jax import lax
from jax.experimental import pallas as pl
from jax.experimental.pallas import tpu as pltpu
from jax.sharding import PartitionSpec as P

WINDOW = 512
BUCKETS = 32
REACH = 128
EPSILON = 1e-05
MASKED = -1e30
GELU_C = 0.7978845608028654
GELU_A = 0.044715
BF = jnp.bfloat16
F32 = jnp.float32


def bucket_edges(bucket_total, far_reach, window):
    exact_count = bucket_total // 2
    boundaries = []
    current = 0
    for distance in range(window):
        if distance < exact_count:
            bucket = distance
        else:
            bucket = exact_count + int(
                math.log(distance / exact_count)
                / math.log(far_reach / exact_count)
                * (bucket_total - exact_count)
            )
            bucket = min(bucket, bucket_total - 1)
        while current < bucket:
            current = current + 1
            boundaries.append(distance)
    return boundaries


EDGES = bucket_edges(BUCKETS, REACH, WINDOW)


def mm(left, right):
    return lax.dot_general(left, right, (((1,), (0,)), ((), ())), preferred_element_type=F32)


def mm_nt(left, right):
    return lax.dot_general(left, right, (((1,), (1,)), ((), ())), preferred_element_type=F32)


def mm_tn(left, right):
    return lax.dot_general(left, right, (((0,), (0,)), ((), ())), preferred_element_type=F32)


def bias_tables(rb_ref, h, levels, seg, bm_ref):
    row = lax.broadcasted_iota(jnp.int32, (seg, seg), 0)
    col = lax.broadcasted_iota(jnp.int32, (seg, seg), 1)
    for lev in range(levels):
        dist = lev * seg + row - col
        low, high = lev * seg - (seg - 1), lev * seg + seg - 1
        if low >= EDGES[-1]:
            val = jnp.full((seg, seg), rb_ref[h, BUCKETS - 1], F32)
        else:
            val = jnp.full((seg, seg), rb_ref[h, 0], F32)
            for i, edge in enumerate(EDGES):
                if edge <= high:
                    val = jnp.where(dist >= edge, rb_ref[h, i + 1], val)
        if low < 0:
            val = jnp.where(dist >= 0, val, MASKED)
        if high >= WINDOW:
            val = jnp.where(dist < WINDOW, val, MASKED)
        bm_ref[:, lev * seg : (lev + 1) * seg] = val


def chain(par_ref, t, first, levels, all_segs, local_segs, ctx):
    out = []
    anc = first
    for lev in range(levels):
        if lev > 0:
            up = par_ref[t, jnp.maximum(anc, 0)]
            anc = jnp.where(anc >= 0, up, -1)
        safe = jnp.maximum(anc, 0)
        owner = lax.div(safe, local_segs)
        out.append((anc >= 0, jnp.bitwise_xor(owner, ctx), safe - owner * local_segs))
    return out


def scores_of(q, kw_ref, bm_ref, line, length, levels, seg, factor):
    win = levels * seg
    col = lax.broadcasted_iota(jnp.int32, (1, seg), 1)
    raw = mm_nt(q, kw_ref[...]) * factor
    parts = []
    for lev in range(levels):
        part = raw[:, lev * seg : (lev + 1) * seg] + bm_ref[:, lev * seg : (lev + 1) * seg]
        if lev == 0:
            part = part + jnp.where(col < length, 0.0, MASKED)
        else:
            part = part + jnp.where(line[lev][0], 0.0, MASKED)
        parts.append(part)
    parts.append(raw[:, win:])
    return jnp.concatenate(parts, axis=1)


def fill_sources(parts_k, parts_v, kall, vall, kw, vw, rows, win):
    for b in range(len(parts_k)):
        for src, dst, wide in ((parts_k[b], kall, kw), (parts_v[b], vall, vw)):
            dst[b] = src[0, :rows, :]
            n = src.shape[1] - rows
            wide[win + b * n : win + (b + 1) * n, :] = src[0, rows:, :]


def fetch_window(line, kall, vall, kw, vw, seg):
    for lev, (_, part, block) in enumerate(line):
        start = pl.multiple_of(block * seg, seg)
        kw[lev * seg : (lev + 1) * seg, :] = kall[part, pl.ds(start, seg), :]
        vw[lev * seg : (lev + 1) * seg, :] = vall[part, pl.ds(start, seg), :]


def attend_kernel(dims, par_ref, len_ref, ctx_ref, rb_ref, q_ref, *refs):
    levels, seg, local_segs, all_segs, factor = dims
    parts_k, parts_v = refs[0:4], refs[4:8]
    att_ref, lse_ref, kall, vall, kw, vw, bm = refs[8:]
    t, h = pl.program_id(0), pl.program_id(1)
    ctx = ctx_ref[0]
    rows, win = local_segs * seg, levels * seg
    bias_tables(rb_ref, h, levels, seg, bm)
    fill_sources(parts_k, parts_v, kall, vall, kw, vw, rows, win)

    def one(s, carry):
        line = chain(par_ref, t, ctx * local_segs + s, levels, all_segs, local_segs, ctx)
        fetch_window(line, kall, vall, kw, vw, seg)
        at = pl.ds(pl.multiple_of(s * seg, seg), seg)
        score = scores_of(q_ref[0, at, :], kw, bm, line, len_ref[t, s], levels, seg, factor)
        top = jnp.max(score, axis=1, keepdims=True)
        prob = jnp.exp(score - top)
        total = jnp.sum(prob, axis=1, keepdims=True)
        lse_ref[0, 0, at, :] = jnp.broadcast_to(top + jnp.log(total), (seg, 128))
        att = mm(prob.astype(BF), vw[...]) / total
        att_ref[0, at, :] = att.astype(BF)
        return carry

    lax.fori_loop(0, local_segs, one, 0)


def attend_back_kernel(dims, par_ref, len_ref, ctx_ref, rb_ref, q_ref, *refs):
    levels, seg, local_segs, all_segs, factor = dims
    parts_k, parts_v = refs[0:4], refs[4:8]
    do_ref, lse_ref, dq_ref, dkv_ref, db_ref = refs[8:13]
    kall, vall, kw, vw, bm, dk, dv, near, far = refs[13:]
    h, t = pl.program_id(0), pl.program_id(1)
    ctx = ctx_ref[0]
    rows, win = local_segs * seg, levels * seg
    states = kw.shape[0] - win
    each = states // 4
    bias_tables(rb_ref, h, levels, seg, bm)
    fill_sources(parts_k, parts_v, kall, vall, kw, vw, rows, win)
    dk[...] = jnp.zeros(dk.shape, F32)
    dv[...] = jnp.zeros(dv.shape, F32)

    @pl.when(t == 0)
    def _():
        near[...] = jnp.zeros(near.shape, F32)
        far[...] = jnp.zeros(far.shape, F32)

    def one(s, carry):
        line = chain(par_ref, t, ctx * local_segs + s, levels, all_segs, local_segs, ctx)
        fetch_window(line, kall, vall, kw, vw, seg)
        at = pl.ds(pl.multiple_of(s * seg, seg), seg)
        q = q_ref[0, at, :]
        do = do_ref[0, at, :]
        score = scores_of(q, kw, bm, line, len_ref[t, s], levels, seg, factor)
        prob = jnp.exp(score - lse_ref[0, 0, at, :][:, 0:1])
        dprob = mm_nt(do, vw[...])
        delta = jnp.sum(prob * dprob, axis=1, keepdims=True)
        dscore = (prob * (dprob - delta)).astype(BF)
        dq_ref[0, at, :] = (mm(dscore, kw[...]) * factor).astype(BF)
        near[...] += dscore[:, : 2 * seg].astype(F32)
        tail = dscore[:, 2 * seg : 3 * seg].astype(F32)
        for lev in range(3, levels):
            tail = tail + dscore[:, lev * seg : (lev + 1) * seg].astype(F32)
        far[...] += tail
        gk = mm_tn(dscore, q) * factor
        gv = mm_tn(prob.astype(BF), do)
        for lev, (_, part, block) in enumerate(line):
            start = pl.ds(pl.multiple_of(block * seg, seg), seg)
            dk[part, start, :] += gk[lev * seg : (lev + 1) * seg]
            dv[part, start, :] += gv[lev * seg : (lev + 1) * seg]
        for b in range(4):
            dk[b, rows:, :] += gk[win + b * each : win + (b + 1) * each]
            dv[b, rows:, :] += gv[win + b * each : win + (b + 1) * each]
        return carry

    lax.fori_loop(0, local_segs, one, 0)
    for place, b in enumerate((0, 2, 1, 3)):
        dkv_ref[place, 0, 0] = dk[b].astype(BF)
        dkv_ref[place, 1, 0] = dv[b].astype(BF)

    @pl.when(t == pl.num_programs(1) - 1)
    def _():
        row = lax.broadcasted_iota(jnp.int32, (seg, seg), 0)
        col = lax.broadcasted_iota(jnp.int32, (seg, seg), 1)
        edges = [-(10**6)] + list(EDGES) + [10**6]
        for b in range(BUCKETS):
            total = far[...] if b == BUCKETS - 1 else jnp.zeros((seg, seg), F32)
            for lev in range(2):
                dist = lev * seg + row - col
                inside = (dist >= edges[b]) & (dist < edges[b + 1])
                total = total + jnp.where(inside, near[:, lev * seg : (lev + 1) * seg], 0.0)
            db_ref[0, b : b + 1, :] = jnp.sum(total, axis=0, keepdims=True)


def attention_calls(trees, heads, local_segs, all_segs, seg, each, head_dim):
    levels = WINDOW // seg + 1
    rows = local_segs * seg
    tall = rows + each
    win = levels * seg
    wide = win + 4 * each
    factor = head_dim ** (-0.5)
    dims = (levels, seg, local_segs, all_segs, factor)
    assert EDGES[-1] <= 2 * seg - (seg - 1)
    flops = 2 * trees * heads * rows * wide * head_dim
    base_scratch = [
        pltpu.VMEM((4, rows, head_dim), BF),
        pltpu.VMEM((4, rows, head_dim), BF),
        pltpu.VMEM((wide, head_dim), BF),
        pltpu.VMEM((wide, head_dim), BF),
        pltpu.VMEM((seg, win), F32),
    ]

    def specs(order):
        def at(col):
            return pl.BlockSpec((1, tall, head_dim), lambda a, b, *_: (order(a, b)[0], 0, col(order(a, b)[1])))

        q_spec = at(lambda h: h)
        own_k, own_v = at(lambda h: heads + h), at(lambda h: 2 * heads + h)
        oth_k, oth_v = at(lambda h: h), at(lambda h: heads + h)
        return [q_spec, own_k, oth_k, oth_k, oth_k, own_v, oth_v, oth_v, oth_v]

    th = lambda a, b: (a, b)
    ht = lambda a, b: (b, a)
    forward = pl.pallas_call(
        functools.partial(attend_kernel, dims),
        out_shape=(
            jax.ShapeDtypeStruct((trees, rows, heads * head_dim), BF),
            jax.ShapeDtypeStruct((trees, heads, rows, 128), F32),
        ),
        grid_spec=pltpu.PrefetchScalarGridSpec(
            num_scalar_prefetch=4,
            grid=(trees, heads),
            in_specs=specs(th),
            out_specs=(
                pl.BlockSpec((1, rows, head_dim), lambda t, h, *_: (t, 0, h)),
                pl.BlockSpec((1, 1, rows, 128), lambda t, h, *_: (t, h, 0, 0)),
            ),
            scratch_shapes=base_scratch,
        ),
        compiler_params=pltpu.CompilerParams(vmem_limit_bytes=32 << 20),
        cost_estimate=pl.CostEstimate(
            flops=2 * flops, transcendentals=trees * heads * rows * wide, bytes_accessed=8 << 20
        ),
        name="attend",
    )
    backward = pl.pallas_call(
        functools.partial(attend_back_kernel, dims),
        out_shape=(
            jax.ShapeDtypeStruct((trees, rows, heads * head_dim), BF),
            jax.ShapeDtypeStruct((4, 2, trees, tall, heads * head_dim), BF),
            jax.ShapeDtypeStruct((heads, BUCKETS, 128), F32),
        ),
        grid_spec=pltpu.PrefetchScalarGridSpec(
            num_scalar_prefetch=4,
            grid=(heads, trees),
            in_specs=specs(ht)
            + [
                pl.BlockSpec((1, rows, head_dim), lambda h, t, *_: (t, 0, h)),
                pl.BlockSpec((1, 1, rows, 128), lambda h, t, *_: (t, h, 0, 0)),
            ],
            out_specs=(
                pl.BlockSpec((1, rows, head_dim), lambda h, t, *_: (t, 0, h)),
                pl.BlockSpec((4, 2, 1, tall, head_dim), lambda h, t, *_: (0, 0, t, 0, h)),
                pl.BlockSpec((1, BUCKETS, 128), lambda h, t, *_: (h, 0, 0)),
            ),
            scratch_shapes=base_scratch
            + [
                pltpu.VMEM((4, tall, head_dim), F32),
                pltpu.VMEM((4, tall, head_dim), F32),
                pltpu.VMEM((seg, 2 * seg), F32),
                pltpu.VMEM((seg, seg), F32),
            ],
        ),
        compiler_params=pltpu.CompilerParams(vmem_limit_bytes=40 << 20),
        cost_estimate=pl.CostEstimate(
            flops=5 * flops, transcendentals=trees * heads * rows * wide, bytes_accessed=16 << 20
        ),
        name="attend_back",
    )
    return forward, backward


def norm_stats(values):
    mean = jnp.mean(values, axis=-1, keepdims=True)
    centered = values - mean
    scale = lax.rsqrt(jnp.mean(centered * centered, axis=-1, keepdims=True) + EPSILON)
    return centered * scale, scale


def norm_back(grad, xhat, scale, gain):
    scaled = grad * gain
    first = jnp.mean(scaled, axis=-1, keepdims=True)
    second = jnp.mean(scaled * xhat, axis=-1, keepdims=True)
    return scale * (scaled - first - xhat * second)


def gelu_parts(u):
    inner = GELU_C * (u + GELU_A * u * u * u)
    th = jnp.tanh(inner)
    value = 0.5 * u * (1.0 + th)
    slope = 0.5 * (1.0 + th) + 0.5 * u * (1.0 - th * th) * GELU_C * (1.0 + 3.0 * GELU_A * u * u)
    return value, slope


def build(mesh):
    nf, nc, nt = mesh.shape["fsdp"], mesh.shape["context"], mesh.shape["tensor"]
    assert nc == 4

    def px(x):
        return lax.ppermute(x, "fsdp", [(0, 1), (1, 0)])

    def pc(x, k):
        return lax.ppermute(x, "context", [(a, a ^ k) for a in range(nc)])

    def pz(x, j):
        return lax.ppermute(x, "tensor", [(a, (a - j) % nt) for a in range(nt)])

    def on_device(
        tokens,
        state,
        parent,
        seg_length,
        cell_gate,
        norm1_gain,
        norm1_shift,
        w_query,
        w_key,
        w_value,
        w_attn_out,
        rel_bias,
        norm2_gain,
        norm2_shift,
        w_in,
        w_out,
        cotangent,
    ):
        trees, rows, width = tokens.shape
        local_segs = seg_length.shape[1]
        seg = rows // local_segs
        all_segs = parent.shape[1]
        heads = rel_bias.shape[0]
        cols = w_query.shape[1]
        head_dim = cols // heads
        each = state.shape[1]
        fi, ci, zi = lax.axis_index("fsdp"), lax.axis_index("context"), lax.axis_index("tensor")
        core = ci & 1
        zr, zs = rows // nt, each // nt

        def zpart(x, k, axis=1):
            n = x.shape[axis] // nt
            return lax.dynamic_slice_in_dim(x, k * n, n, axis)

        def place(blocks, starts, axis, total):
            shape = list(blocks[0].shape)
            shape[axis] = total
            out = jnp.zeros(shape, blocks[0].dtype)
            for block, start in zip(blocks, starts):
                out = lax.dynamic_update_slice_in_dim(out, block, start, axis)
            return out

        def gather_f(x, axis):
            n = x.shape[axis]
            if nf == 2:
                return place([x, px(x)], [fi * n, (1 - fi) * n], axis, 2 * n)
            return lax.all_gather(x, "fsdp", axis=axis, tiled=True)

        def scatter_f(x, axis):
            n = x.shape[axis] // nf
            if nf == 2:
                sent = lax.dynamic_slice_in_dim(x, (1 - fi) * n, n, axis).astype(BF)
                return lax.dynamic_slice_in_dim(x, fi * n, n, axis) + px(sent).astype(F32)
            return lax.psum_scatter(
                x.astype(BF), "fsdp", scatter_dimension=axis, tiled=True
            ).astype(F32)

        def gather_c(x, axis):
            n = x.shape[axis]
            y = pc(x, 2)
            return place(
                [x, y, pc(x, 1), pc(y, 1)],
                [ci * n, (ci ^ 2) * n, (ci ^ 1) * n, (ci ^ 3) * n],
                axis,
                nc * n,
            )

        def cpart(x, k, axis):
            n = x.shape[axis] // nc
            return lax.dynamic_slice_in_dim(x, k * n, n, axis)

        def scatter_c(x, axis):
            sent = jnp.stack([cpart(x, ci ^ 1, axis), cpart(x, ci ^ 3, axis)]).astype(BF)
            got = pc(sent, 1).astype(F32)
            far = (cpart(x, ci ^ 2, axis) + got[1]).astype(BF)
            return cpart(x, ci, axis) + got[0] + pc(far, 2).astype(F32)

        w_qkv = jnp.concatenate([w_query, w_key, w_value], axis=1)
        depth = w_qkv.shape[0]
        if nf == 2:
            half = depth // 2
            near = px(lax.dynamic_slice_in_dim(w_qkv, core * half, half, 0))
            over = pc(near, 1)
            base = (1 - fi) * depth
            qkv_w = place(
                [w_qkv, near, over],
                [fi * depth, base + core * half, base + (1 - core) * half],
                0,
                2 * depth,
            )
        else:
            qkv_w = lax.all_gather(w_qkv, "fsdp", axis=0, tiled=True)

        both = jnp.concatenate([tokens, state], axis=1).astype(F32)
        xhat_one, _ = norm_stats(both)
        normed = (xhat_one * norm1_gain + norm1_shift).astype(BF).reshape(-1, width)
        qkv = mm(normed, qkv_w).astype(BF).reshape(trees, rows + each, 3 * cols)
        kv = qkv[:, :, cols:]
        kv_y = pc(kv, 2)
        kv_c = pc(kv, 1)
        kv_cy = pc(kv_y, 1)

        fc = w_in.shape[1] // nc
        in_z = lax.dynamic_slice_in_dim(w_in, ci * fc, fc, 1)
        out_z = lax.dynamic_slice_in_dim(w_out, ci * fc, fc, 0)
        o_rows = w_attn_out.shape[0] // nc
        o_z = lax.dynamic_slice_in_dim(w_attn_out, ci * o_rows, o_rows, 0)
        in_blocks = [in_z] + [pz(in_z, j) for j in range(1, nt)]
        out_blocks = [out_z] + [pz(out_z, j) for j in range(1, nt)]
        o_blocks = [o_z] + [pz(o_z, j) for j in range(1, nt)]
        in_c = gather_f(jnp.concatenate(in_blocks, axis=1), 0)
        out_c = gather_f(jnp.concatenate(out_blocks, axis=0), 1)
        o_w = gather_c(gather_f(jnp.stack(o_blocks), 2), 1).reshape(nt * nc * o_rows, width)

        forward, backward = attention_calls(
            trees, heads, local_segs, all_segs, seg, each, head_dim
        )
        tables = (parent, seg_length, ci.reshape(1).astype(jnp.int32), rel_bias)
        sources = (qkv, qkv, kv_c, kv_y, kv_cy, qkv, kv_c, kv_y, kv_cy)
        attended, log_total = forward(*tables, *sources)

        att_blocks = [zpart(attended, zi)]
        for j in range(1, nt):
            att_blocks.append(pz(zpart(attended, (zi - j) % nt), j))
        att = jnp.concatenate(att_blocks, axis=2).reshape(trees * zr, nt * cols)
        inputs = zpart(tokens, zi).astype(F32).reshape(trees * zr, width)
        branch = mm(att, o_w)
        gated = cell_gate * branch
        hidden = inputs + gated
        xhat_two, scale_two = norm_stats(hidden)
        normed_two = (xhat_two * norm2_gain + norm2_shift).astype(BF)

        def spread(x):
            y = pc(x, 2)
            return jnp.concatenate([x, y, pc(x, 1), pc(y, 1)], axis=0)

        grad_low = zpart(cotangent, zi).reshape(trees * zr, width)
        grad_rows = spread(grad_low)
        ff_rows = spread(normed_two)
        up_proj = mm(ff_rows, in_c)
        active, slope = gelu_parts(up_proj)
        active = active.astype(BF)
        grad_up = (mm_nt(grad_rows, out_c) * slope).astype(BF)

        def collect(part):
            part = part.reshape(4, trees * zr, width)
            got = pc(part[2:].astype(BF), 1).astype(F32)
            far = (part[1] + got[1]).astype(BF)
            return part[0] + got[0] + pc(far, 2).astype(F32)

        grad_normed_two = collect(mm_nt(grad_up, in_c))
        mlp_out = collect(mm(active, out_c))
        part_in = mm_tn(ff_rows, grad_up)
        part_out = mm_tn(active, grad_rows)

        def broadcast_z(x):
            n = x.shape[1]
            blocks = [x] + [pz(x, j) for j in range(1, nt)]
            return place(blocks, [((zi + j) % nt) * n for j in range(nt)], 1, nt * n)

        result = (hidden + mlp_out).astype(BF).reshape(trees, zr, width)
        output = broadcast_z(result)

        grad_result = grad_low.astype(F32)
        gain_two = jnp.sum(grad_normed_two * xhat_two, axis=0)
        shift_two = jnp.sum(grad_normed_two, axis=0)
        grad_hidden = grad_result + norm_back(grad_normed_two, xhat_two, scale_two, norm2_gain)
        grad_branch = (cell_gate * grad_hidden).astype(BF)
        grad_att = mm_nt(grad_branch, o_w).astype(BF).reshape(trees, zr, nt, cols)
        part_attn = mm_tn(att, grad_branch)
        heads_blocks = [grad_att[:, :, 0]]
        heads_at = [zi * zr]
        for j in range(1, nt):
            heads_blocks.append(
                lax.ppermute(grad_att[:, :, j], "tensor", [(a, (a + j) % nt) for a in range(nt)])
            )
            heads_at.append(((zi - j) % nt) * zr)
        grad_heads = place(heads_blocks, heads_at, 1, rows)

        grad_q, parts, bias_rows = backward(*tables, *sources, grad_heads, log_total)
        got = pc(parts[2:], 1).astype(F32)
        far = (parts[1].astype(F32) + got[1]).astype(BF)
        grad_kv = (
            parts[0].astype(F32) + got[0] + pc(far, 2).astype(F32)
        ).astype(BF)

        o_depth = qkv_w.shape[0] // nc
        slab = lax.dynamic_slice_in_dim(qkv_w, ci * o_depth, o_depth, 0)
        all_w = gather_c(
            jnp.concatenate([slab] + [pz(slab, j) for j in range(1, nt)], axis=1), 0
        )
        q_blocks, kv_blocks = [], []
        for j in range(nt):
            k = (zi - j) % nt
            q_piece = zpart(grad_q, k)
            kv_piece = jnp.concatenate(
                [zpart(grad_kv[:, :, :rows], k, 2), zpart(grad_kv[:, :, rows:], k, 2)], axis=2
            )
            q_blocks.append(pz(q_piece, j) if j else q_piece)
            kv_blocks.append(pz(kv_piece, j) if j else kv_piece)
        line = []
        for j in range(nt):
            line.append(jnp.pad(q_blocks[j], ((0, 0), (0, zs), (0, 0))))
            line.append(kv_blocks[j][0])
            line.append(kv_blocks[j][1])
        line = jnp.concatenate(line, axis=2).reshape(trees * (zr + zs), nt * 3 * cols)
        grad_normed = mm_nt(line, all_w).reshape(trees, zr + zs, width)
        own = jnp.concatenate([zpart(tokens, zi), zpart(state, zi)], axis=1).astype(F32)
        xhat_own, scale_own = norm_stats(own)
        gain_one = jnp.sum(grad_normed * xhat_own, axis=(0, 1))
        shift_one = jnp.sum(grad_normed, axis=(0, 1))
        grad_own = norm_back(grad_normed, xhat_own, scale_own, norm1_gain)
        grad_tokens_own = (grad_hidden.reshape(trees, zr, width) + grad_own[:, :zr]).astype(BF)
        tokens_grad = broadcast_z(grad_tokens_own)
        state_grad = broadcast_z(grad_own[:, zr:].astype(BF))

        def sum_z(blocks):
            total = blocks[0]
            for j in range(1, nt):
                total = total + lax.ppermute(
                    blocks[j].astype(BF), "tensor", [(a, (a + j) % nt) for a in range(nt)]
                ).astype(F32)
            return total

        in_sum = scatter_f(part_in, 0)
        in_own = sum_z([in_sum[:, j * fc : (j + 1) * fc] for j in range(nt)])
        grad_in = gather_c(in_own.astype(BF), 1).astype(F32)
        out_sum = scatter_f(part_out, 1)
        out_own = sum_z([out_sum[j * fc : (j + 1) * fc] for j in range(nt)])
        grad_out = gather_c(out_own.astype(BF), 0).astype(F32)
        attn_sum = scatter_f(
            scatter_c(part_attn.reshape(nt, nc * o_rows, width), 1), 2
        )
        attn_own = sum_z([attn_sum[j] for j in range(nt)])
        grad_attn_out = gather_c(attn_own.astype(BF), 0).astype(F32)

        normed3 = normed.reshape(trees, rows + each, width)
        part_q = mm_tn(
            normed3[:, :rows].reshape(-1, width), grad_q.reshape(-1, cols)
        )
        part_k = mm_tn(normed, grad_kv[0].reshape(-1, cols))
        part_v = mm_tn(normed, grad_kv[1].reshape(-1, cols))
        part_qkv = jnp.concatenate([part_q, part_k, part_v], axis=1)
        part_qkv = part_qkv.reshape(nf, depth, 3 * cols)
        qkv_sum = scatter_f(scatter_c(part_qkv, 1), 0)[0]
        grad_qkv = gather_c(qkv_sum.astype(BF), 0).astype(F32)

        def total(x):
            if nf == 2:
                x = x + px(x)
            else:
                x = lax.psum(x, "fsdp")
            x = x + pc(x, 1)
            x = x + pc(x, 2)
            if nt & (nt - 1) == 0:
                k = 1
                while k < nt:
                    x = x + lax.ppermute(x, "tensor", [(a, a ^ k) for a in range(nt)])
                    k = 2 * k
                return x
            return lax.psum(x, "tensor")

        bias_own = jnp.sum(bias_rows, axis=2)
        bias_all = lax.dynamic_update_slice(
            jnp.zeros((heads * nt, BUCKETS), F32), bias_own, (zi * heads, 0)
        )
        squares = jnp.stack(
            [jnp.sum(inputs * inputs), jnp.sum(gated * gated), jnp.sum(mlp_out * mlp_out)]
        )
        early = total(
            jnp.concatenate([gain_two, shift_two, bias_all.reshape(-1), squares])
        )
        late = total(jnp.concatenate([gain_one, shift_one]))
        at = 2 * width + bias_all.size
        bias_sum = early[2 * width : at].reshape(bias_all.shape)
        grad_bias = lax.dynamic_slice_in_dim(bias_sum, zi * heads, heads, 0)
        cell_count = trees * rows * width * nf * nc
        norms = jnp.sqrt(early[at : at + 3] / cell_count)
        return (
            output,
            tokens_grad,
            state_grad,
            grad_qkv[:, :cols],
            grad_qkv[:, cols : 2 * cols],
            grad_qkv[:, 2 * cols :],
            grad_attn_out,
            grad_bias,
            late[:width],
            late[width:],
            early[:width],
            early[width : 2 * width],
            grad_in,
            grad_out,
            norms,
        )

    return on_device


def solution(mesh):
    return jax.shard_map(
        build(mesh),
        mesh=mesh,
        in_specs=(
            P("fsdp", "context", None),
            P("fsdp", "context", None),
            P("fsdp", None),
            P("fsdp", "context"),
            P(),
            P(),
            P(),
            P("fsdp", "tensor"),
            P("fsdp", "tensor"),
            P("fsdp", "tensor"),
            P("tensor", "fsdp"),
            P("tensor", None),
            P(),
            P(),
            P("fsdp", "tensor"),
            P("tensor", "fsdp"),
            P("fsdp", "context", None),
        ),
        out_specs=(
            P("fsdp", "context", None),
            P("fsdp", "context", None),
            P("fsdp", "context", None),
            P("fsdp", "tensor"),
            P("fsdp", "tensor"),
            P("fsdp", "tensor"),
            P("tensor", "fsdp"),
            P("tensor", None),
            P(),
            P(),
            P(),
            P(),
            P("fsdp", "tensor"),
            P("tensor", "fsdp"),
            P(),
        ),
        check_vma=False,
    )
```

```python
import functools
import math

import jax
import jax.numpy as jnp
from jax import lax
from jax.experimental import pallas as pl
from jax.experimental.pallas import tpu as pltpu
from jax.sharding import PartitionSpec as P

WINDOW = 512
BUCKETS = 32
REACH = 128
EPSILON = 1e-05
MASKED = -1e30
GELU_C = 0.7978845608028654
GELU_A = 0.044715
BF = jnp.bfloat16
F32 = jnp.float32


def cost(us):
    return pl.CostEstimate(
        flops=int(us * 1e9), transcendentals=0, bytes_accessed=int(us * 3e6)
    )


def bucket_edges(bucket_total, far_reach, window):
    exact_count = bucket_total // 2
    boundaries = []
    current = 0
    for distance in range(window):
        if distance < exact_count:
            bucket = distance
        else:
            bucket = exact_count + int(
                math.log(distance / exact_count)
                / math.log(far_reach / exact_count)
                * (bucket_total - exact_count)
            )
            bucket = min(bucket, bucket_total - 1)
        while current < bucket:
            current = current + 1
            boundaries.append(distance)
    return boundaries


EDGES = bucket_edges(BUCKETS, REACH, WINDOW)


def mm(left, right):
    return lax.dot_general(left, right, (((1,), (0,)), ((), ())), preferred_element_type=F32)


def mm_nt(left, right):
    return lax.dot_general(left, right, (((1,), (1,)), ((), ())), preferred_element_type=F32)


def mm_tn(left, right):
    return lax.dot_general(left, right, (((0,), (0,)), ((), ())), preferred_element_type=F32)


def bias_tables(rb_ref, h, levels, seg, bm_ref):
    row = lax.broadcasted_iota(jnp.int32, (seg, seg), 0)
    col = lax.broadcasted_iota(jnp.int32, (seg, seg), 1)
    for lev in range(levels):
        dist = lev * seg + row - col
        low, high = lev * seg - (seg - 1), lev * seg + seg - 1
        if low >= EDGES[-1]:
            val = jnp.full((seg, seg), rb_ref[h, BUCKETS - 1], F32)
        else:
            val = jnp.full((seg, seg), rb_ref[h, 0], F32)
            for i, edge in enumerate(EDGES):
                if edge <= high:
                    val = jnp.where(dist >= edge, rb_ref[h, i + 1], val)
        if low < 0:
            val = jnp.where(dist >= 0, val, MASKED)
        if high >= WINDOW:
            val = jnp.where(dist < WINDOW, val, MASKED)
        bm_ref[:, lev * seg : (lev + 1) * seg] = val


def chain(par_ref, t, first, levels, all_segs, local_segs, ctx):
    out = []
    anc = first
    for lev in range(levels):
        if lev > 0:
            up = par_ref[t, jnp.maximum(anc, 0)]
            anc = jnp.where(anc >= 0, up, -1)
        safe = jnp.maximum(anc, 0)
        owner = lax.div(safe, local_segs)
        out.append((anc >= 0, jnp.bitwise_xor(owner, ctx), safe - owner * local_segs))
    return out


def scores_of(q, kw_ref, bm_ref, line, length, levels, seg, factor):
    win = levels * seg
    col = lax.broadcasted_iota(jnp.int32, (1, seg), 1)
    raw = mm_nt(q, kw_ref[...]) * factor
    parts = []
    for lev in range(levels):
        part = raw[:, lev * seg : (lev + 1) * seg] + bm_ref[:, lev * seg : (lev + 1) * seg]
        if lev == 0:
            part = part + jnp.where(col < length, 0.0, MASKED)
        else:
            part = part + jnp.where(line[lev][0], 0.0, MASKED)
        parts.append(part)
    parts.append(raw[:, win:])
    return jnp.concatenate(parts, axis=1)


def fill_sources(parts_k, parts_v, kall, vall, kw, vw, rows, win):
    for b in range(len(parts_k)):
        for src, dst, wide in ((parts_k[b], kall, kw), (parts_v[b], vall, vw)):
            dst[b] = src[0, :rows, :]
            n = src.shape[1] - rows
            wide[win + b * n : win + (b + 1) * n, :] = src[0, rows:, :]


def fetch_window(line, kall, vall, kw, vw, seg):
    for lev, (_, part, block) in enumerate(line):
        start = pl.multiple_of(block * seg, seg)
        kw[lev * seg : (lev + 1) * seg, :] = kall[part, pl.ds(start, seg), :]
        vw[lev * seg : (lev + 1) * seg, :] = vall[part, pl.ds(start, seg), :]


def attend_kernel(dims, par_ref, len_ref, pos_ref, rb_ref, q_ref, *refs):
    levels, seg, local_segs, all_segs, factor, nt = dims
    parts_k, parts_v = refs[0:4], refs[4:8]
    att_refs, lse_ref = refs[8 : 8 + nt], refs[8 + nt]
    kall, vall, kw, vw, bm, whole = refs[9 + nt :]
    t, h = pl.program_id(0), pl.program_id(1)
    ctx, zi = pos_ref[0], pos_ref[1]
    rows, win = local_segs * seg, levels * seg
    bias_tables(rb_ref, h, levels, seg, bm)
    fill_sources(parts_k, parts_v, kall, vall, kw, vw, rows, win)

    def one(s, carry):
        line = chain(par_ref, t, ctx * local_segs + s, levels, all_segs, local_segs, ctx)
        fetch_window(line, kall, vall, kw, vw, seg)
        at = pl.ds(pl.multiple_of(s * seg, seg), seg)
        score = scores_of(q_ref[0, at, :], kw, bm, line, len_ref[t, s], levels, seg, factor)
        top = jnp.max(score, axis=1, keepdims=True)
        prob = jnp.exp(score - top)
        total = jnp.sum(prob, axis=1, keepdims=True)
        lse_ref[0, 0, at, :] = jnp.broadcast_to(top + jnp.log(total), (seg, 128))
        att = mm(prob.astype(BF), vw[...]) / total
        whole[at, :] = att.astype(BF)
        return carry

    lax.fori_loop(0, local_segs, one, 0)
    n = rows // nt
    for j in range(nt):
        k = lax.rem(zi - j + nt, nt)
        att_refs[j][0] = whole[pl.ds(pl.multiple_of(k * n, n), n), :]


def attend_back_kernel(dims, par_ref, len_ref, pos_ref, rb_ref, q_ref, *refs):
    levels, seg, local_segs, all_segs, factor, nt = dims
    parts_k, parts_v = refs[0:4], refs[4:8]
    do_refs, lse_ref = refs[8 : 8 + nt], refs[8 + nt]
    dq_refs = refs[9 + nt : 9 + 2 * nt]
    dq_ref, near_ref, far_ref, db_ref = refs[9 + 2 * nt : 13 + 2 * nt]
    kall, vall, kw, vw, bm, dk, dv, near, far, dos = refs[13 + 2 * nt :]
    h, t = pl.program_id(0), pl.program_id(1)
    ctx, zi = pos_ref[0], pos_ref[1]
    rows, win = local_segs * seg, levels * seg
    states = kw.shape[0] - win
    each = states // 4
    n = rows // nt
    bias_tables(rb_ref, h, levels, seg, bm)
    fill_sources(parts_k, parts_v, kall, vall, kw, vw, rows, win)
    dk[...] = jnp.zeros(dk.shape, F32)
    dv[...] = jnp.zeros(dv.shape, F32)
    for j in range(nt):
        k = lax.rem(zi - j + nt, nt)
        dos[pl.ds(pl.multiple_of(k * n, n), n), :] = do_refs[j][0]

    @pl.when(t == 0)
    def _():
        near[...] = jnp.zeros(near.shape, F32)
        far[...] = jnp.zeros(far.shape, F32)

    def one(s, carry):
        line = chain(par_ref, t, ctx * local_segs + s, levels, all_segs, local_segs, ctx)
        fetch_window(line, kall, vall, kw, vw, seg)
        at = pl.ds(pl.multiple_of(s * seg, seg), seg)
        q = q_ref[0, at, :]
        do = dos[at, :]
        score = scores_of(q, kw, bm, line, len_ref[t, s], levels, seg, factor)
        prob = jnp.exp(score - lse_ref[0, 0, at, :][:, 0:1])
        dprob = mm_nt(do, vw[...])
        delta = jnp.sum(prob * dprob, axis=1, keepdims=True)
        dscore = (prob * (dprob - delta)).astype(BF)
        dq_ref[0, at, :] = (mm(dscore, kw[...]) * factor).astype(BF)
        near[...] += dscore[:, : 2 * seg].astype(F32)
        tail = dscore[:, 2 * seg : 3 * seg].astype(F32)
        for lev in range(3, levels):
            tail = tail + dscore[:, lev * seg : (lev + 1) * seg].astype(F32)
        far[...] += tail
        gk = mm_tn(dscore, q) * factor
        gv = mm_tn(prob.astype(BF), do)
        for lev, (_, part, block) in enumerate(line):
            start = pl.ds(pl.multiple_of(block * seg, seg), seg)
            dk[part, start, :] += gk[lev * seg : (lev + 1) * seg]
            dv[part, start, :] += gv[lev * seg : (lev + 1) * seg]
        for b in range(4):
            dk[b, rows:, :] += gk[win + b * each : win + (b + 1) * each]
            dv[b, rows:, :] += gv[win + b * each : win + (b + 1) * each]
        return carry

    lax.fori_loop(0, local_segs, one, 0)
    for ref, pair in ((near_ref, (0, 2)), (far_ref, (1, 3))):
        for place, b in enumerate(pair):
            ref[place, 0, 0] = dk[b].astype(BF)
            ref[place, 1, 0] = dv[b].astype(BF)
    for j in range(nt):
        k = lax.rem(zi - j + nt, nt)
        dq_refs[j][0] = dq_ref[0, pl.ds(pl.multiple_of(k * n, n), n), :]

    @pl.when(t == pl.num_programs(1) - 1)
    def _():
        row = lax.broadcasted_iota(jnp.int32, (seg, seg), 0)
        col = lax.broadcasted_iota(jnp.int32, (seg, seg), 1)
        edges = [-(10**6)] + list(EDGES) + [10**6]
        for b in range(BUCKETS):
            total = far[...] if b == BUCKETS - 1 else jnp.zeros((seg, seg), F32)
            for lev in range(2):
                dist = lev * seg + row - col
                inside = (dist >= edges[b]) & (dist < edges[b + 1])
                total = total + jnp.where(inside, near[:, lev * seg : (lev + 1) * seg], 0.0)
            db_ref[0, b : b + 1, :] = jnp.sum(total, axis=0, keepdims=True)


def hbm_call(prefetch, body, out_shape, keep=False, **kw):
    if not keep:
        return pl.pallas_call(body, out_shape=out_shape, **kw)
    several = isinstance(out_shape, tuple)
    outs = tuple(
        pltpu.HBM(o.shape, o.dtype) for o in (out_shape if several else (out_shape,))
    )
    kernel = pl.pallas_call(body, out_shape=outs if several else outs[0], **kw)

    def run(*args):
        rest = [pltpu.with_memory_space_constraint(a, pltpu.HBM) for a in args[prefetch:]]
        return kernel(*args[:prefetch], *rest)

    return run


def attention_calls(trees, heads, local_segs, all_segs, seg, each, head_dim, nt):
    levels = WINDOW // seg + 1
    rows = local_segs * seg
    tall = rows + each
    win = levels * seg
    wide = win + 4 * each
    factor = head_dim ** (-0.5)
    dims = (levels, seg, local_segs, all_segs, factor, nt)
    assert EDGES[-1] <= 2 * seg - (seg - 1)
    base_scratch = [
        pltpu.VMEM((4, rows, head_dim), BF),
        pltpu.VMEM((4, rows, head_dim), BF),
        pltpu.VMEM((wide, head_dim), BF),
        pltpu.VMEM((wide, head_dim), BF),
        pltpu.VMEM((seg, win), F32),
    ]

    def specs(order):
        def at(col):
            return pl.BlockSpec(
                (1, tall, head_dim), lambda a, b, *_: (order(a, b)[0], 0, col(order(a, b)[1]))
            )

        k, v = at(lambda h: h), at(lambda h: heads + h)
        return [k, k, k, k, k, v, v, v, v]

    th = lambda a, b: (a, b)
    ht = lambda a, b: (b, a)
    chunk_shape = jax.ShapeDtypeStruct((trees, rows // nt, heads * head_dim), BF)

    def chunk_spec(order):
        return pl.BlockSpec(
            (1, rows // nt, head_dim), lambda a, b, *_: (order(a, b)[0], 0, order(a, b)[1])
        )

    forward = hbm_call(
        4,
        functools.partial(attend_kernel, dims),
        out_shape=(chunk_shape,) * nt + (jax.ShapeDtypeStruct((trees, heads, rows, 128), F32),),
        grid_spec=pltpu.PrefetchScalarGridSpec(
            num_scalar_prefetch=4,
            grid=(trees, heads),
            in_specs=specs(th),
            out_specs=(chunk_spec(th),) * nt
            + (pl.BlockSpec((1, 1, rows, 128), lambda t, h, *_: (t, h, 0, 0)),),
            scratch_shapes=base_scratch + [pltpu.VMEM((rows, head_dim), BF)],
        ),
        compiler_params=pltpu.CompilerParams(vmem_limit_bytes=24 << 20),
        cost_estimate=cost(16),
        keep=True,
        name="attend",
    )
    pair = jax.ShapeDtypeStruct((2, 2, trees, tall, heads * head_dim), BF)
    pair_spec = pl.BlockSpec((2, 2, 1, tall, head_dim), lambda h, t, *_: (0, 0, t, 0, h))
    backward = hbm_call(
        4,
        functools.partial(attend_back_kernel, dims),
        out_shape=(chunk_shape,) * nt
        + (
            jax.ShapeDtypeStruct((trees, rows, heads * head_dim), BF),
            pair,
            pair,
            jax.ShapeDtypeStruct((heads, BUCKETS, 128), F32),
        ),
        grid_spec=pltpu.PrefetchScalarGridSpec(
            num_scalar_prefetch=4,
            grid=(heads, trees),
            in_specs=specs(ht)
            + [chunk_spec(ht)] * nt
            + [pl.BlockSpec((1, 1, rows, 128), lambda h, t, *_: (t, h, 0, 0))],
            out_specs=(chunk_spec(ht),) * nt
            + (
                pl.BlockSpec((1, rows, head_dim), lambda h, t, *_: (t, 0, h)),
                pair_spec,
                pair_spec,
                pl.BlockSpec((1, BUCKETS, 128), lambda h, t, *_: (h, 0, 0)),
            ),
            scratch_shapes=base_scratch
            + [
                pltpu.VMEM((4, tall, head_dim), F32),
                pltpu.VMEM((4, tall, head_dim), F32),
                pltpu.VMEM((seg, 2 * seg), F32),
                pltpu.VMEM((seg, seg), F32),
                pltpu.VMEM((rows, head_dim), BF),
            ],
        ),
        compiler_params=pltpu.CompilerParams(vmem_limit_bytes=32 << 20),
        cost_estimate=cost(24),
        keep=True,
        name="attend_back",
    )
    return forward, backward


def norm_stats(values):
    mean = jnp.mean(values, axis=-1, keepdims=True)
    centered = values - mean
    scale = lax.rsqrt(jnp.mean(centered * centered, axis=-1, keepdims=True) + EPSILON)
    return centered * scale, scale


def norm_back(grad, xhat, scale, gain):
    scaled = grad * gain
    first = jnp.mean(scaled, axis=-1, keepdims=True)
    second = jnp.mean(scaled * xhat, axis=-1, keepdims=True)
    return scale * (scaled - first - xhat * second)


def gelu_parts(u):
    square = u * u
    th = jnp.tanh(u * (GELU_C + GELU_C * GELU_A * square))
    half = 0.5 * (1.0 + th)
    slope = half + (0.5 * u) * (1.0 - th * th) * (GELU_C + 3.0 * GELU_C * GELU_A * square)
    return u * half, slope


def norm_kernel(gain, shift, tok, st, out):
    each = st.shape[1]
    rows = tok.shape[1]
    for lo in range(0, rows + each, each):
        x = (tok[0, lo : lo + each, :] if lo < rows else st[0]).astype(F32)
        xhat, _ = norm_stats(x)
        out[0, lo : lo + each, :] = (xhat * gain[...] + shift[...]).astype(BF)


def project_kernel(pos, x, *refs):
    if len(refs) == 3:
        w = refs[0]
        q_ref, kv_ref = refs[1:]
    else:
        wq, wk, wv, near, over, q_ref, kv_ref, w = refs

        @pl.when((pl.program_id(0) == 0) & (pl.program_id(1) == 0))
        def _():
            fi, core = pos[2], pos[0] & 1
            depth, cols = wq.shape
            half = depth // 2
            for i, part in enumerate((wq, wk, wv)):
                w[pl.ds(pl.multiple_of(fi * depth, depth), depth), i * cols : (i + 1) * cols] = (
                    part[...]
                )
            base = (1 - fi) * depth
            w[pl.ds(pl.multiple_of(base + core * half, half), half), :] = near[...]
            w[pl.ds(pl.multiple_of(base + (1 - core) * half, half), half), :] = over[...]

    y = mm(x[0], w[...]).astype(BF)
    cols = q_ref.shape[2]
    q_ref[0] = y[:, :cols]
    kv_ref[0] = y[:, cols:]


def load_projection(pos, blocks, w):
    n = len(blocks) if blocks[0].shape[1] == w.shape[1] else len(blocks) // 2
    rows, depth = blocks[0].shape
    for j in range(n):
        at = slice(j * rows, (j + 1) * rows)
        if n == len(blocks):
            w[at, :] = blocks[j][...]
        else:
            fi = pos[2]
            w[at, pl.ds(pl.multiple_of(fi * depth, depth), depth)] = blocks[j][...]
            w[at, pl.ds(pl.multiple_of((1 - fi) * depth, depth), depth)] = blocks[n + j][...]


def mix_kernel(n, pos, *refs):
    att, blocks = refs[:n], refs[n:-8]
    tok, cell, gain, shift, hid_ref, n2_ref, stat_ref, w = refs[-8:]

    @pl.when(pl.program_id(0) == 0)
    def _():
        load_projection(pos, blocks, w)
        stat_ref[...] = jnp.zeros(stat_ref.shape, F32)

    cols = att[0].shape[2]
    branch = mm(att[0][0], w[:cols, :])
    for j in range(1, n):
        branch = branch + mm(att[j][0], w[j * cols : (j + 1) * cols, :])
    x = tok[0].astype(F32)
    gated = cell[...] * branch
    hidden = x + gated
    hid_ref[0] = hidden
    xhat, _ = norm_stats(hidden)
    n2_ref[0] = (xhat * gain[...] + shift[...]).astype(BF)
    stat_ref[0:1, :] += jnp.sum(x * x, axis=0, keepdims=True)
    stat_ref[1:2, :] += jnp.sum(gated * gated, axis=0, keepdims=True)


def ff_kernel(*refs):
    xs, gs = refs[0:4], refs[4:8]
    pack, near_ref, far_ref, act_ref, gup_ref, xall, gall, win, wout = refs[8:]
    nt, nf, _, depth, fc = pack.shape
    width = nf * depth
    for z in range(nt):
        for f in range(nf):
            win[z, f * depth : (f + 1) * depth, :] = pack[z, f, 0]
            wout[z, f * depth : (f + 1) * depth, :] = pack[z, f, 1]
    for p in range(4):
        xall[p] = xs[p][...]
        gall[p] = gs[p][...]
    step = 256

    def one(i, carry):
        p = lax.rem(i + 2, 4)
        x, g = xall[p], gall[p]
        for z in range(nt):
            value, slope = gelu_parts(mm(x, win[z]))
            act_ref[p, :, z * fc : (z + 1) * fc] = value.astype(BF)
            gup_ref[p, :, z * fc : (z + 1) * fc] = (mm(g, wout[z]) * slope).astype(BF)
        for n in range(0, width, step):
            part = mm_nt(gup_ref[p, :, :fc], win[0, n : n + step, :])
            for z in range(1, nt):
                part = part + mm_nt(
                    gup_ref[p, :, z * fc : (z + 1) * fc], win[z, n : n + step, :]
                )
            part = part.astype(BF)

            @pl.when(p < 2)
            def _():
                near_ref[p, :, n : n + step] = part

            @pl.when(p >= 2)
            def _():
                far_ref[p - 2, :, n : n + step] = part

        return carry

    lax.fori_loop(0, 4, one, 0)


def ff_grad_kernel(*refs):
    xs, gs = refs[0:4], refs[4:8]
    act, gup, pack, sent_ref, near_ref, far_ref, xall, gall, acc, wout = refs[8:]
    _, nf, _, depth, fc = pack.shape
    mine = xs[0].shape[0]

    @pl.when(pl.program_id(0) == 0)
    def _():
        for p in range(4):
            xall[p * mine : (p + 1) * mine, :] = xs[p][...]
            gall[p * mine : (p + 1) * mine, :] = gs[p][...]
        acc[...] = jnp.zeros(acc.shape, F32)

    for f in range(nf):
        wout[f * depth : (f + 1) * depth, :] = pack[0, f, 1]
    a = act[...].reshape(4 * mine, fc)
    acc[...] += mm_nt(a, wout[...])
    for i, part in ((0, mm_tn(xall[...], gup[...].reshape(4 * mine, fc))), (1, mm_tn(gall[...], a))):
        for f in range(nf):
            sent_ref[f, 0, i] = part[f * depth : (f + 1) * depth].astype(BF)

    @pl.when(pl.program_id(0) == pl.num_programs(0) - 1)
    def _():
        near_ref[...] = acc[: 2 * mine, :].reshape(near_ref.shape).astype(BF)
        far_ref[...] = acc[2 * mine :, :].reshape(far_ref.shape).astype(BF)


def branch_back_kernel(nt, pos, *refs):
    blocks, (own, got, far, hid, cot, cell, gain) = refs[: -(nt + 11)], refs[-(nt + 11) : -(nt + 4)]
    gh_ref, gb_ref = refs[-(nt + 4) : -(nt + 2)]
    ga_refs, stat_ref, w = refs[-(nt + 2) : -2], refs[-2], refs[-1]

    @pl.when(pl.program_id(0) == 0)
    def _():
        load_projection(pos, blocks, w)
        stat_ref[...] = jnp.zeros(stat_ref.shape, F32)

    grad = own[0, 0].astype(F32) + got[0, 0].astype(F32) + far[0].astype(F32)
    xhat, scale = norm_stats(hid[0])
    gh = cot[0].astype(F32) + norm_back(grad, xhat, scale, gain[...])
    gh_ref[0] = gh
    gb = (cell[...] * gh).astype(BF)
    gb_ref[0] = gb
    cols = ga_refs[0].shape[2]
    for j, ref in enumerate(ga_refs):
        ref[0] = mm_nt(gb, w[j * cols : (j + 1) * cols, :]).astype(BF)

    stat_ref[0:1, :] += jnp.sum(grad * xhat, axis=0, keepdims=True)
    stat_ref[1:2, :] += jnp.sum(grad, axis=0, keepdims=True)


def combine_kernel(rows, pos, own, got, far, *refs):
    nt = (len(refs) - 1) // 2
    dq, total_ref, send = refs[:nt], refs[nt], refs[nt + 1 :]
    total = (
        own[0, 0, 0].astype(F32) + got[0, 0, 0].astype(F32) + far[0, 0].astype(F32)
    ).astype(BF)
    total_ref[0, 0] = total
    n = rows // nt
    m = (total_ref.shape[2] - rows) // nt
    kv = pl.program_id(1)
    for j in range(nt):
        k = lax.rem(pos[1] - j + nt, nt)

        @pl.when(kv == 0)
        def _():
            send[j][0, 0, :n, :] = dq[j][0]
            send[j][0, 0, n:, :] = jnp.zeros((m, dq[j].shape[2]), BF)

        send[j][1 + kv, 0, :n, :] = total_ref[0, 0, pl.ds(pl.multiple_of(k * n, n), n), :]
        send[j][1 + kv, 0, n:, :] = total_ref[0, 0, pl.ds(pl.multiple_of(rows + k * m, m), m), :]


def input_back_kernel(nt, pos, *refs):
    blocks = refs[:nt]
    w, tok, st, gh, gain, out_ref, stat_ref = refs[nt:]
    cols = blocks[0].shape[3]
    n = tok.shape[1]
    every = None
    for j in range(nt):
        k = lax.rem(pos[1] + j, nt)
        for i in range(3):
            part = mm_nt(blocks[j][i, 0], w[k, :, i * cols : (i + 1) * cols])
            every = part if every is None else every + part

    @pl.when(pl.program_id(0) == 0)
    def _():
        stat_ref[...] = jnp.zeros(stat_ref.shape, F32)

    for x_ref, grad, lo, hi, extra in (
        (tok, every[:n], 0, n, gh),
        (st, every[n:], n, every.shape[0], None),
    ):
        xhat, scale = norm_stats(x_ref[0].astype(F32))
        back = norm_back(grad, xhat, scale, gain[...])
        if extra is not None:
            back = back + extra[0]
        out_ref[0, lo:hi, :] = back.astype(BF)
        stat_ref[0:1, :] += jnp.sum(grad * xhat, axis=0, keepdims=True)
        stat_ref[1:2, :] += jnp.sum(grad, axis=0, keepdims=True)


def qkv_grad_kernel(nf, pos, x, gq, gkv, far_ref, mid_ref, own_ref, acc, right):
    t = pl.program_id(0)
    rows, cols = gq.shape[1], gq.shape[2]
    tall = x.shape[1]
    right[:rows, :cols] = gq[0]
    right[rows:, :cols] = jnp.zeros((tall - rows, cols), BF)
    right[:, cols : 2 * cols] = gkv[0, 0]
    right[:, 2 * cols :] = gkv[1, 0]
    part = mm_tn(x[0], right[...])

    @pl.when(t == 0)
    def _():
        acc[...] = part

    @pl.when(t > 0)
    def _():
        acc[...] += part

    @pl.when(t == pl.num_programs(0) - 1)
    def _():
        n = own_ref.shape[1]
        for f in range(nf):
            for flip, ref in ((0, own_ref), (2, mid_ref), (1, far_ref), (3, far_ref)):
                k = jnp.bitwise_xor(pos[0], flip)
                start = pl.multiple_of(f * (acc.shape[0] // nf) + k * n, n)
                piece = acc[pl.ds(start, n), :]
                if flip & 1:
                    ref[flip // 2, f] = piece.astype(BF)
                else:
                    ref[f] = piece


def order_kernel(sizes, places, *refs):
    outs = refs[-len(sizes) :]
    for i, block in enumerate(refs[: -len(sizes)]):
        lo = 0
        for n, out in zip(sizes, outs):
            out[0, pl.ds(pl.multiple_of(places[i] * n, n), n), :] = block[0, lo : lo + n, :]
            lo = lo + n


def finish_ff_kernel(rows, pos, *refs):
    gin, gout, gatt = refs[4:]
    depth, fc = gin.shape[0], refs[0].shape[1]
    for flip, b in zip((0, 2, 1, 3), refs[:4]):
        k = jnp.bitwise_xor(pos[0], flip)
        at = pl.ds(pl.multiple_of(k * fc, fc), fc)
        gin[:, at] = b[:depth, :].astype(F32)
        gout[at, :] = b[depth : 2 * depth, :].astype(F32).T
        att = pl.ds(pl.multiple_of(k * rows, rows), rows)
        for i in range(depth // fc):
            lo = 2 * depth + i * rows
            gatt[att, i * fc : (i + 1) * fc] = b[lo : lo + rows, :].astype(F32)


def finish_qkv_kernel(pos, *refs):
    for flip, b in zip((0, 2, 1, 3), refs[:4]):
        n = b.shape[0]
        at = pl.ds(pl.multiple_of(jnp.bitwise_xor(pos[0], flip) * n, n), n)
        for i, out in enumerate(refs[4:]):
            cols = out.shape[1]
            out[at, :] = b[:, i * cols : (i + 1) * cols].astype(F32)


def build(mesh):
    nf, nc, nt = mesh.shape["fsdp"], mesh.shape["context"], mesh.shape["tensor"]
    assert nc == 4

    def px(x):
        return lax.ppermute(x, "fsdp", [(0, 1), (1, 0)])

    def pc(x, k):
        return lax.ppermute(x, "context", [(a, a ^ k) for a in range(nc)])

    def pz(x, j):
        return lax.ppermute(x, "tensor", [(a, (a - j) % nt) for a in range(nt)])

    def ps(x, j):
        return lax.ppermute(x, "tensor", [(a, (a + j) % nt) for a in range(nt)])

    def on_device(
        tokens,
        state,
        parent,
        seg_length,
        cell_gate,
        norm1_gain,
        norm1_shift,
        w_query,
        w_key,
        w_value,
        w_attn_out,
        rel_bias,
        norm2_gain,
        norm2_shift,
        w_in,
        w_out,
        cotangent,
    ):
        trees, rows, width = tokens.shape
        local_segs = seg_length.shape[1]
        seg = rows // local_segs
        all_segs = parent.shape[1]
        heads = rel_bias.shape[0]
        depth, cols = w_query.shape
        head_dim = cols // heads
        each = state.shape[1]
        tall = rows + each
        fi, ci, zi = lax.axis_index("fsdp"), lax.axis_index("context"), lax.axis_index("tensor")
        core = ci & 1
        zr, zs = rows // nt, each // nt
        mine = trees * zr
        pos = jnp.stack([ci, zi, fi]).astype(jnp.int32)
        cell, gain_1, shift_1, gain_2, shift_2 = (
            v.reshape(1, width)
            for v in (cell_gate, norm1_gain, norm1_shift, norm2_gain, norm2_shift)
        )
        sds = jax.ShapeDtypeStruct

        def gate(*xs):
            return lax.optimization_barrier(xs)

        stat = sds((8, width), F32)

        def call(body, grid, ins, outs, out_shape, scratch=(), prefetch=1, vmem=24, name="", us=4, keep=False):
            return hbm_call(
                prefetch,
                body,
                out_shape=out_shape,
                grid_spec=pltpu.PrefetchScalarGridSpec(
                    num_scalar_prefetch=prefetch,
                    grid=grid,
                    in_specs=ins,
                    out_specs=outs,
                    scratch_shapes=scratch,
                ),
                compiler_params=pltpu.CompilerParams(vmem_limit_bytes=vmem << 20),
                cost_estimate=cost(us),
                keep=keep,
                name=name,
            )

        def whole(shape):
            return pl.BlockSpec(shape, lambda *_: (0,) * len(shape))

        row_1 = whole((1, width))
        stat_spec = whole((8, width))

        def place(blocks, starts, axis, total):
            shape = list(blocks[0].shape)
            shape[axis] = total
            out = jnp.zeros(shape, blocks[0].dtype)
            for block, start in zip(blocks, starts):
                out = lax.dynamic_update_slice_in_dim(out, block, start, axis)
            return out

        def half_of(x, k, axis, parts):
            n = x.shape[axis] // parts
            return lax.dynamic_slice_in_dim(x, k * n, n, axis)

        def gather_f(x, axis):
            n = x.shape[axis]
            if nf == 2:
                return place([x, px(x)], [fi * n, (1 - fi) * n], axis, 2 * n)
            return lax.all_gather(x, "fsdp", axis=axis, tiled=True)

        def scatter_f(x, axis):
            if nf == 2:
                sent = half_of(x, 1 - fi, axis, 2).astype(BF)
                return half_of(x, fi, axis, 2) + px(sent).astype(F32)
            return lax.psum_scatter(
                x.astype(BF), "fsdp", scatter_dimension=axis, tiled=True
            ).astype(F32)

        def gather_c(x, axis):
            n = x.shape[axis]
            pair = jnp.stack([x, pc(x, 2)])
            over = pc(pair, 1)
            return place(
                [x, pair[1], over[0], over[1]],
                [ci * n, (ci ^ 2) * n, (ci ^ 1) * n, (ci ^ 3) * n],
                axis,
                nc * n,
            )

        def scatter_c(x, axis):
            cut = lambda k: half_of(x, k, axis, nc)
            sent = jnp.stack([cut(ci ^ 1), cut(ci ^ 3)]).astype(BF)
            got = pc(sent, 1).astype(F32)
            far = (cut(ci ^ 2) + got[1]).astype(BF)
            return cut(ci) + got[0] + pc(far, 2).astype(F32)

        if nf == 2:
            half = depth // 2
            near_send = jnp.concatenate(
                [half_of(w, core, 0, 2) for w in (w_query, w_key, w_value)], axis=1
            )
            near_send, w_in, w_out = gate(near_send, w_in, w_out)
            near_w = px(near_send)
            near_w, w_attn_out = gate(near_w, w_attn_out)
            over_w = pc(near_w, 1)
            weights = (w_query, w_key, w_value, near_w, over_w)
            weight_specs = [whole((depth, cols))] * 3 + [whole((half, 3 * cols))] * 2
            w_scratch = [pltpu.VMEM((2 * depth, 3 * cols), BF)]
        else:
            full_w = lax.all_gather(
                jnp.concatenate([w_query, w_key, w_value], axis=1), "fsdp", axis=0, tiled=True
            )
            weights = (full_w,)
            weight_specs = [whole(full_w.shape)]
            w_scratch = []

        fc = w_in.shape[1] // nc
        pack = jnp.stack([half_of(w_in, ci, 1, nc), half_of(w_out, ci, 0, nc).T])
        packs = lax.all_gather(pack, ("tensor", "fsdp"), axis=0, tiled=False)
        packs = packs.reshape(nt, nf, 2, depth, fc)

        o_blocks = [w_attn_out] + [pz(w_attn_out, j) for j in range(1, nt)]
        o_over = [px(w_attn_out)] if nf == 2 else []

        normed = call(
            norm_kernel,
            (trees,),
            [
                row_1,
                row_1,
                pl.BlockSpec((1, rows, width), lambda t: (t, 0, 0)),
                pl.BlockSpec((1, each, width), lambda t: (t, 0, 0)),
            ],
            pl.BlockSpec((1, tall, width), lambda t: (t, 0, 0)),
            sds((trees, tall, width), BF),
            prefetch=0,
            name="norm",
            us=5,
        )(gain_1, shift_1, tokens, state)
        tile = tall // 3
        queries, kv = call(
            project_kernel,
            (trees, 3),
            [pl.BlockSpec((1, tile, width), lambda t, i, *_: (t, i, 0))] + weight_specs,
            (
                pl.BlockSpec((1, tile, cols), lambda t, i, *_: (t, i, 0)),
                pl.BlockSpec((1, tile, 2 * cols), lambda t, i, *_: (t, i, 0)),
            ),
            (sds((trees, tall, cols), BF), sds((trees, tall, 2 * cols), BF)),
            w_scratch,
            name="project",
        )(pos, normed, *weights)
        kv_y = pc(kv, 2)
        kv_c = pc(kv, 1)
        grad_low = half_of(cotangent, zi, 1, nt).reshape(mine, width)
        kv_y, grad_low, *o_blocks = gate(kv_y, grad_low, *o_blocks)
        kv_cy = pc(kv_y, 1)
        if nf == 2:
            o_over += [px(b) for b in o_blocks[1:]]
        else:
            full = lax.all_gather(jnp.stack(o_blocks), "fsdp", axis=2, tiled=True)
            o_blocks = [full[j] for j in range(nt)]
        grad_y = pc(grad_low, 2)
        grad_c = pc(grad_low, 1)

        forward, backward = attention_calls(
            trees, heads, local_segs, all_segs, seg, each, head_dim, nt
        )
        tables = (parent, seg_length, pos, rel_bias)
        sources = (queries, kv, kv_c, kv_y, kv_cy, kv, kv_c, kv_y, kv_cy)
        *att_send, log_total = forward(*tables, *sources)
        quarter = jnp.concatenate(
            [half_of(w, ci, 0, nc) for w in (w_query, w_key, w_value)], axis=1
        )
        att_send[0], quarter, grad_y, *o_over = gate(att_send[0], quarter, grad_y, *o_over)
        all_w = lax.all_gather(quarter, ("tensor", "fsdp", "context"), axis=0, tiled=False)
        all_w = all_w.reshape(nt, nf * depth, 3 * cols)
        grad_rows = [grad_low, grad_y, grad_c, pc(grad_y, 1)]

        att = [att_send[0]] + [pz(att_send[j], j) for j in range(1, nt)]
        chunk = pl.BlockSpec((1, zr, width), lambda t, *_: (t, 0, 0))
        chunk_z = pl.BlockSpec((1, zr, width), lambda t, pos: (t, pos[1], 0))
        small = pl.BlockSpec((1, zr, cols), lambda t, *_: (t, 0, 0))
        o_all = tuple(o_blocks) + tuple(o_over)
        o_specs = [whole(o_all[0].shape)] * len(o_all)
        o_scratch = [pltpu.VMEM((nt * cols, width), BF)]
        hidden, normed_two, stat_a = call(
            functools.partial(mix_kernel, nt),
            (trees,),
            [small] * nt + o_specs + [chunk_z, row_1, row_1, row_1],
            (chunk, chunk, stat_spec),
            (sds((trees, zr, width), F32), sds((trees, zr, width), BF), stat),
            o_scratch,
            name="mix",
            keep=True,
        )(pos, *att, *o_all, tokens, cell, gain_2, shift_2)

        rows_two = normed_two.reshape(mine, width)
        rows_y = pc(rows_two, 2)
        ff_rows = [rows_two, rows_y, pc(rows_two, 1), pc(rows_y, 1)]
        block = whole((mine, width))
        units = nt * fc
        half_spec, full_spec = whole((2, mine, width)), whole((4, mine, units))
        half_sds, full_sds = sds((2, mine, width), BF), sds((4, mine, units), BF)
        gn_near, gn_far, active, grad_up = call(
            ff_kernel,
            (1,),
            [block] * 8 + [whole(packs.shape)],
            (half_spec, half_spec, full_spec, full_spec),
            (half_sds, half_sds, full_sds, full_sds),
            [pltpu.VMEM((4, mine, width), BF)] * 2 + [pltpu.VMEM((nt, width, fc), BF)] * 2,
            prefetch=0,
            vmem=48,
            name="feed",
            keep=True,
            us=20,
        )(*ff_rows, *grad_rows, packs)
        gn_got = pc(gn_far, 1)
        gn_mid = (gn_near[1].astype(F32) + gn_got[1].astype(F32)).astype(BF)
        gn_end = pc(gn_mid, 2)
        unit_spec = pl.BlockSpec((4, mine, fc), lambda z, *_: (0, 0, z))
        pack_spec = pl.BlockSpec((1,) + packs.shape[1:], lambda z, *_: (z, 0, 0, 0, 0))
        ff_sent, ff_near, ff_far = call(
            ff_grad_kernel,
            (nt,),
            [block] * 8 + [unit_spec, unit_spec, pack_spec],
            (
                pl.BlockSpec((nf, 1, 2, depth, fc), lambda z, *_: (0, z, 0, 0, 0)),
                half_spec,
                half_spec,
            ),
            (sds((nf, nt, 2, depth, fc), BF), half_sds, half_sds),
            [pltpu.VMEM((4 * mine, width), BF)] * 2
            + [pltpu.VMEM((4 * mine, width), F32), pltpu.VMEM((width, fc), BF)],
            prefetch=0,
            vmem=56,
            name="feed_grads",
            keep=True,
            us=16,
        )(*ff_rows, *grad_rows, active, grad_up, packs)
        gn_end, ff_sent, ff_near, ff_far = gate(gn_end, ff_sent, ff_near, ff_far)
        ff_got = pc(ff_far, 1)

        pair = pl.BlockSpec((1, 1, zr, width), lambda t, *_: (0, t, 0, 0))
        grad_hidden, grad_branch, *rest = call(
            functools.partial(branch_back_kernel, nt),
            (trees,),
            o_specs + [pair, pair, chunk, chunk, chunk_z, row_1, row_1],
            (chunk, chunk) + (small,) * nt + (stat_spec,),
            (sds((trees, zr, width), F32), sds((trees, zr, width), BF))
            + (sds((trees, zr, cols), BF),) * nt
            + (stat,),
            o_scratch,
            name="branch_back",
            keep=True,
        )(
            pos,
            *o_all,
            gn_near.reshape(2, trees, zr, width),
            gn_got.reshape(2, trees, zr, width),
            gn_end.reshape(trees, zr, width),
            hidden,
            cotangent,
            cell,
            gain_2,
        )
        stat_b = rest.pop()
        ff_got, grad_branch, *rest = gate(ff_got, grad_branch, *rest)
        grad_heads = [rest[0]] + [ps(rest[j], j) for j in range(1, nt)]
        ff_mid = (ff_near[1].astype(F32) + ff_got[1].astype(F32)).astype(BF)
        ff_end = pc(ff_mid, 2)
        part_attn = mm_tn(
            jnp.concatenate([a.reshape(mine, cols) for a in att], axis=1),
            grad_branch.reshape(mine, width),
        ).reshape(nt, cols, width)
        cut = lambda k: half_of(part_attn, k, 1, nc)
        attn_got = pc(jnp.stack([cut(ci ^ 1), cut(ci ^ 3)]).astype(BF), 1).astype(F32)
        attn_near = cut(ci) + attn_got[0]
        attn_mid = (cut(ci ^ 2) + attn_got[1]).astype(BF)

        mlp_out = ff_near[0].astype(F32) + ff_got[0].astype(F32) + ff_end.astype(F32)
        result = (hidden.reshape(mine, width) + mlp_out).astype(BF)
        result, attn_near, attn_mid, *grad_heads = gate(
            result, attn_near, attn_mid, *grad_heads
        )
        result = result.reshape(trees, zr, width)
        o_rows = cols // nc

        def spread_near(x):
            if nt == 4:
                return [
                    lax.ppermute(x, "tensor", [(0, 1), (1, 2), (2, 3)]),
                    lax.ppermute(x, "tensor", [(1, 0), (2, 1), (3, 2)]),
                ]
            return [pz(x, 1), pz(x, nt - 1)]

        def ordered(blocks, places, sizes):
            n = blocks[0].shape[1]
            return call(
                functools.partial(order_kernel, sizes),
                (trees,),
                [pl.BlockSpec((1, n, width), lambda t, *_: (t, 0, 0))] * len(blocks),
                tuple(
                    pl.BlockSpec((1, nt * m, width), lambda t, *_: (t, 0, 0)) for m in sizes
                ),
                tuple(sds((trees, nt * m, width), BF) for m in sizes),
                name="order",
                us=1,
            )(jnp.stack(places).astype(jnp.int32), *blocks)

        def swap(x, pairs):
            return lax.ppermute(x, "tensor", pairs + [(b, a) for a, b in pairs])

        first_at = [jnp.maximum(zi - 1, 0), jnp.minimum(zi + 1, nt - 1), zi]
        ends = (zi == 0) | (zi == 3)

        out_near = spread_near(result)
        attn_end = pc(attn_mid, 2)

        *dq_send, grad_q, kv_near, kv_far, bias_rows = backward(
            *tables, *sources, *grad_heads, log_total
        )
        ff_half = lax.psum_scatter(ff_sent, "fsdp", scatter_dimension=0, tiled=True)[0]
        ff_half = ff_half.reshape(nt, 2 * depth, fc)
        kv_far, kv_near, attn_end, *out_near = gate(kv_far, kv_near, attn_end, *out_near)
        kv_got = pc(kv_far, 1)
        kv_mid = (kv_near[1].astype(F32) + kv_got[1].astype(F32)).astype(BF)
        kv_mid, result, attn_end, ff_half = gate(kv_mid, result, attn_end, ff_half)
        kv_end = pc(kv_mid, 2)
        if nt == 4:
            out_far = [swap(result, [(0, 3)]), swap(result, [(0, 2), (1, 3)])]
        else:
            out_far = [pz(result, j) for j in range(2, nt - 1)]
        attn_sum = attn_near + attn_end.astype(F32)
        attn_sum = scatter_f(attn_sum, 2).astype(BF)
        attn_sum = lax.dynamic_slice_in_dim(
            jnp.concatenate([attn_sum, attn_sum], axis=0), nt - zi, nt, 0
        )
        if depth == 2 * fc:
            ff_half = jnp.concatenate(
                [ff_half, attn_sum[:, :, :fc], attn_sum[:, :, fc:]], axis=1
            )
        kv_end, ff_half, attn_sum, *out_far = gate(kv_end, ff_half, attn_sum, *out_far)
        own = lax.psum_scatter(ff_half, "tensor", scatter_dimension=0, tiled=True)[0]
        five = pl.BlockSpec((1, 1, 1, tall, cols), lambda t, k, *_: (0, k, t, 0, 0))
        four = pl.BlockSpec((1, 1, tall, cols), lambda t, k, *_: (k, t, 0, 0))
        send = pl.BlockSpec((3, 1, zr + zs, cols), lambda t, k, *_: (0, t, 0, 0))
        grad_kv, *kv_send = call(
            functools.partial(combine_kernel, rows),
            (trees, 2),
            [five, five, four]
            + [pl.BlockSpec((1, zr, cols), lambda t, k, *_: (t, 0, 0))] * nt,
            (four,) + (send,) * nt,
            (sds((2, trees, tall, cols), BF),) + (sds((3, trees, zr + zs, cols), BF),) * nt,
            name="combine",
            keep=True,
        )(pos, kv_near, kv_got, kv_end, *dq_send)
        dqkv = [kv_send[0]] + [pz(kv_send[j], j) for j in range(1, nt)]

        dq_rows = depth // nc
        cut_specs = (whole((2, nf, dq_rows, 3 * cols)),) + (whole((nf, dq_rows, 3 * cols)),) * 2
        qkv_far, qkv_mid, qkv_own = call(
            functools.partial(qkv_grad_kernel, nf),
            (trees,),
            [
                pl.BlockSpec((1, tall, width), lambda t, *_: (t, 0, 0)),
                pl.BlockSpec((1, rows, cols), lambda t, *_: (t, 0, 0)),
                pl.BlockSpec((2, 1, tall, cols), lambda t, *_: (0, t, 0, 0)),
            ],
            cut_specs,
            (
                sds((2, nf, dq_rows, 3 * cols), BF),
                sds((nf, dq_rows, 3 * cols), F32),
                sds((nf, dq_rows, 3 * cols), F32),
            ),
            [pltpu.VMEM((nf * depth, 3 * cols), F32), pltpu.VMEM((tall, 3 * cols), BF)],
            name="qkv_grads",
            keep=True,
            us=8,
        )(pos, normed, grad_q, grad_kv)
        if nt == 4:
            places = [first_at[0], first_at[1], jnp.where(ends, 3 - zi, zi), zi, zi ^ 2]
            blocks = [out_near[0], out_near[1], out_far[0], result, out_far[1]]
        else:
            blocks = [result, *out_near, *out_far]
            places = [zi, (zi + 1) % nt, (zi - 1) % nt] + [(zi + j) % nt for j in range(2, nt - 1)]
        (output,) = ordered(blocks, places, (zr,))
        qkv_far, qkv_mid, qkv_own, output, *dqkv = gate(
            qkv_far, qkv_mid, qkv_own, output, *dqkv
        )
        qkv_got = pc(qkv_far, 1).astype(F32)

        chunk_sz = pl.BlockSpec((1, zs, width), lambda t, pos: (t, pos[1], 0))
        grads_own, stat_c = call(
            functools.partial(input_back_kernel, nt),
            (trees,),
            [pl.BlockSpec((3, 1, zr + zs, cols), lambda t, *_: (0, t, 0, 0))] * nt
            + [whole(all_w.shape), chunk_z, chunk_sz, chunk, row_1],
            (pl.BlockSpec((1, zr + zs, width), lambda t, *_: (t, 0, 0)), stat_spec),
            (sds((trees, zr + zs, width), BF), stat),
            vmem=32,
            name="input_back",
            keep=True,
        )(pos, *dqkv, all_w, tokens, state, grad_hidden, gain_1)
        qkv_got, grads_own = gate(qkv_got, grads_own)

        bias_own = jnp.sum(bias_rows, axis=2)
        bias_all = lax.dynamic_update_slice(
            jnp.zeros((heads * nt, BUCKETS), F32), bias_own, (zi * heads, 0)
        )
        squares = jnp.stack([jnp.sum(stat_a[0]), jnp.sum(stat_a[1]), jnp.sum(mlp_out * mlp_out)])
        spare = jnp.zeros((2 * width - bias_all.size - 3,), F32)
        early = jnp.concatenate(
            [
                stat_b[:2],
                jnp.concatenate([bias_all.reshape(-1), squares, spare]).reshape(2, width),
            ],
            axis=0,
        )
        early, grads_own = gate(early, grads_own)
        sums = jnp.concatenate([stat_c[:2], early], axis=0)

        in_near = spread_near(grads_own)
        if nt == 4:
            in_far = [swap(grads_own, [(0, 2), (1, 3)])]
        else:
            in_far = [pz(grads_own, j) for j in range(2, nt - 1)]
        qkv_end = pc((qkv_mid + qkv_got[1]).astype(BF), 2)
        if depth == 2 * fc:
            parts = [own]
        else:
            parts = [own, lax.psum_scatter(attn_sum, "tensor", scatter_dimension=0, tiled=True)[0]]
        parts_y = [pc(p, 2) for p in parts]
        sums = sums + px(sums) if nf == 2 else lax.psum(sums, "fsdp")
        sums = sums + pc(sums, 1)
        sums = sums + pc(sums, 2)
        in_far[0], qkv_end, sums, *parts_y = gate(in_far[0], qkv_end, sums, *parts_y)
        if nt == 4:
            in_far.append(
                lax.ppermute(in_far[0], "tensor", [(2, 3), (1, 0), (3, 2), (0, 1)])
            )
            places = first_at + [zi ^ 2, 3 - zi]
            blocks = [in_near[0], in_near[1], grads_own, in_far[0], in_far[1]]
        else:
            blocks = [grads_own, *in_near, *in_far]
        tokens_grad, state_grad = ordered(blocks, places, (zr, zs))
        if nt & (nt - 1):
            sums = lax.psum(sums, "tensor")
        else:
            k = 1
            while k < nt:
                sums = sums + lax.ppermute(sums, "tensor", [(a, a ^ k) for a in range(nt)])
                k = 2 * k

        qkv_sum = scatter_f(qkv_own + qkv_got[0] + qkv_end.astype(F32), 0)[0].astype(BF)
        qkv_y = pc(qkv_sum, 2)
        qkv_blocks = (qkv_sum, qkv_y, pc(qkv_sum, 1), pc(qkv_y, 1))
        grad_qkv = call(
            finish_qkv_kernel,
            (1,),
            [whole((dq_rows, 3 * cols))] * 4,
            (whole((depth, cols)),) * 3,
            (sds((depth, cols), F32),) * 3,
            name="finish_qkv",
            us=1,
        )(pos, *qkv_blocks)
        over = [pc(p, 1) for p in parts] + [pc(p, 1) for p in parts_y]
        if depth == 2 * fc:
            grad_in, grad_out, grad_attn_out = call(
                functools.partial(finish_ff_kernel, o_rows),
                (1,),
                [whole(own.shape)] * 4,
                (whole((depth, nc * fc)), whole((nc * fc, depth)), whole((nc * o_rows, depth))),
                (
                    sds((depth, nc * fc), F32),
                    sds((nc * fc, depth), F32),
                    sds((nc * o_rows, depth), F32),
                ),
                name="finish_ff",
                us=1,
            )(pos, own, parts_y[0], over[0], over[1])
        else:
            flips = (ci, ci ^ 2, ci ^ 1, ci ^ 3)
            ff_blocks = [parts[0], parts_y[0], over[0], over[2]]
            at = [k * fc for k in flips]
            grad_in = place([b[:depth] for b in ff_blocks], at, 1, nc * fc).astype(F32)
            grad_out = place([b[depth:].T for b in ff_blocks], at, 0, nc * fc).astype(F32)
            grad_attn_out = place(
                [parts[1], parts_y[1], over[1], over[3]],
                [k * o_rows for k in flips],
                0,
                nc * o_rows,
            ).astype(F32)

        last = sums[4:].reshape(-1)
        bias_sum = last[: bias_all.size].reshape(bias_all.shape)
        grad_bias = lax.dynamic_slice_in_dim(bias_sum, zi * heads, heads, 0)
        cell_count = trees * rows * width * nf * nc
        norms = jnp.sqrt(last[bias_all.size : bias_all.size + 3] / cell_count)
        return (
            output,
            tokens_grad,
            state_grad,
            *grad_qkv,
            grad_attn_out,
            grad_bias,
            sums[0],
            sums[1],
            sums[2],
            sums[3],
            grad_in,
            grad_out,
            norms,
        )

    return on_device


def solution(mesh):
    return jax.shard_map(
        build(mesh),
        mesh=mesh,
        in_specs=(
            P("fsdp", "context", None),
            P("fsdp", "context", None),
            P("fsdp", None),
            P("fsdp", "context"),
            P(),
            P(),
            P(),
            P("fsdp", "tensor"),
            P("fsdp", "tensor"),
            P("fsdp", "tensor"),
            P("tensor", "fsdp"),
            P("tensor", None),
            P(),
            P(),
            P("fsdp", "tensor"),
            P("tensor", "fsdp"),
            P("fsdp", "context", None),
        ),
        out_specs=(
            P("fsdp", "context", None),
            P("fsdp", "context", None),
            P("fsdp", "context", None),
            P("fsdp", "tensor"),
            P("fsdp", "tensor"),
            P("fsdp", "tensor"),
            P("tensor", "fsdp"),
            P("tensor", None),
            P(),
            P(),
            P(),
            P(),
            P("fsdp", "tensor"),
            P("tensor", "fsdp"),
            P(),
        ),
        check_vma=False,
    )
```

```python
import functools
import math

import jax
import jax.numpy as jnp
from jax import lax
from jax.experimental import pallas as pl
from jax.experimental.pallas import tpu as pltpu
from jax.sharding import PartitionSpec as P

WINDOW = 512
BUCKETS = 32
REACH = 128
EPSILON = 1e-05
MASKED = -1e30
GELU_C = 0.7978845608028654
GELU_A = 0.044715
BF = jnp.bfloat16
F32 = jnp.float32


def cost(us):
    return pl.CostEstimate(
        flops=int(us * 1e9), transcendentals=0, bytes_accessed=int(us * 3e6)
    )


def bucket_edges(bucket_total, far_reach, window):
    exact_count = bucket_total // 2
    boundaries = []
    current = 0
    for distance in range(window):
        if distance < exact_count:
            bucket = distance
        else:
            bucket = exact_count + int(
                math.log(distance / exact_count)
                / math.log(far_reach / exact_count)
                * (bucket_total - exact_count)
            )
            bucket = min(bucket, bucket_total - 1)
        while current < bucket:
            current = current + 1
            boundaries.append(distance)
    return boundaries


EDGES = bucket_edges(BUCKETS, REACH, WINDOW)


def mm(left, right):
    return lax.dot_general(left, right, (((1,), (0,)), ((), ())), preferred_element_type=F32)


def mm_nt(left, right):
    return lax.dot_general(left, right, (((1,), (1,)), ((), ())), preferred_element_type=F32)


def mm_tn(left, right):
    return lax.dot_general(left, right, (((0,), (0,)), ((), ())), preferred_element_type=F32)


def bias_tables(rb_ref, h, levels, seg, bm_ref):
    key = lax.broadcasted_iota(jnp.int32, (seg, seg), 0)
    query = lax.broadcasted_iota(jnp.int32, (seg, seg), 1)
    for lev in range(levels):
        dist = lev * seg + query - key
        low, high = lev * seg - (seg - 1), lev * seg + seg - 1
        if low >= EDGES[-1]:
            val = jnp.full((seg, seg), rb_ref[h, BUCKETS - 1], F32)
        else:
            val = jnp.full((seg, seg), rb_ref[h, 0], F32)
            for i, edge in enumerate(EDGES):
                if edge <= high:
                    val = jnp.where(dist >= edge, rb_ref[h, i + 1], val)
        if low < 0:
            val = jnp.where(dist >= 0, val, MASKED)
        if high >= WINDOW:
            val = jnp.where(dist < WINDOW, val, MASKED)
        bm_ref[lev * seg : (lev + 1) * seg, :] = val


def chain(par_ref, t, first, levels, all_segs, local_segs, ctx):
    out = []
    anc = first
    for lev in range(levels):
        if lev > 0:
            up = par_ref[t, jnp.maximum(anc, 0)]
            anc = jnp.where(anc >= 0, up, -1)
        safe = jnp.maximum(anc, 0)
        owner = lax.div(safe, local_segs)
        out.append((anc >= 0, jnp.bitwise_xor(owner, ctx), safe - owner * local_segs))
    return out


def window_score(raw, lev, bm_ref, line, length, seg):
    part = raw + bm_ref[lev * seg : (lev + 1) * seg, :]
    if lev == 0:
        key = lax.broadcasted_iota(jnp.int32, (seg, 1), 0)
        return part + jnp.where(key < length, 0.0, MASKED)
    return part + jnp.where(line[lev][0], 0.0, MASKED)


def fold(value, op):
    out = value[0:8]
    for i in range(8, value.shape[0], 8):
        out = op(out, value[i : i + 8])
    return out


def attend_kernel(dims, par_ref, len_ref, pos_ref, rb_ref, q_ref, *refs):
    levels, seg, local_segs, all_segs, factor, nt = dims
    parts_k, parts_v = refs[0:4], refs[4:8]
    att_refs, lse_ref = refs[8 : 8 + nt], refs[8 + nt]
    kall, vall_t, kws, vw_ts, bm, whole, q_t, raws_a, probs_a = refs[9 + nt :]
    t, h = pl.program_id(0), pl.program_id(1)
    ctx, zi = pos_ref[0], pos_ref[1]
    rows, win = local_segs * seg, levels * seg
    each = (kws.shape[1] - win) // 4
    blocks = kws.shape[1] // seg
    bias_tables(rb_ref, h, levels, seg, bm)
    for b in range(4):
        at = slice(win + b * each, win + (b + 1) * each)
        kall[b] = parts_k[b][0, :rows, :]
        turned = parts_v[b][0].T
        vall_t[b] = turned[:, :rows]
        for i in range(2):
            kws[i, at, :] = parts_k[b][0, rows:, :]
            vw_ts[i, :, at] = turned[:, rows:]
    q_t[...] = q_ref[0, :rows, :].T

    def one(s, carry):
        kw, vw_t, raws, probs = (r.at[s % 2] for r in (kws, vw_ts, raws_a, probs_a))
        line = chain(par_ref, t, ctx * local_segs + s, levels, all_segs, local_segs, ctx)
        for lev, (_, part, block) in enumerate(line):
            start = pl.ds(pl.multiple_of(block * seg, seg), seg)
            kw[lev * seg : (lev + 1) * seg, :] = kall[part, start, :]
            vw_t[:, lev * seg : (lev + 1) * seg] = vall_t[part, :, start]
        at = slice(s * seg, (s + 1) * seg)
        turned = q_t[:, at]
        top = None
        for c in range(blocks):
            raw = mm(kw[c * seg : (c + 1) * seg, :], turned) * factor
            if c < levels:
                raw = window_score(raw, c, bm, line, len_ref[t, s], seg)
            raws[c * seg : (c + 1) * seg, :] = raw
            high = fold(raw, jnp.maximum)
            top = high if top is None else jnp.maximum(top, high)
        top = jnp.max(top, axis=0, keepdims=True)
        total = None
        for c in range(blocks):
            prob = jnp.exp(raws[c * seg : (c + 1) * seg, :] - top)
            probs[c * seg : (c + 1) * seg, :] = prob.astype(BF)
            part = fold(prob, jnp.add)
            total = part if total is None else total + part
        total = jnp.sum(total, axis=0, keepdims=True)
        lse_ref[0, 0, 0:1, at] = top + jnp.log(total)
        att = mm(vw_t[...], probs[...]) / total
        whole[at, :] = att.T.astype(BF)
        return carry

    for s in range(local_segs):
        one(s, 0)
    n = rows // nt
    for j in range(nt):
        k = lax.rem(zi - j + nt, nt)
        att_refs[j][0] = whole[pl.ds(pl.multiple_of(k * n, n), n), :]


def attend_back_kernel(dims, par_ref, len_ref, pos_ref, rb_ref, q_ref, *refs):
    levels, seg, local_segs, all_segs, factor, nt = dims
    parts_k, parts_v = refs[0:4], refs[4:8]
    do_refs, lse_ref = refs[8 : 8 + nt], refs[8 + nt]
    dq_refs = refs[9 + nt : 9 + 2 * nt]
    dq_ref, near_ref, far_ref, db_ref = refs[9 + 2 * nt : 13 + 2 * nt]
    kall, vall, kall_t, kws, vws, kw_ts, bm, dk, dv, near, far, dos, do_t, q_t, raws_a, dps_a, dss_a, pbs_a = refs[
        13 + 2 * nt :
    ]
    h, t = pl.program_id(0), pl.program_id(1)
    ctx, zi = pos_ref[0], pos_ref[1]
    rows, win = local_segs * seg, levels * seg
    each = (kws.shape[1] - win) // 4
    blocks = kws.shape[1] // seg
    n = rows // nt
    bias_tables(rb_ref, h, levels, seg, bm)
    for b in range(4):
        at = slice(win + b * each, win + (b + 1) * each)
        kall[b] = parts_k[b][0, :rows, :]
        vall[b] = parts_v[b][0, :rows, :]
        turned = parts_k[b][0].T
        kall_t[b] = turned[:, :rows]
        for i in range(2):
            kws[i, at, :] = parts_k[b][0, rows:, :]
            vws[i, at, :] = parts_v[b][0, rows:, :]
            kw_ts[i, :, at] = turned[:, rows:]
    dk[...] = jnp.zeros(dk.shape, F32)
    dv[...] = jnp.zeros(dv.shape, F32)
    for j in range(nt):
        k = lax.rem(zi - j + nt, nt)
        dos[pl.ds(pl.multiple_of(k * n, n), n), :] = do_refs[j][0]
    q_t[...] = q_ref[0, :rows, :].T
    do_t[...] = dos[...].T

    @pl.when(t == 0)
    def _():
        near[...] = jnp.zeros(near.shape, F32)
        far[...] = jnp.zeros(far.shape, F32)

    def one(s, carry):
        kw, vw, kw_t = (r.at[s % 2] for r in (kws, vws, kw_ts))
        raws, dps, dss, pbs = (r.at[s % 2] for r in (raws_a, dps_a, dss_a, pbs_a))
        line = chain(par_ref, t, ctx * local_segs + s, levels, all_segs, local_segs, ctx)
        for lev, (_, part, block) in enumerate(line):
            start = pl.ds(pl.multiple_of(block * seg, seg), seg)
            at = slice(lev * seg, (lev + 1) * seg)
            kw[at, :] = kall[part, start, :]
            vw[at, :] = vall[part, start, :]
            kw_t[:, at] = kall_t[part, :, start]
        at = slice(s * seg, (s + 1) * seg)
        turned, do_turned = q_t[:, at], do_t[:, at]
        lse = lse_ref[0, 0, 0:1, at]
        delta = None
        for c in range(blocks):
            cut = slice(c * seg, (c + 1) * seg)
            raw = mm(kw[cut, :], turned) * factor
            if c < levels:
                raw = window_score(raw, c, bm, line, len_ref[t, s], seg)
            prob = jnp.exp(raw - lse)
            dprob = mm(vw[cut, :], do_turned)
            raws[cut, :] = prob
            dps[cut, :] = dprob
            pbs[cut, :] = prob.astype(BF)
            part = fold(prob * dprob, jnp.add)
            delta = part if delta is None else delta + part
        delta = jnp.sum(delta, axis=0, keepdims=True)
        for c in range(blocks):
            cut = slice(c * seg, (c + 1) * seg)
            dscore = (raws[cut, :] * (dps[cut, :] - delta)).astype(BF)
            dss[cut, :] = dscore
            if c < 2:
                near[cut, :] += dscore.astype(F32)
            elif c < levels:
                far[...] += dscore.astype(F32)
        dq = mm(kw_t[...], dss[...]) * factor
        dq_ref[0, at, :] = dq.T.astype(BF)
        q, do = q_ref[0, at, :], dos[at, :]
        for c in range(blocks):
            cut = slice(c * seg, (c + 1) * seg)
            gk = mm(dss[cut, :], q) * factor
            gv = mm(pbs[cut, :], do)
            if c < levels:
                _, part, block = line[c]
                to = pl.ds(pl.multiple_of(block * seg, seg), seg)
                dk[part, to, :] += gk
                dv[part, to, :] += gv
            else:
                for i in range(0, seg, each):
                    b = ((c - levels) * seg + i) // each
                    dk[b, rows:, :] += gk[i : i + each]
                    dv[b, rows:, :] += gv[i : i + each]
        return carry

    for s in range(local_segs):
        one(s, 0)
    for ref, pair in ((near_ref, (0, 2)), (far_ref, (1, 3))):
        for place, b in enumerate(pair):
            ref[place, 0, 0] = dk[b].astype(BF)
            ref[place, 1, 0] = dv[b].astype(BF)
    for j in range(nt):
        k = lax.rem(zi - j + nt, nt)
        dq_refs[j][0] = dq_ref[0, pl.ds(pl.multiple_of(k * n, n), n), :]

    @pl.when(t == pl.num_programs(1) - 1)
    def _():
        key = lax.broadcasted_iota(jnp.int32, (seg, seg), 0)
        query = lax.broadcasted_iota(jnp.int32, (seg, seg), 1)
        edges = [-(10**6)] + list(EDGES) + [10**6]
        for b in range(BUCKETS):
            total = far[...] if b == BUCKETS - 1 else jnp.zeros((seg, seg), F32)
            for lev in range(2):
                dist = lev * seg + query - key
                inside = (dist >= edges[b]) & (dist < edges[b + 1])
                total = total + jnp.where(inside, near[lev * seg : (lev + 1) * seg, :], 0.0)
            db_ref[0, b : b + 1, :] = jnp.sum(total, axis=0, keepdims=True)


def hbm_call(prefetch, body, out_shape, keep=False, **kw):
    if not keep:
        return pl.pallas_call(body, out_shape=out_shape, **kw)
    several = isinstance(out_shape, tuple)
    outs = tuple(
        pltpu.HBM(o.shape, o.dtype) for o in (out_shape if several else (out_shape,))
    )
    kernel = pl.pallas_call(body, out_shape=outs if several else outs[0], **kw)

    def run(*args):
        rest = [pltpu.with_memory_space_constraint(a, pltpu.HBM) for a in args[prefetch:]]
        return kernel(*args[:prefetch], *rest)

    return run


def attention_calls(trees, heads, local_segs, all_segs, seg, each, head_dim, nt):
    levels = WINDOW // seg + 1
    rows = local_segs * seg
    tall = rows + each
    win = levels * seg
    wide = win + 4 * each
    factor = head_dim ** (-0.5)
    dims = (levels, seg, local_segs, all_segs, factor, nt)
    assert EDGES[-1] <= 2 * seg - (seg - 1)
    assert seg == head_dim == 128 and wide % seg == 0 and seg % each == 0
    vm = lambda dt, *shape: pltpu.VMEM(shape, dt)
    forward_scratch = [
        vm(BF, 4, rows, head_dim),
        vm(BF, 4, head_dim, rows),
        vm(BF, 2, wide, head_dim),
        vm(BF, 2, head_dim, wide),
        vm(F32, win, seg),
        vm(BF, rows, head_dim),
        vm(BF, head_dim, rows),
        vm(F32, 2, wide, seg),
        vm(BF, 2, wide, seg),
    ]
    backward_scratch = [
        vm(BF, 4, rows, head_dim),
        vm(BF, 4, rows, head_dim),
        vm(BF, 4, head_dim, rows),
        vm(BF, 2, wide, head_dim),
        vm(BF, 2, wide, head_dim),
        vm(BF, 2, head_dim, wide),
        vm(F32, win, seg),
        vm(F32, 4, tall, head_dim),
        vm(F32, 4, tall, head_dim),
        vm(F32, 2 * seg, seg),
        vm(F32, seg, seg),
        vm(BF, rows, head_dim),
        vm(BF, head_dim, rows),
        vm(BF, head_dim, rows),
        vm(F32, 2, wide, seg),
        vm(F32, 2, wide, seg),
        vm(BF, 2, wide, seg),
        vm(BF, 2, wide, seg),
    ]
    lse_shape = jax.ShapeDtypeStruct((trees, heads, 8, rows), F32)

    def specs(order):
        def at(col):
            return pl.BlockSpec(
                (1, tall, head_dim), lambda a, b, *_: (order(a, b)[0], 0, col(order(a, b)[1]))
            )

        k, v = at(lambda h: h), at(lambda h: heads + h)
        return [k, k, k, k, k, v, v, v, v]

    th = lambda a, b: (a, b)
    ht = lambda a, b: (b, a)
    chunk_shape = jax.ShapeDtypeStruct((trees, rows // nt, heads * head_dim), BF)

    def chunk_spec(order):
        return pl.BlockSpec(
            (1, rows // nt, head_dim), lambda a, b, *_: (order(a, b)[0], 0, order(a, b)[1])
        )

    forward = hbm_call(
        4,
        functools.partial(attend_kernel, dims),
        out_shape=(chunk_shape,) * nt + (lse_shape,),
        grid_spec=pltpu.PrefetchScalarGridSpec(
            num_scalar_prefetch=4,
            grid=(trees, heads),
            in_specs=specs(th),
            out_specs=(chunk_spec(th),) * nt
            + (pl.BlockSpec((1, 1, 8, rows), lambda t, h, *_: (t, h, 0, 0)),),
            scratch_shapes=forward_scratch,
        ),
        compiler_params=pltpu.CompilerParams(vmem_limit_bytes=24 << 20),
        cost_estimate=cost(16),
        keep=True,
        name="attend",
    )
    pair = jax.ShapeDtypeStruct((2, 2, trees, tall, heads * head_dim), BF)
    pair_spec = pl.BlockSpec((2, 2, 1, tall, head_dim), lambda h, t, *_: (0, 0, t, 0, h))
    backward = hbm_call(
        4,
        functools.partial(attend_back_kernel, dims),
        out_shape=(chunk_shape,) * nt
        + (
            jax.ShapeDtypeStruct((trees, rows, heads * head_dim), BF),
            pair,
            pair,
            jax.ShapeDtypeStruct((heads, BUCKETS, 128), F32),
        ),
        grid_spec=pltpu.PrefetchScalarGridSpec(
            num_scalar_prefetch=4,
            grid=(heads, trees),
            in_specs=specs(ht)
            + [chunk_spec(ht)] * nt
            + [pl.BlockSpec((1, 1, 8, rows), lambda h, t, *_: (t, h, 0, 0))],
            out_specs=(chunk_spec(ht),) * nt
            + (
                pl.BlockSpec((1, rows, head_dim), lambda h, t, *_: (t, 0, h)),
                pair_spec,
                pair_spec,
                pl.BlockSpec((1, BUCKETS, 128), lambda h, t, *_: (h, 0, 0)),
            ),
            scratch_shapes=backward_scratch,
        ),
        compiler_params=pltpu.CompilerParams(vmem_limit_bytes=32 << 20),
        cost_estimate=cost(24),
        keep=True,
        name="attend_back",
    )
    return forward, backward


def norm_stats(values):
    mean = jnp.mean(values, axis=-1, keepdims=True)
    centered = values - mean
    scale = lax.rsqrt(jnp.mean(centered * centered, axis=-1, keepdims=True) + EPSILON)
    return centered * scale, scale


def norm_back(grad, xhat, scale, gain):
    scaled = grad * gain
    first = jnp.mean(scaled, axis=-1, keepdims=True)
    second = jnp.mean(scaled * xhat, axis=-1, keepdims=True)
    return scale * (scaled - first - xhat * second)


def gelu_parts(u):
    square = u * u
    th = jnp.tanh(u * (GELU_C + GELU_C * GELU_A * square))
    half = 0.5 * (1.0 + th)
    slope = half + (0.5 * u) * (1.0 - th * th) * (GELU_C + 3.0 * GELU_C * GELU_A * square)
    return u * half, slope


def norm_kernel(gain, shift, tok, st, out):
    each = st.shape[1]
    rows = tok.shape[1]
    for lo in range(0, rows + each, each):
        x = (tok[0, lo : lo + each, :] if lo < rows else st[0]).astype(F32)
        xhat, _ = norm_stats(x)
        out[0, lo : lo + each, :] = (xhat * gain[...] + shift[...]).astype(BF)


def project_kernel(pos, x, *refs):
    if len(refs) == 3:
        w = refs[0]
        q_ref, kv_ref = refs[1:]
    else:
        wq, wk, wv, near, over, q_ref, kv_ref, w = refs

        @pl.when((pl.program_id(0) == 0) & (pl.program_id(1) == 0))
        def _():
            fi, core = pos[2], pos[0] & 1
            depth, cols = wq.shape
            half = depth // 2
            for i, part in enumerate((wq, wk, wv)):
                w[pl.ds(pl.multiple_of(fi * depth, depth), depth), i * cols : (i + 1) * cols] = (
                    part[...]
                )
            base = (1 - fi) * depth
            w[pl.ds(pl.multiple_of(base + core * half, half), half), :] = near[...]
            w[pl.ds(pl.multiple_of(base + (1 - core) * half, half), half), :] = over[...]

    y = mm(x[0], w[...]).astype(BF)
    cols = q_ref.shape[2]
    q_ref[0] = y[:, :cols]
    kv_ref[0] = y[:, cols:]


def load_projection(pos, blocks, w):
    rows, depth = blocks[0].shape
    n = w.shape[0] // rows
    for j in range(n):
        at = slice(j * rows, (j + 1) * rows)
        if n == len(blocks):
            w[at, :] = blocks[j][...]
        else:
            fi = pos[2]
            w[at, pl.ds(pl.multiple_of(fi * depth, depth), depth)] = blocks[j][...]
            w[at, pl.ds(pl.multiple_of((1 - fi) * depth, depth), depth)] = blocks[n][j]


def mix_kernel(n, pos, *refs):
    att, blocks = refs[:n], refs[n:-8]
    tok, cell, gain, shift, hid_ref, n2_ref, stat_ref, w = refs[-8:]

    load_projection(pos, blocks, w)
    stat_ref[...] = jnp.zeros(stat_ref.shape, F32)
    cols = att[0].shape[2]
    shape = tok.shape
    mine = shape[0] * shape[1]
    branch = None
    for j in range(n):
        part = mm(att[j][...].reshape(mine, cols), w[j * cols : (j + 1) * cols, :])
        branch = part if branch is None else branch + part
    x = tok[...].astype(F32).reshape(mine, shape[2])
    gated = cell[...] * branch
    hidden = x + gated
    hid_ref[...] = hidden.reshape(shape)
    xhat, _ = norm_stats(hidden)
    n2_ref[...] = (xhat * gain[...] + shift[...]).astype(BF).reshape(shape)
    stat_ref[0:1, :] = jnp.sum(x * x, axis=0, keepdims=True)
    stat_ref[1:2, :] = jnp.sum(gated * gated, axis=0, keepdims=True)


def ff_kernel(*refs):
    xs, gs = refs[0:2], refs[2:4]
    pack, first_ref, second_ref, act_ref, gup_ref, acc = refs[4:]
    nf, depth = pack.shape[1], pack.shape[3]
    z = pl.program_id(0)
    mine = xs[0].shape[0]
    cut = [slice(f * depth, (f + 1) * depth) for f in range(nf)]
    for p in range(2):
        up = mm(xs[p][:, cut[0]], pack[0, 0, 0])
        back = mm(gs[p][:, cut[0]], pack[0, 0, 1])
        for f in range(1, nf):
            up = up + mm(xs[p][:, cut[f]], pack[0, f, 0])
            back = back + mm(gs[p][:, cut[f]], pack[0, f, 1])
        value, slope = gelu_parts(up)
        act_ref[p] = value.astype(BF)
        gup = (back * slope).astype(BF)
        gup_ref[p] = gup
        at = slice(p * mine, (p + 1) * mine)
        for f in range(nf):
            part = mm_nt(gup, pack[0, f, 0])

            @pl.when(z == 0)
            def _():
                acc[at, cut[f]] = part

            @pl.when(z > 0)
            def _():
                acc[at, cut[f]] += part

    @pl.when(z == pl.num_programs(0) - 1)
    def _():
        first_ref[...] = acc[:mine, :].astype(BF)
        second_ref[...] = acc[mine:, :].astype(BF)


def ff_grad_kernel(*refs):
    xs, gs = refs[0:4], refs[4:8]
    act_a, gup_a, act_b, gup_b, pack = refs[8:13]
    sent_ref, near_ref, far_ref, xall, gall, acc, wout, act, gup = refs[13:]
    _, nf, _, depth, fc = pack.shape
    mine = xs[0].shape[0]

    @pl.when(pl.program_id(0) == 0)
    def _():
        for p in range(4):
            xall[p * mine : (p + 1) * mine, :] = xs[p][...]
            gall[p * mine : (p + 1) * mine, :] = gs[p][...]
        acc[...] = jnp.zeros(acc.shape, F32)

    for f in range(nf):
        wout[f * depth : (f + 1) * depth, :] = pack[0, f, 1]
    for half, (a_ref, u_ref) in enumerate(((act_a, gup_a), (act_b, gup_b))):
        for p in range(2):
            at = slice((2 * half + p) * mine, (2 * half + p + 1) * mine)
            act[at, :] = a_ref[p]
            gup[at, :] = u_ref[p]
    acc[...] += mm_nt(act[...], wout[...])
    for i, part in ((0, mm_tn(xall[...], gup[...])), (1, mm_tn(gall[...], act[...]))):
        for f in range(nf):
            sent_ref[f, 0, i] = part[f * depth : (f + 1) * depth].astype(BF)

    @pl.when(pl.program_id(0) == pl.num_programs(0) - 1)
    def _():
        for i, ref in enumerate((near_ref, far_ref)):
            for p in range(2):
                lo = (2 * p + i) * mine
                ref[p] = acc[lo : lo + mine, :].astype(BF)


def branch_back_kernel(nt, pos, *refs):
    blocks, (own, got, far, hid, cot, cell, gain) = refs[: -(nt + 11)], refs[-(nt + 11) : -(nt + 4)]
    gh_ref, gb_ref = refs[-(nt + 4) : -(nt + 2)]
    ga_refs, stat_ref, w = refs[-(nt + 2) : -2], refs[-2], refs[-1]

    load_projection(pos, blocks, w)
    stat_ref[...] = jnp.zeros(stat_ref.shape, F32)
    shape = cot.shape
    mine = shape[0] * shape[1]
    flat = lambda v: v.astype(F32).reshape(mine, shape[2])
    grad = flat(own[...]) + flat(got[...]) + flat(far[...])
    xhat, scale = norm_stats(flat(hid[...]))
    gh = flat(cot[...]) + norm_back(grad, xhat, scale, gain[...])
    gh_ref[...] = gh.reshape(shape)
    gb = (cell[...] * gh).astype(BF)
    gb_ref[...] = gb.reshape(shape)
    cols = ga_refs[0].shape[2]
    for j, ref in enumerate(ga_refs):
        ref[...] = mm_nt(gb, w[j * cols : (j + 1) * cols, :]).astype(BF).reshape(ref.shape)
    stat_ref[0:1, :] = jnp.sum(grad * xhat, axis=0, keepdims=True)
    stat_ref[1:2, :] = jnp.sum(grad, axis=0, keepdims=True)


def combine_kernel(rows, pos, own, got, far, *refs):
    nt = (len(refs) - 1) // 2
    dq, total_ref, send = refs[:nt], refs[nt], refs[nt + 1 :]
    total = (
        own[0, 0, 0].astype(F32) + got[0, 0, 0].astype(F32) + far[0, 0].astype(F32)
    ).astype(BF)
    total_ref[0, 0] = total
    n = rows // nt
    m = (total_ref.shape[2] - rows) // nt
    kv = pl.program_id(1)
    for j in range(nt):
        k = lax.rem(pos[1] - j + nt, nt)

        @pl.when(kv == 0)
        def _():
            send[j][0, 0, :n, :] = dq[j][0]
            send[j][0, 0, n:, :] = jnp.zeros((m, dq[j].shape[2]), BF)

        send[j][1 + kv, 0, :n, :] = total_ref[0, 0, pl.ds(pl.multiple_of(k * n, n), n), :]
        send[j][1 + kv, 0, n:, :] = total_ref[0, 0, pl.ds(pl.multiple_of(rows + k * m, m), m), :]


def input_back_kernel(nt, pos, *refs):
    blocks = refs[:nt]
    parts, (tok, st, gh, gain, out_ref, stat_ref, w, every) = refs[nt : nt + 4], refs[nt + 4 :]
    m = parts[0].shape[1]
    nf = parts[0].shape[0] // nt
    for flip, part in zip((0, 2, 1, 3), parts):
        for z in range(nt):
            for f in range(nf):
                at = (f * 4 + jnp.bitwise_xor(pos[0], flip)) * m
                w[z, pl.ds(pl.multiple_of(at, m), m), :] = part[z * nf + f]
    cols = blocks[0].shape[3]
    trees, n = tok.shape[0], tok.shape[1]
    tall = blocks[0].shape[2]
    total = None
    for j in range(nt):
        k = lax.rem(pos[1] + j, nt)
        for i in range(3):
            left = blocks[j][i].reshape(trees * tall, cols)
            part = mm_nt(left, w[k, :, i * cols : (i + 1) * cols])
            total = part if total is None else total + part
    every[...] = total
    stat_ref[...] = jnp.zeros(stat_ref.shape, F32)
    for t in range(trees):
        for x_ref, lo, hi, extra in ((tok, 0, n, gh), (st, n, tall, None)):
            grad = every[t * tall + lo : t * tall + hi, :]
            xhat, scale = norm_stats(x_ref[t].astype(F32))
            back = norm_back(grad, xhat, scale, gain[...])
            if extra is not None:
                back = back + extra[t]
            out_ref[t, lo:hi, :] = back.astype(BF)
            stat_ref[0:1, :] += jnp.sum(grad * xhat, axis=0, keepdims=True)
            stat_ref[1:2, :] += jnp.sum(grad, axis=0, keepdims=True)


def attn_grad_kernel(nt, pos, *refs):
    blocks, grad = refs[:nt], refs[nt]
    far_ref, mid_ref, own_ref, acc = refs[nt + 1 :]
    n = own_ref.shape[1]
    rows = grad.shape[0] * grad.shape[1]
    right = grad[...].reshape(rows, grad.shape[2])
    for j in range(nt):
        acc[...] = mm_tn(blocks[j][...].reshape(rows, acc.shape[0]), right)
        for flip, ref in ((0, own_ref), (2, mid_ref), (1, far_ref), (3, far_ref)):
            k = jnp.bitwise_xor(pos[0], flip)
            piece = acc[pl.ds(pl.multiple_of(k * n, n), n), :]
            if flip & 1:
                ref[flip // 2, j] = piece.astype(BF)
            else:
                ref[j] = piece


def qkv_grad_kernel(nf, pos, x, gq, gkv, far_ref, mid_ref, own_ref, acc, right):
    t = pl.program_id(0)
    rows, cols = gq.shape[1], gq.shape[2]
    tall = x.shape[1]
    right[:rows, :cols] = gq[0]
    right[rows:, :cols] = jnp.zeros((tall - rows, cols), BF)
    right[:, cols : 2 * cols] = gkv[0, 0]
    right[:, 2 * cols :] = gkv[1, 0]
    part = mm_tn(x[0], right[...])

    @pl.when(t == 0)
    def _():
        acc[...] = part

    @pl.when(t > 0)
    def _():
        acc[...] += part

    @pl.when(t == pl.num_programs(0) - 1)
    def _():
        n = own_ref.shape[1]
        for f in range(nf):
            for flip, ref in ((0, own_ref), (2, mid_ref), (1, far_ref), (3, far_ref)):
                k = jnp.bitwise_xor(pos[0], flip)
                start = pl.multiple_of(f * (acc.shape[0] // nf) + k * n, n)
                piece = acc[pl.ds(start, n), :]
                if flip & 1:
                    ref[flip // 2, f] = piece.astype(BF)
                else:
                    ref[f] = piece


def order_kernel(sizes, places, *refs):
    outs = refs[-len(sizes) :]
    for i, block in enumerate(refs[: -len(sizes)]):
        lo = 0
        for n, out in zip(sizes, outs):
            out[0, pl.ds(pl.multiple_of(places[i] * n, n), n), :] = block[0, lo : lo + n, :]
            lo = lo + n


def finish_ff_kernel(pos, *refs):
    gin, gout = refs[4:]
    depth, fc = gin.shape[0], refs[0].shape[1]
    for flip, b in zip((0, 2, 1, 3), refs[:4]):
        k = jnp.bitwise_xor(pos[0], flip)
        at = pl.ds(pl.multiple_of(k * fc, fc), fc)
        gin[:, at] = b[:depth, :].astype(F32)
        gout[at, :] = b[depth:, :].astype(F32).T


def finish_qkv_kernel(pos, *refs):
    for flip, b in zip((0, 2, 1, 3), refs[:4]):
        n = b.shape[0]
        k = jnp.bitwise_xor(pos[0], flip)
        at = pl.ds(pl.multiple_of(k * n, n), n)
        cols = refs[4].shape[1]
        for i, out in enumerate(refs[4:7]):
            out[at, :] = b[:, i * cols : (i + 1) * cols].astype(F32)
        for out in refs[7:]:
            m = n * (b.shape[1] - 3 * cols) // out.shape[1]
            wide = b.shape[1] - 3 * cols
            at = pl.ds(pl.multiple_of(k * m, m), m)
            for i in range(n // m):
                out[at, i * wide : (i + 1) * wide] = b[
                    i * m : (i + 1) * m, 3 * cols :
                ].astype(F32)


def build(mesh):
    nf, nc, nt = mesh.shape["fsdp"], mesh.shape["context"], mesh.shape["tensor"]
    assert nc == 4

    def px(x):
        return lax.ppermute(x, "fsdp", [(0, 1), (1, 0)])

    def pc(x, k):
        return lax.ppermute(x, "context", [(a, a ^ k) for a in range(nc)])

    def pz(x, j):
        return lax.ppermute(x, "tensor", [(a, (a - j) % nt) for a in range(nt)])

    def ps(x, j):
        return lax.ppermute(x, "tensor", [(a, (a + j) % nt) for a in range(nt)])

    def on_device(
        tokens,
        state,
        parent,
        seg_length,
        cell_gate,
        norm1_gain,
        norm1_shift,
        w_query,
        w_key,
        w_value,
        w_attn_out,
        rel_bias,
        norm2_gain,
        norm2_shift,
        w_in,
        w_out,
        cotangent,
    ):
        trees, rows, width = tokens.shape
        local_segs = seg_length.shape[1]
        seg = rows // local_segs
        all_segs = parent.shape[1]
        heads = rel_bias.shape[0]
        depth, cols = w_query.shape
        head_dim = cols // heads
        each = state.shape[1]
        tall = rows + each
        fi, ci, zi = lax.axis_index("fsdp"), lax.axis_index("context"), lax.axis_index("tensor")
        core = ci & 1
        zr, zs = rows // nt, each // nt
        mine = trees * zr
        pos = jnp.stack([ci, zi, fi]).astype(jnp.int32)
        cell, gain_1, shift_1, gain_2, shift_2 = (
            v.reshape(1, width)
            for v in (cell_gate, norm1_gain, norm1_shift, norm2_gain, norm2_shift)
        )
        sds = jax.ShapeDtypeStruct

        def gate(*xs):
            return lax.optimization_barrier(xs)

        stat = sds((8, width), F32)

        def call(body, grid, ins, outs, out_shape, scratch=(), prefetch=1, vmem=24, name="", us=4, keep=False):
            return hbm_call(
                prefetch,
                body,
                out_shape=out_shape,
                grid_spec=pltpu.PrefetchScalarGridSpec(
                    num_scalar_prefetch=prefetch,
                    grid=grid,
                    in_specs=ins,
                    out_specs=outs,
                    scratch_shapes=scratch,
                ),
                compiler_params=pltpu.CompilerParams(vmem_limit_bytes=vmem << 20),
                cost_estimate=cost(us),
                keep=keep,
                name=name,
            )

        def whole(shape):
            return pl.BlockSpec(shape, lambda *_: (0,) * len(shape))

        row_1 = whole((1, width))
        stat_spec = whole((8, width))

        def place(blocks, starts, axis, total):
            shape = list(blocks[0].shape)
            shape[axis] = total
            out = jnp.zeros(shape, blocks[0].dtype)
            for block, start in zip(blocks, starts):
                out = lax.dynamic_update_slice_in_dim(out, block, start, axis)
            return out

        def half_of(x, k, axis, parts):
            n = x.shape[axis] // parts
            return lax.dynamic_slice_in_dim(x, k * n, n, axis)

        def gather_f(x, axis):
            n = x.shape[axis]
            if nf == 2:
                return place([x, px(x)], [fi * n, (1 - fi) * n], axis, 2 * n)
            return lax.all_gather(x, "fsdp", axis=axis, tiled=True)

        def scatter_f(x, axis):
            if nf == 2:
                sent = half_of(x, 1 - fi, axis, 2).astype(BF)
                return half_of(x, fi, axis, 2) + px(sent).astype(F32)
            return lax.psum_scatter(
                x.astype(BF), "fsdp", scatter_dimension=axis, tiled=True
            ).astype(F32)

        def gather_c(x, axis):
            n = x.shape[axis]
            pair = jnp.stack([x, pc(x, 2)])
            over = pc(pair, 1)
            return place(
                [x, pair[1], over[0], over[1]],
                [ci * n, (ci ^ 2) * n, (ci ^ 1) * n, (ci ^ 3) * n],
                axis,
                nc * n,
            )

        def scatter_c(x, axis):
            cut = lambda k: half_of(x, k, axis, nc)
            sent = jnp.stack([cut(ci ^ 1), cut(ci ^ 3)]).astype(BF)
            got = pc(sent, 1).astype(F32)
            far = (cut(ci ^ 2) + got[1]).astype(BF)
            return cut(ci) + got[0] + pc(far, 2).astype(F32)

        if nf == 2:
            half = depth // 2
            near_send = jnp.concatenate(
                [half_of(w, core, 0, 2) for w in (w_query, w_key, w_value)], axis=1
            )
            near_send, w_in, w_out = gate(near_send, w_in, w_out)
            near_w = px(near_send)
            near_w, w_attn_out = gate(near_w, w_attn_out)
            over_w = pc(near_w, 1)
            weights = (w_query, w_key, w_value, near_w, over_w)
            weight_specs = [whole((depth, cols))] * 3 + [whole((half, 3 * cols))] * 2
            w_scratch = [pltpu.VMEM((2 * depth, 3 * cols), BF)]
        else:
            full_w = lax.all_gather(
                jnp.concatenate([w_query, w_key, w_value], axis=1), "fsdp", axis=0, tiled=True
            )
            weights = (full_w,)
            weight_specs = [whole(full_w.shape)]
            w_scratch = []

        fc = w_in.shape[1] // nc
        pack = jnp.stack([half_of(w_in, ci, 1, nc), half_of(w_out, ci, 0, nc).T])
        packs = lax.all_gather(pack, ("tensor", "fsdp"), axis=0, tiled=False)
        packs = packs.reshape(nt, nf, 2, depth, fc)

        o_blocks = [w_attn_out] + [pz(w_attn_out, j) for j in range(1, nt)]
        o_over = []

        normed = call(
            norm_kernel,
            (trees,),
            [
                row_1,
                row_1,
                pl.BlockSpec((1, rows, width), lambda t: (t, 0, 0)),
                pl.BlockSpec((1, each, width), lambda t: (t, 0, 0)),
            ],
            pl.BlockSpec((1, tall, width), lambda t: (t, 0, 0)),
            sds((trees, tall, width), BF),
            prefetch=0,
            name="norm",
            us=5,
        )(gain_1, shift_1, tokens, state)
        tile = tall // 3
        queries, kv = call(
            project_kernel,
            (trees, 3),
            [pl.BlockSpec((1, tile, width), lambda t, i, *_: (t, i, 0))] + weight_specs,
            (
                pl.BlockSpec((1, tile, cols), lambda t, i, *_: (t, i, 0)),
                pl.BlockSpec((1, tile, 2 * cols), lambda t, i, *_: (t, i, 0)),
            ),
            (sds((trees, tall, cols), BF), sds((trees, tall, 2 * cols), BF)),
            w_scratch,
            name="project",
        )(pos, normed, *weights)
        kv_y = pc(kv, 2)
        kv_c = pc(kv, 1)
        grad_low = half_of(cotangent, zi, 1, nt).reshape(mine, width)
        kv_y, grad_low, *o_blocks = gate(kv_y, grad_low, *o_blocks)
        kv_cy = pc(kv_y, 1)
        if nf == 2:
            o_over = [px(jnp.stack(o_blocks))]
        else:
            full = lax.all_gather(jnp.stack(o_blocks), "fsdp", axis=2, tiled=True)
            o_blocks = [full[j] for j in range(nt)]
        grad_y = pc(grad_low, 2)
        grad_c = pc(grad_low, 1)

        forward, backward = attention_calls(
            trees, heads, local_segs, all_segs, seg, each, head_dim, nt
        )
        tables = (parent, seg_length, pos, rel_bias)
        sources = (queries, kv, kv_c, kv_y, kv_cy, kv, kv_c, kv_y, kv_cy)
        *att_send, log_total = forward(*tables, *sources)
        quarter = jnp.concatenate(
            [half_of(w, ci, 0, nc) for w in (w_query, w_key, w_value)], axis=1
        )
        att_send[0], quarter = gate(att_send[0], quarter)
        all_q = lax.all_gather(quarter, ("tensor", "fsdp"), axis=0, tiled=False)

        att = [att_send[0]] + [pz(att_send[j], j) for j in range(1, nt)]
        att[1], grad_y, *o_over = gate(att[1], grad_y, *o_over)
        grad_rows = [grad_low, grad_y, grad_c, pc(grad_y, 1)]
        chunk = whole((trees, zr, width))
        chunk_z = pl.BlockSpec((trees, zr, width), lambda i, pos: (0, pos[1], 0))
        small = whole((trees, zr, cols))
        o_all = tuple(o_blocks) + tuple(o_over)
        o_specs = [whole(o.shape) for o in o_all]
        o_scratch = [pltpu.VMEM((nt * cols, width), BF)]
        hidden, normed_two, stat_a = call(
            functools.partial(mix_kernel, nt),
            (1,),
            [small] * nt + o_specs + [chunk_z, row_1, row_1, row_1],
            (chunk, chunk, stat_spec),
            (sds((trees, zr, width), F32), sds((trees, zr, width), BF), stat),
            o_scratch,
            name="mix",
            keep=True,
        )(pos, *att, *o_all, tokens, cell, gain_2, shift_2)

        rows_two = normed_two.reshape(mine, width)
        rows_y = pc(rows_two, 2)
        rows_c = pc(rows_two, 1)
        block = whole((mine, width))
        units = nt * fc
        half_spec = whole((2, mine, width))
        half_sds, full_sds = sds((2, mine, width), BF), sds((2, mine, units), BF)
        unit_spec = pl.BlockSpec((2, mine, fc), lambda z, *_: (0, 0, z))
        pack_spec = pl.BlockSpec((1,) + packs.shape[1:], lambda z, *_: (z, 0, 0, 0, 0))
        feed = call(
            ff_kernel,
            (nt,),
            [block] * 4 + [pack_spec],
            (block, block, unit_spec, unit_spec),
            (sds((mine, width), BF), sds((mine, width), BF), full_sds, full_sds),
            [pltpu.VMEM((2 * mine, width), F32)],
            prefetch=0,
            vmem=32,
            name="feed",
            keep=True,
            us=9,
        )
        gn_own, gn_c, act_a, gup_a = feed(rows_two, rows_c, grad_rows[0], grad_rows[2], packs)
        rows_y, gn_own, gn_c = gate(rows_y, gn_own, gn_c)
        rows_cy = pc(rows_y, 1)
        gn_got = [pc(gn_c, 1)]
        gn_y, gn_cy, act_b, gup_b = feed(rows_y, rows_cy, grad_rows[1], grad_rows[3], packs)
        ff_rows = [rows_two, rows_c, rows_y, rows_cy]
        cot_rows = [grad_rows[0], grad_rows[2], grad_rows[1], grad_rows[3]]
        gn_got.append(pc(gn_cy, 1))
        gn_mid = (gn_y.astype(F32) + gn_got[1].astype(F32)).astype(BF)
        gn_mid, gn_got[0], act_b, gup_b = gate(gn_mid, gn_got[0], act_b, gup_b)
        gn_end = pc(gn_mid, 2)
        ff_sent, ff_near, ff_far = call(
            ff_grad_kernel,
            (nt,),
            [block] * 8 + [unit_spec] * 4 + [pack_spec],
            (
                pl.BlockSpec((nf, 1, 2, depth, fc), lambda z, *_: (0, z, 0, 0, 0)),
                half_spec,
                half_spec,
            ),
            (sds((nf, nt, 2, depth, fc), BF), half_sds, half_sds),
            [pltpu.VMEM((4 * mine, width), BF)] * 2
            + [pltpu.VMEM((4 * mine, width), F32), pltpu.VMEM((width, fc), BF)]
            + [pltpu.VMEM((4 * mine, fc), BF)] * 2,
            prefetch=0,
            vmem=56,
            name="feed_grads",
            keep=True,
            us=16,
        )(*ff_rows, *cot_rows, act_a, gup_a, act_b, gup_b, packs)
        gn_end, ff_sent, ff_near, ff_far, all_q = gate(gn_end, ff_sent, ff_near, ff_far, all_q)
        ff_got = pc(ff_far, 1)

        grad_hidden, grad_branch, *rest = call(
            functools.partial(branch_back_kernel, nt),
            (1,),
            o_specs + [chunk] * 4 + [chunk_z, row_1, row_1],
            (chunk, chunk) + (small,) * nt + (stat_spec,),
            (sds((trees, zr, width), F32), sds((trees, zr, width), BF))
            + (sds((trees, zr, cols), BF),) * nt
            + (stat,),
            o_scratch,
            name="branch_back",
            keep=True,
        )(
            pos,
            *o_all,
            gn_own.reshape(trees, zr, width),
            gn_got[0].reshape(trees, zr, width),
            gn_end.reshape(trees, zr, width),
            hidden,
            cotangent,
            cell,
            gain_2,
        )
        stat_b = rest.pop()
        ff_got, grad_branch, *rest = gate(ff_got, grad_branch, *rest)
        all_q, rest[0] = gate(all_q, rest[0])
        all_y = pc(all_q, 2)
        grad_heads = [rest[0]] + [ps(rest[j], j) for j in range(1, nt)]
        ff_mid = (ff_near[1].astype(F32) + ff_got[1].astype(F32)).astype(BF)
        ff_end = pc(ff_mid, 2)
        o_rows = cols // nc
        att_specs = (whole((2, nt, o_rows, width)),) + (whole((nt, o_rows, width)),) * 2
        attn_far, attn_mid, attn_near = call(
            functools.partial(attn_grad_kernel, nt),
            (1,),
            [whole((trees, zr, cols))] * nt + [whole((trees, zr, width))],
            att_specs,
            (
                sds((2, nt, o_rows, width), BF),
                sds((nt, o_rows, width), F32),
                sds((nt, o_rows, width), F32),
            ),
            [pltpu.VMEM((cols, width), F32)],
            name="attn_grads",
            us=4,
        )(pos, *att, grad_branch)

        mlp_out = ff_near[0].astype(F32) + ff_got[0].astype(F32) + ff_end.astype(F32)
        result = (hidden.reshape(mine, width) + mlp_out).astype(BF)
        result, attn_near, attn_mid, attn_far, *grad_heads = gate(
            result, attn_near, attn_mid, attn_far, *grad_heads
        )
        result = result.reshape(trees, zr, width)

        def spread_near(x):
            if nt == 4:
                return [
                    lax.ppermute(x, "tensor", [(0, 1), (1, 2), (2, 3)]),
                    lax.ppermute(x, "tensor", [(1, 0), (2, 1), (3, 2)]),
                ]
            return [pz(x, 1), pz(x, nt - 1)]

        def ordered(blocks, places, sizes):
            n = blocks[0].shape[1]
            return call(
                functools.partial(order_kernel, sizes),
                (trees,),
                [pl.BlockSpec((1, n, width), lambda t, *_: (t, 0, 0))] * len(blocks),
                tuple(
                    pl.BlockSpec((1, nt * m, width), lambda t, *_: (t, 0, 0)) for m in sizes
                ),
                tuple(sds((trees, nt * m, width), BF) for m in sizes),
                name="order",
                us=1,
            )(jnp.stack(places).astype(jnp.int32), *blocks)

        def swap(x, pairs):
            return lax.ppermute(x, "tensor", pairs + [(b, a) for a, b in pairs])

        first_at = [jnp.maximum(zi - 1, 0), jnp.minimum(zi + 1, nt - 1), zi]

        out_near = spread_near(result)
        attn_got = pc(attn_far, 1)

        *dq_send, grad_q, kv_near, kv_far, bias_rows = backward(
            *tables, *sources, *grad_heads, log_total
        )
        ff_half = lax.psum_scatter(ff_sent, "fsdp", scatter_dimension=0, tiled=True)[0]
        ff_half = ff_half.reshape(nt, 2 * depth, fc)
        kv_far, kv_near, attn_got, all_y, *out_near = gate(
            kv_far, kv_near, attn_got, all_y, *out_near
        )
        kv_got = pc(kv_far, 1)
        kv_mid = (kv_near[1].astype(F32) + kv_got[1].astype(F32)).astype(BF)
        own = lax.psum_scatter(ff_half, "tensor", scatter_dimension=0, tiled=True)[0]
        kv_mid, result, attn_got, attn_near, attn_mid, all_q, all_y = gate(
            kv_mid, result, attn_got, attn_near, attn_mid, all_q, all_y
        )
        all_w = [all_q, all_y, pc(all_q, 1), pc(all_y, 1)]
        kv_end = pc(kv_mid, 2)
        if nt == 4:
            out_far = [swap(result, [(0, 2), (1, 3)])]
            out_far.append(
                lax.ppermute(out_far[0], "tensor", [(2, 3), (1, 0), (3, 2), (0, 1)])
            )
        else:
            out_far = [pz(result, j) for j in range(2, nt - 1)]
        attn_two = jnp.stack([attn_near, attn_mid]) + attn_got.astype(F32)
        attn_two = scatter_f(attn_two, 3)
        attn_end = pc(attn_two[1].astype(BF), 2)
        kv_end, attn_two, attn_end, all_w, *out_far = gate(
            kv_end, attn_two, attn_end, all_w, *out_far
        )
        attn_sum = (attn_two[0] + attn_end.astype(F32)).astype(BF)
        attn_sum = lax.dynamic_slice_in_dim(
            jnp.concatenate([attn_sum, attn_sum], axis=0), nt - zi, nt, 0
        )
        attn_own = lax.psum_scatter(attn_sum, "tensor", scatter_dimension=0, tiled=True)[0]
        five = pl.BlockSpec((1, 1, 1, tall, cols), lambda t, k, *_: (0, k, t, 0, 0))
        four = pl.BlockSpec((1, 1, tall, cols), lambda t, k, *_: (k, t, 0, 0))
        send = pl.BlockSpec((3, 1, zr + zs, cols), lambda t, k, *_: (0, t, 0, 0))
        grad_kv, *kv_send = call(
            functools.partial(combine_kernel, rows),
            (trees, 2),
            [five, five, four]
            + [pl.BlockSpec((1, zr, cols), lambda t, k, *_: (t, 0, 0))] * nt,
            (four,) + (send,) * nt,
            (sds((2, trees, tall, cols), BF),) + (sds((3, trees, zr + zs, cols), BF),) * nt,
            name="combine",
            keep=True,
        )(pos, kv_near, kv_got, kv_end, *dq_send)
        dqkv = [kv_send[0]] + [pz(kv_send[j], j) for j in range(1, nt)]

        dq_rows = depth // nc
        cut_specs = (whole((2, nf, dq_rows, 3 * cols)),) + (whole((nf, dq_rows, 3 * cols)),) * 2
        qkv_far, qkv_mid, qkv_own = call(
            functools.partial(qkv_grad_kernel, nf),
            (trees,),
            [
                pl.BlockSpec((1, tall, width), lambda t, *_: (t, 0, 0)),
                pl.BlockSpec((1, rows, cols), lambda t, *_: (t, 0, 0)),
                pl.BlockSpec((2, 1, tall, cols), lambda t, *_: (0, t, 0, 0)),
            ],
            cut_specs,
            (
                sds((2, nf, dq_rows, 3 * cols), BF),
                sds((nf, dq_rows, 3 * cols), F32),
                sds((nf, dq_rows, 3 * cols), F32),
            ),
            [pltpu.VMEM((nf * depth, 3 * cols), F32), pltpu.VMEM((tall, 3 * cols), BF)],
            name="qkv_grads",
            keep=True,
            us=8,
        )(pos, normed, grad_q, grad_kv)
        if nt == 4:
            places = first_at + [zi ^ 2, 3 - zi]
            blocks = [out_near[0], out_near[1], result, *out_far]
        else:
            blocks = [result, *out_near, *out_far]
            places = [zi, (zi + 1) % nt, (zi - 1) % nt] + [(zi + j) % nt for j in range(2, nt - 1)]
        (output,) = ordered(blocks, places, (zr,))
        own_y = pc(own, 2)
        qkv_mid, qkv_own, qkv_far, own_y, output, attn_own, *dqkv = gate(
            qkv_mid, qkv_own, qkv_far, own_y, output, attn_own, *dqkv
        )
        qkv_got = pc(qkv_far, 1)
        own_blocks = (own, own_y, pc(own, 1), pc(own_y, 1))

        chunk_sz = pl.BlockSpec((trees, zs, width), lambda i, pos: (0, pos[1], 0))
        grads_own, stat_c = call(
            functools.partial(input_back_kernel, nt),
            (1,),
            [whole((3, trees, zr + zs, cols))] * nt
            + [whole(all_q.shape)] * 4
            + [chunk_z, chunk_sz, chunk, row_1],
            (whole((trees, zr + zs, width)), stat_spec),
            (sds((trees, zr + zs, width), BF), stat),
            [
                pltpu.VMEM((nt, nf * depth, 3 * cols), BF),
                pltpu.VMEM((trees * (zr + zs), width), F32),
            ],
            vmem=44,
            name="input_back",
            keep=True,
        )(pos, *dqkv, *all_w, tokens, state, grad_hidden, gain_1)
        grads_own, qkv_got, *own_blocks = gate(grads_own, qkv_got, *own_blocks)
        qkv_got = qkv_got.astype(F32)

        bias_own = jnp.sum(bias_rows, axis=2)
        bias_all = lax.dynamic_update_slice(
            jnp.zeros((heads * nt, BUCKETS), F32), bias_own, (zi * heads, 0)
        )
        squares = jnp.stack([jnp.sum(stat_a[0]), jnp.sum(stat_a[1]), jnp.sum(mlp_out * mlp_out)])
        spare = jnp.zeros((2 * width - bias_all.size - 3,), F32)
        early = jnp.concatenate(
            [
                stat_b[:2],
                jnp.concatenate([bias_all.reshape(-1), squares, spare]).reshape(2, width),
            ],
            axis=0,
        )
        early, grads_own = gate(early, grads_own)
        sums = jnp.concatenate([stat_c[:2], early], axis=0)

        in_near = spread_near(grads_own)
        *in_near, sums, attn_own, qkv_got = gate(*in_near, sums, attn_own, qkv_got)
        qkv_end = pc((qkv_mid + qkv_got[1]).astype(BF), 2)
        if nt == 4:
            c = swap(grads_own, [(0, 2), (1, 3)])
            d = lax.ppermute(c, "tensor", [(2, 3), (1, 0), (3, 2), (0, 1)])
            places = first_at + [zi ^ 2, 3 - zi]
            blocks = [in_near[0], in_near[1], grads_own, c, d]
        else:
            in_far = [pz(grads_own, j) for j in range(2, nt - 1)]
            blocks = [grads_own, *in_near, *in_far]
        tokens_grad, state_grad = ordered(blocks, places, (zr, zs))
        sums = sums + px(sums) if nf == 2 else lax.psum(sums, "fsdp")
        sums = sums + pc(sums, 1)
        sums = sums + pc(sums, 2)
        if nt & (nt - 1):
            sums = lax.psum(sums, "tensor")
        else:
            k = 1
            while k < nt:
                sums = sums + lax.ppermute(sums, "tensor", [(a, a ^ k) for a in range(nt)])
                k = 2 * k

        qkv_sum = scatter_f(qkv_own + qkv_got[0] + qkv_end.astype(F32), 0)[0].astype(BF)
        if depth % o_rows == 0 and depth * o_rows % dq_rows == 0 and nf == 2:
            folded = jnp.concatenate([attn_own[:, :fc], attn_own[:, fc:]], axis=0)
            qkv_sum = jnp.concatenate([qkv_sum, folded], axis=1)
        else:
            attn_full = gather_c(attn_own, 0).astype(F32)
            folded = None
        qkv_y = pc(qkv_sum, 2)
        qkv_blocks = (qkv_sum, qkv_y, pc(qkv_sum, 1), pc(qkv_y, 1))
        last_shapes = ((depth, cols),) * 3
        if folded is not None:
            last_shapes += ((nc * o_rows, depth),)
        *grad_qkv, grad_attn_out = call(
            finish_qkv_kernel,
            (1,),
            [whole(qkv_sum.shape)] * 4,
            tuple(whole(v) for v in last_shapes),
            tuple(sds(v, F32) for v in last_shapes),
            name="finish_qkv",
            us=0,
        )(pos, *qkv_blocks) + (() if folded is not None else (attn_full,))
        grad_in, grad_out = call(
            finish_ff_kernel,
            (1,),
            [whole(own.shape)] * 4,
            (whole((depth, nc * fc)), whole((nc * fc, depth))),
            (sds((depth, nc * fc), F32), sds((nc * fc, depth), F32)),
            name="finish_ff",
            us=0,
        )(pos, *own_blocks)
        last = sums[4:].reshape(-1)
        bias_sum = last[: bias_all.size].reshape(bias_all.shape)
        grad_bias = lax.dynamic_slice_in_dim(bias_sum, zi * heads, heads, 0)
        cell_count = trees * rows * width * nf * nc
        norms = jnp.sqrt(last[bias_all.size : bias_all.size + 3] / cell_count)
        return (
            output,
            tokens_grad,
            state_grad,
            *grad_qkv,
            grad_attn_out,
            grad_bias,
            sums[0],
            sums[1],
            sums[2],
            sums[3],
            grad_in,
            grad_out,
            norms,
        )

    return on_device


def solution(mesh):
    return jax.shard_map(
        build(mesh),
        mesh=mesh,
        in_specs=(
            P("fsdp", "context", None),
            P("fsdp", "context", None),
            P("fsdp", None),
            P("fsdp", "context"),
            P(),
            P(),
            P(),
            P("fsdp", "tensor"),
            P("fsdp", "tensor"),
            P("fsdp", "tensor"),
            P("tensor", "fsdp"),
            P("tensor", None),
            P(),
            P(),
            P("fsdp", "tensor"),
            P("tensor", "fsdp"),
            P("fsdp", "context", None),
        ),
        out_specs=(
            P("fsdp", "context", None),
            P("fsdp", "context", None),
            P("fsdp", "context", None),
            P("fsdp", "tensor"),
            P("fsdp", "tensor"),
            P("fsdp", "tensor"),
            P("tensor", "fsdp"),
            P("tensor", None),
            P(),
            P(),
            P(),
            P(),
            P("fsdp", "tensor"),
            P("tensor", "fsdp"),
            P(),
        ),
        check_vma=False,
    )
```

```python
import functools
import math

import jax
import jax.numpy as jnp
from jax import lax
from jax.experimental import pallas as pl
from jax.experimental.pallas import tpu as pltpu
from jax.sharding import PartitionSpec as P

WINDOW = 512
BUCKETS = 32
REACH = 128
EPSILON = 1e-05
MASKED = -1e30
GELU_C = 0.7978845608028654
GELU_A = 0.044715
BF = jnp.bfloat16
F32 = jnp.float32


def cost(us):
    return pl.CostEstimate(
        flops=int(us * 1e9), transcendentals=0, bytes_accessed=int(us * 3e6)
    )


def bucket_edges(bucket_total, far_reach, window):
    exact_count = bucket_total // 2
    boundaries = []
    current = 0
    for distance in range(window):
        if distance < exact_count:
            bucket = distance
        else:
            bucket = exact_count + int(
                math.log(distance / exact_count)
                / math.log(far_reach / exact_count)
                * (bucket_total - exact_count)
            )
            bucket = min(bucket, bucket_total - 1)
        while current < bucket:
            current = current + 1
            boundaries.append(distance)
    return boundaries


EDGES = bucket_edges(BUCKETS, REACH, WINDOW)


def mm(left, right):
    return lax.dot_general(left, right, (((1,), (0,)), ((), ())), preferred_element_type=F32)


def mm_nt(left, right):
    return lax.dot_general(left, right, (((1,), (1,)), ((), ())), preferred_element_type=F32)


def mm_tn(left, right):
    return lax.dot_general(left, right, (((0,), (0,)), ((), ())), preferred_element_type=F32)


def bias_tables(rb_ref, h, levels, seg, bm_ref):
    key = lax.broadcasted_iota(jnp.int32, (seg, seg), 0)
    query = lax.broadcasted_iota(jnp.int32, (seg, seg), 1)
    for lev in range(levels):
        dist = lev * seg + query - key
        low, high = lev * seg - (seg - 1), lev * seg + seg - 1
        if low >= EDGES[-1]:
            val = jnp.full((seg, seg), rb_ref[h, BUCKETS - 1], F32)
        else:
            val = jnp.full((seg, seg), rb_ref[h, 0], F32)
            for i, edge in enumerate(EDGES):
                if edge <= high:
                    val = jnp.where(dist >= edge, rb_ref[h, i + 1], val)
        if low < 0:
            val = jnp.where(dist >= 0, val, MASKED)
        if high >= WINDOW:
            val = jnp.where(dist < WINDOW, val, MASKED)
        bm_ref[lev * seg : (lev + 1) * seg, :] = val


def chain(par_ref, t, first, levels, all_segs, local_segs, ctx):
    out = []
    anc = first
    for lev in range(levels):
        if lev > 0:
            up = par_ref[t, jnp.maximum(anc, 0)]
            anc = jnp.where(anc >= 0, up, -1)
        safe = jnp.maximum(anc, 0)
        owner = lax.div(safe, local_segs)
        out.append((anc >= 0, jnp.bitwise_xor(owner, ctx), safe - owner * local_segs))
    return out


def window_score(raw, lev, bm_ref, line, length, seg):
    part = raw + bm_ref[lev * seg : (lev + 1) * seg, :]
    if lev == 0:
        key = lax.broadcasted_iota(jnp.int32, (seg, 1), 0)
        return part + jnp.where(key < length, 0.0, MASKED)
    return part + jnp.where(line[lev][0], 0.0, MASKED)


def fold(value, op):
    out = value[0:8]
    for i in range(8, value.shape[0], 8):
        out = op(out, value[i : i + 8])
    return out


def attend_kernel(dims, par_ref, len_ref, pos_ref, rb_ref, q_ref, *refs):
    levels, seg, local_segs, all_segs, factor, nt = dims
    parts_k, parts_v = refs[0:4], refs[4:8]
    att_refs, lse_ref = refs[8 : 8 + nt], refs[8 + nt]
    kall, vall_t, kws, vw_ts, bm, whole, q_t, raws_a, probs_a = refs[9 + nt :]
    t, h = pl.program_id(0), pl.program_id(1)
    ctx, zi = pos_ref[0], pos_ref[1]
    rows, win = local_segs * seg, levels * seg
    each = (kws.shape[1] - win) // 4
    blocks = kws.shape[1] // seg
    bias_tables(rb_ref, h, levels, seg, bm)
    for b in range(4):
        at = slice(win + b * each, win + (b + 1) * each)
        kall[b] = parts_k[b][0, :rows, :]
        turned = parts_v[b][0].T
        vall_t[b] = turned[:, :rows]
        for i in range(2):
            kws[i, at, :] = parts_k[b][0, rows:, :]
            vw_ts[i, :, at] = turned[:, rows:]
    q_t[...] = q_ref[0, :rows, :].T

    def one(s, carry):
        kw, vw_t, raws, probs = (r.at[s % 2] for r in (kws, vw_ts, raws_a, probs_a))
        line = chain(par_ref, t, ctx * local_segs + s, levels, all_segs, local_segs, ctx)
        for lev, (_, part, block) in enumerate(line):
            start = pl.ds(pl.multiple_of(block * seg, seg), seg)
            kw[lev * seg : (lev + 1) * seg, :] = kall[part, start, :]
            vw_t[:, lev * seg : (lev + 1) * seg] = vall_t[part, :, start]
        at = slice(s * seg, (s + 1) * seg)
        turned = q_t[:, at]
        top = None
        for c in range(blocks):
            raw = mm(kw[c * seg : (c + 1) * seg, :], turned) * factor
            if c < levels:
                raw = window_score(raw, c, bm, line, len_ref[t, s], seg)
            raws[c * seg : (c + 1) * seg, :] = raw
            high = fold(raw, jnp.maximum)
            top = high if top is None else jnp.maximum(top, high)
        top = jnp.max(top, axis=0, keepdims=True)
        total = None
        for c in range(blocks):
            prob = jnp.exp(raws[c * seg : (c + 1) * seg, :] - top)
            probs[c * seg : (c + 1) * seg, :] = prob.astype(BF)
            part = fold(prob, jnp.add)
            total = part if total is None else total + part
        total = jnp.sum(total, axis=0, keepdims=True)
        lse_ref[0, 0, 0:1, at] = top + jnp.log(total)
        att = mm(vw_t[...], probs[...]) / total
        whole[at, :] = att.T.astype(BF)
        return carry

    for s in range(local_segs):
        one(s, 0)
    n = rows // nt
    for j in range(nt):
        k = lax.rem(zi - j + nt, nt)
        att_refs[j][0] = whole[pl.ds(pl.multiple_of(k * n, n), n), :]


def attend_back_kernel(dims, par_ref, len_ref, pos_ref, rb_ref, q_ref, *refs):
    levels, seg, local_segs, all_segs, factor, nt = dims
    parts_k, parts_v = refs[0:4], refs[4:8]
    do_refs, lse_ref = refs[8 : 8 + nt], refs[8 + nt]
    dq_refs = refs[9 + nt : 9 + 2 * nt]
    dq_ref, near_ref, far_ref, db_ref = refs[9 + 2 * nt : 13 + 2 * nt]
    kall, vall, kall_t, kw, vw, kw_t, bm, dk, dv, near, far, dos, do_t, q_t, raws, dps, dss, pbs = refs[
        13 + 2 * nt :
    ]
    h, t = pl.program_id(0), pl.program_id(1)
    ctx, zi = pos_ref[0], pos_ref[1]
    rows, win = local_segs * seg, levels * seg
    each = (kw.shape[0] - win) // 4
    blocks = kw.shape[0] // seg
    n = rows // nt
    bias_tables(rb_ref, h, levels, seg, bm)
    for b in range(4):
        at = slice(win + b * each, win + (b + 1) * each)
        kall[b] = parts_k[b][0, :rows, :]
        vall[b] = parts_v[b][0, :rows, :]
        turned = parts_k[b][0].T
        kall_t[b] = turned[:, :rows]
        kw[at, :] = parts_k[b][0, rows:, :]
        vw[at, :] = parts_v[b][0, rows:, :]
        kw_t[:, at] = turned[:, rows:]
    dk[...] = jnp.zeros(dk.shape, F32)
    dv[...] = jnp.zeros(dv.shape, F32)
    for j in range(nt):
        k = lax.rem(zi - j + nt, nt)
        dos[pl.ds(pl.multiple_of(k * n, n), n), :] = do_refs[j][0]
    q_t[...] = q_ref[0, :rows, :].T
    do_t[...] = dos[...].T

    @pl.when(t == 0)
    def _():
        near[...] = jnp.zeros(near.shape, F32)
        far[...] = jnp.zeros(far.shape, F32)

    def one(s, carry):
        line = chain(par_ref, t, ctx * local_segs + s, levels, all_segs, local_segs, ctx)
        for lev, (_, part, block) in enumerate(line):
            start = pl.ds(pl.multiple_of(block * seg, seg), seg)
            at = slice(lev * seg, (lev + 1) * seg)
            kw[at, :] = kall[part, start, :]
            vw[at, :] = vall[part, start, :]
            kw_t[:, at] = kall_t[part, :, start]
        at = pl.ds(pl.multiple_of(s * seg, seg), seg)
        turned, do_turned = q_t[:, at], do_t[:, at]
        lse = lse_ref[0, 0, 0:1, at]
        delta = None
        for c in range(blocks):
            cut = slice(c * seg, (c + 1) * seg)
            raw = mm(kw[cut, :], turned) * factor
            if c < levels:
                raw = window_score(raw, c, bm, line, len_ref[t, s], seg)
            prob = jnp.exp(raw - lse)
            dprob = mm(vw[cut, :], do_turned)
            raws[cut, :] = prob
            dps[cut, :] = dprob
            pbs[cut, :] = prob.astype(BF)
            part = fold(prob * dprob, jnp.add)
            delta = part if delta is None else delta + part
        delta = jnp.sum(delta, axis=0, keepdims=True)
        for c in range(blocks):
            cut = slice(c * seg, (c + 1) * seg)
            dscore = (raws[cut, :] * (dps[cut, :] - delta)).astype(BF)
            dss[cut, :] = dscore
            if c < 2:
                near[cut, :] += dscore.astype(F32)
            elif c < levels:
                far[...] += dscore.astype(F32)
        dq = mm(kw_t[...], dss[...]) * factor
        dq_ref[0, at, :] = dq.T.astype(BF)
        q, do = q_ref[0, at, :], dos[at, :]
        for c in range(blocks):
            cut = slice(c * seg, (c + 1) * seg)
            gk = mm(dss[cut, :], q) * factor
            gv = mm(pbs[cut, :], do)
            if c < levels:
                _, part, block = line[c]
                to = pl.ds(pl.multiple_of(block * seg, seg), seg)
                dk[part, to, :] += gk
                dv[part, to, :] += gv
            else:
                for i in range(0, seg, each):
                    b = ((c - levels) * seg + i) // each
                    dk[b, rows:, :] += gk[i : i + each]
                    dv[b, rows:, :] += gv[i : i + each]
        return carry

    lax.fori_loop(0, local_segs, one, 0)
    for ref, pair in ((near_ref, (0, 2)), (far_ref, (1, 3))):
        for place, b in enumerate(pair):
            ref[place, 0, 0] = dk[b].astype(BF)
            ref[place, 1, 0] = dv[b].astype(BF)
    for j in range(nt):
        k = lax.rem(zi - j + nt, nt)
        dq_refs[j][0] = dq_ref[0, pl.ds(pl.multiple_of(k * n, n), n), :]

    @pl.when(t == pl.num_programs(1) - 1)
    def _():
        key = lax.broadcasted_iota(jnp.int32, (seg, seg), 0)
        query = lax.broadcasted_iota(jnp.int32, (seg, seg), 1)
        edges = [-(10**6)] + list(EDGES) + [10**6]
        for b in range(BUCKETS):
            total = far[...] if b == BUCKETS - 1 else jnp.zeros((seg, seg), F32)
            for lev in range(2):
                dist = lev * seg + query - key
                inside = (dist >= edges[b]) & (dist < edges[b + 1])
                total = total + jnp.where(inside, near[lev * seg : (lev + 1) * seg, :], 0.0)
            db_ref[0, b : b + 1, :] = jnp.sum(total, axis=0, keepdims=True)


def hbm_call(prefetch, body, out_shape, keep=False, **kw):
    if not keep:
        return pl.pallas_call(body, out_shape=out_shape, **kw)
    several = isinstance(out_shape, tuple)
    outs = tuple(
        pltpu.HBM(o.shape, o.dtype) for o in (out_shape if several else (out_shape,))
    )
    kernel = pl.pallas_call(body, out_shape=outs if several else outs[0], **kw)

    def run(*args):
        rest = [pltpu.with_memory_space_constraint(a, pltpu.HBM) for a in args[prefetch:]]
        return kernel(*args[:prefetch], *rest)

    return run


def attention_calls(trees, heads, local_segs, all_segs, seg, each, head_dim, nt):
    levels = WINDOW // seg + 1
    rows = local_segs * seg
    tall = rows + each
    win = levels * seg
    wide = win + 4 * each
    factor = head_dim ** (-0.5)
    dims = (levels, seg, local_segs, all_segs, factor, nt)
    assert EDGES[-1] <= 2 * seg - (seg - 1)
    assert seg == head_dim == 128 and wide % seg == 0 and seg % each == 0
    vm = lambda dt, *shape: pltpu.VMEM(shape, dt)
    forward_scratch = [
        vm(BF, 4, rows, head_dim),
        vm(BF, 4, head_dim, rows),
        vm(BF, 2, wide, head_dim),
        vm(BF, 2, head_dim, wide),
        vm(F32, win, seg),
        vm(BF, rows, head_dim),
        vm(BF, head_dim, rows),
        vm(F32, 2, wide, seg),
        vm(BF, 2, wide, seg),
    ]
    backward_scratch = [
        vm(BF, 4, rows, head_dim),
        vm(BF, 4, rows, head_dim),
        vm(BF, 4, head_dim, rows),
        vm(BF, wide, head_dim),
        vm(BF, wide, head_dim),
        vm(BF, head_dim, wide),
        vm(F32, win, seg),
        vm(F32, 4, tall, head_dim),
        vm(F32, 4, tall, head_dim),
        vm(F32, 2 * seg, seg),
        vm(F32, seg, seg),
        vm(BF, rows, head_dim),
        vm(BF, head_dim, rows),
        vm(BF, head_dim, rows),
        vm(F32, wide, seg),
        vm(F32, wide, seg),
        vm(BF, wide, seg),
        vm(BF, wide, seg),
    ]
    lse_shape = jax.ShapeDtypeStruct((trees, heads, 8, rows), F32)

    def specs(order):
        def at(col):
            return pl.BlockSpec(
                (1, tall, head_dim), lambda a, b, *_: (order(a, b)[0], 0, col(order(a, b)[1]))
            )

        k, v = at(lambda h: h), at(lambda h: heads + h)
        return [k, k, k, k, k, v, v, v, v]

    th = lambda a, b: (a, b)
    ht = lambda a, b: (b, a)
    chunk_shape = jax.ShapeDtypeStruct((trees, rows // nt, heads * head_dim), BF)

    def chunk_spec(order):
        return pl.BlockSpec(
            (1, rows // nt, head_dim), lambda a, b, *_: (order(a, b)[0], 0, order(a, b)[1])
        )

    forward = hbm_call(
        4,
        functools.partial(attend_kernel, dims),
        out_shape=(chunk_shape,) * nt + (lse_shape,),
        grid_spec=pltpu.PrefetchScalarGridSpec(
            num_scalar_prefetch=4,
            grid=(trees, heads),
            in_specs=specs(th),
            out_specs=(chunk_spec(th),) * nt
            + (pl.BlockSpec((1, 1, 8, rows), lambda t, h, *_: (t, h, 0, 0)),),
            scratch_shapes=forward_scratch,
        ),
        compiler_params=pltpu.CompilerParams(vmem_limit_bytes=24 << 20),
        cost_estimate=cost(16),
        keep=True,
        name="attend",
    )
    pair = jax.ShapeDtypeStruct((2, 2, trees, tall, heads * head_dim), BF)
    pair_spec = pl.BlockSpec((2, 2, 1, tall, head_dim), lambda h, t, *_: (0, 0, t, 0, h))
    backward = hbm_call(
        4,
        functools.partial(attend_back_kernel, dims),
        out_shape=(chunk_shape,) * nt
        + (
            jax.ShapeDtypeStruct((trees, rows, heads * head_dim), BF),
            pair,
            pair,
            jax.ShapeDtypeStruct((heads, BUCKETS, 128), F32),
        ),
        grid_spec=pltpu.PrefetchScalarGridSpec(
            num_scalar_prefetch=4,
            grid=(heads, trees),
            in_specs=specs(ht)
            + [chunk_spec(ht)] * nt
            + [pl.BlockSpec((1, 1, 8, rows), lambda h, t, *_: (t, h, 0, 0))],
            out_specs=(chunk_spec(ht),) * nt
            + (
                pl.BlockSpec((1, rows, head_dim), lambda h, t, *_: (t, 0, h)),
                pair_spec,
                pair_spec,
                pl.BlockSpec((1, BUCKETS, 128), lambda h, t, *_: (h, 0, 0)),
            ),
            scratch_shapes=backward_scratch,
        ),
        compiler_params=pltpu.CompilerParams(vmem_limit_bytes=32 << 20),
        cost_estimate=cost(24),
        keep=True,
        name="attend_back",
    )
    return forward, backward


def norm_stats(values):
    mean = jnp.mean(values, axis=-1, keepdims=True)
    centered = values - mean
    scale = lax.rsqrt(jnp.mean(centered * centered, axis=-1, keepdims=True) + EPSILON)
    return centered * scale, scale


def norm_back(grad, xhat, scale, gain):
    scaled = grad * gain
    first = jnp.mean(scaled, axis=-1, keepdims=True)
    second = jnp.mean(scaled * xhat, axis=-1, keepdims=True)
    return scale * (scaled - first - xhat * second)


def gelu_parts(u):
    square = u * u
    th = jnp.tanh(u * (GELU_C + GELU_C * GELU_A * square))
    half = 0.5 * (1.0 + th)
    slope = half + (0.5 * u) * (1.0 - th * th) * (GELU_C + 3.0 * GELU_C * GELU_A * square)
    return u * half, slope


def norm_kernel(gain, shift, tok, st, out):
    each = st.shape[1]
    rows = tok.shape[1]
    for lo in range(0, rows + each, each):
        x = (tok[0, lo : lo + each, :] if lo < rows else st[0]).astype(F32)
        xhat, _ = norm_stats(x)
        out[0, lo : lo + each, :] = (xhat * gain[...] + shift[...]).astype(BF)


def project_kernel(pos, x, *refs):
    if len(refs) == 3:
        w = refs[0]
        q_ref, kv_ref = refs[1:]
    else:
        wq, wk, wv, near, over, q_ref, kv_ref, w = refs

        @pl.when((pl.program_id(0) == 0) & (pl.program_id(1) == 0))
        def _():
            fi, core = pos[2], pos[0] & 1
            depth, cols = wq.shape
            half = depth // 2
            for i, part in enumerate((wq, wk, wv)):
                w[pl.ds(pl.multiple_of(fi * depth, depth), depth), i * cols : (i + 1) * cols] = (
                    part[...]
                )
            base = (1 - fi) * depth
            w[pl.ds(pl.multiple_of(base + core * half, half), half), :] = near[...]
            w[pl.ds(pl.multiple_of(base + (1 - core) * half, half), half), :] = over[...]

    y = mm(x[0], w[...]).astype(BF)
    cols = q_ref.shape[2]
    q_ref[0] = y[:, :cols]
    kv_ref[0] = y[:, cols:]


def load_projection(pos, blocks, w):
    rows, depth = blocks[0].shape
    n = w.shape[0] // rows
    for j in range(n):
        at = slice(j * rows, (j + 1) * rows)
        if n == len(blocks):
            w[at, :] = blocks[j][...]
        else:
            fi = pos[2]
            w[at, pl.ds(pl.multiple_of(fi * depth, depth), depth)] = blocks[j][...]
            w[at, pl.ds(pl.multiple_of((1 - fi) * depth, depth), depth)] = blocks[n][j]


def mix_kernel(n, pos, *refs):
    att, blocks = refs[:n], refs[n:-10]
    tok, cell, gain, shift, hid_ref, n2_ref, stat_ref, w, left, branch = refs[-10:]

    load_projection(pos, blocks, w)
    stat_ref[...] = jnp.zeros(stat_ref.shape, F32)
    cols = att[0].shape[2]
    shape = tok.shape
    mine = shape[0] * shape[1]
    for j in range(n):
        left[:, j * cols : (j + 1) * cols] = att[j][...].reshape(mine, cols)
    branch[...] = mm(left[...], w[...])
    x = tok[...].astype(F32).reshape(mine, shape[2])
    gated = cell[...] * branch[...]
    hidden = x + gated
    hid_ref[...] = hidden.reshape(shape)
    xhat, _ = norm_stats(hidden)
    n2_ref[...] = (xhat * gain[...] + shift[...]).astype(BF).reshape(shape)
    stat_ref[0:1, :] = jnp.sum(x * x, axis=0, keepdims=True)
    stat_ref[1:2, :] = jnp.sum(gated * gated, axis=0, keepdims=True)


def ff_kernel(*refs):
    xs, gs = refs[0:2], refs[2:4]
    pack, first_ref, second_ref, act_ref, gup_ref, acc, xall, gall = refs[4:]
    nf, depth = pack.shape[1], pack.shape[3]
    z = pl.program_id(0)
    mine = xs[0].shape[0]
    cut = [slice(f * depth, (f + 1) * depth) for f in range(nf)]

    @pl.when(z == 0)
    def _():
        for p in range(2):
            xall[p] = xs[p][...]
            gall[p] = gs[p][...]
        acc[...] = jnp.zeros(acc.shape, F32)

    def one(p, carry):
        up = mm(xall[p, :, cut[0]], pack[0, 0, 0])
        back = mm(gall[p, :, cut[0]], pack[0, 0, 1])
        for f in range(1, nf):
            up = up + mm(xall[p, :, cut[f]], pack[0, f, 0])
            back = back + mm(gall[p, :, cut[f]], pack[0, f, 1])
        value, slope = gelu_parts(up)
        act_ref[p] = value.astype(BF)
        gup = (back * slope).astype(BF)
        gup_ref[p] = gup
        for f in range(nf):
            acc[p, :, cut[f]] += mm_nt(gup, pack[0, f, 0])
        return carry

    lax.fori_loop(0, 2, one, 0)

    @pl.when(z == pl.num_programs(0) - 1)
    def _():
        first_ref[...] = acc[0].astype(BF)
        second_ref[...] = acc[1].astype(BF)


def ff_grad_kernel(*refs):
    xs, gs = refs[0:4], refs[4:8]
    act_a, gup_a, act_b, gup_b, pack = refs[8:13]
    sent_ref, near_ref, far_ref, rows, acc, wout, units = refs[13:]
    _, nf, _, depth, fc = pack.shape
    mine = xs[0].shape[0]

    @pl.when(pl.program_id(0) == 0)
    def _():
        for p in range(4):
            rows[0, p * mine : (p + 1) * mine, :] = xs[p][...]
            rows[1, p * mine : (p + 1) * mine, :] = gs[p][...]
        acc[...] = jnp.zeros(acc.shape, F32)

    for f in range(nf):
        wout[f * depth : (f + 1) * depth, :] = pack[0, f, 1]
    for half, (a_ref, u_ref) in enumerate(((act_a, gup_a), (act_b, gup_b))):
        for p in range(2):
            at = slice((2 * half + p) * mine, (2 * half + p + 1) * mine)
            units[1, at, :] = a_ref[p]
            units[0, at, :] = u_ref[p]

    acc[...] += mm_nt(units[1], wout[...])

    def grads(i, carry):
        part = mm_tn(rows[i], units[i])
        for f in range(nf):
            sent_ref[f, 0, i] = part[f * depth : (f + 1) * depth].astype(BF)
        return carry

    lax.fori_loop(0, 2, grads, 0)

    @pl.when(pl.program_id(0) == pl.num_programs(0) - 1)
    def _():
        for i, ref in enumerate((near_ref, far_ref)):
            for p in range(2):
                lo = (2 * p + i) * mine
                ref[p] = acc[lo : lo + mine, :].astype(BF)


def branch_back_kernel(nt, pos, *refs):
    blocks, (own, got, far, hid, cot, cell, gain) = refs[: -(nt + 11)], refs[-(nt + 11) : -(nt + 4)]
    gh_ref, gb_ref = refs[-(nt + 4) : -(nt + 2)]
    ga_refs, stat_ref, w = refs[-(nt + 2) : -2], refs[-2], refs[-1]

    load_projection(pos, blocks, w)
    stat_ref[...] = jnp.zeros(stat_ref.shape, F32)
    shape = cot.shape
    mine = shape[0] * shape[1]
    flat = lambda v: v.astype(F32).reshape(mine, shape[2])
    grad = flat(own[...]) + flat(got[...]) + flat(far[...])
    xhat, scale = norm_stats(flat(hid[...]))
    gh = flat(cot[...]) + norm_back(grad, xhat, scale, gain[...])
    gh_ref[...] = gh.reshape(shape)
    gb = (cell[...] * gh).astype(BF)
    gb_ref[...] = gb.reshape(shape)
    cols = ga_refs[0].shape[2]
    for j, ref in enumerate(ga_refs):
        ref[...] = mm_nt(gb, w[j * cols : (j + 1) * cols, :]).astype(BF).reshape(ref.shape)
    stat_ref[0:1, :] = jnp.sum(grad * xhat, axis=0, keepdims=True)
    stat_ref[1:2, :] = jnp.sum(grad, axis=0, keepdims=True)


def combine_kernel(rows, pos, own, got, far, *refs):
    nt = (len(refs) - 1) // 2
    dq, total_ref, send = refs[:nt], refs[nt], refs[nt + 1 :]
    total = (
        own[0, 0, 0].astype(F32) + got[0, 0, 0].astype(F32) + far[0, 0].astype(F32)
    ).astype(BF)
    total_ref[0, 0] = total
    n = rows // nt
    m = (total_ref.shape[2] - rows) // nt
    kv = pl.program_id(1)
    for j in range(nt):
        k = lax.rem(pos[1] - j + nt, nt)

        @pl.when(kv == 0)
        def _():
            send[j][0, 0, :n, :] = dq[j][0]
            send[j][0, 0, n:, :] = jnp.zeros((m, dq[j].shape[2]), BF)

        send[j][1 + kv, 0, :n, :] = total_ref[0, 0, pl.ds(pl.multiple_of(k * n, n), n), :]
        send[j][1 + kv, 0, n:, :] = total_ref[0, 0, pl.ds(pl.multiple_of(rows + k * m, m), m), :]


def input_back_kernel(nt, pos, *refs):
    blocks = refs[:nt]
    parts, (tok, st, gh, gain, out_ref, stat_ref, w, left, every) = (
        refs[nt : nt + 4],
        refs[nt + 4 :],
    )
    m = parts[0].shape[1]
    nf = parts[0].shape[0] // nt
    cols = blocks[0].shape[3]
    trees, n = tok.shape[0], tok.shape[1]
    tall = blocks[0].shape[2]
    for flip, part in zip((0, 2, 1, 3), parts):

        def put(i, carry, flip=flip, part=part):
            z = lax.div(i, nf)
            at = ((i - z * nf) * 4 + jnp.bitwise_xor(pos[0], flip)) * m
            w[z, pl.ds(pl.multiple_of(at, m), m), :] = part[i]
            return carry

        lax.fori_loop(0, nt * nf, put, 0)
    for j in range(nt):
        for i in range(3):
            left[j, :, i * cols : (i + 1) * cols] = blocks[j][i].reshape(trees * tall, cols)
    step = 256

    def one(i, carry):
        at = pl.ds(pl.multiple_of(i * step, step), step)
        total = mm_nt(left[0], w[pos[1], at, :])
        for j in range(1, nt):
            total = total + mm_nt(left[j], w[lax.rem(pos[1] + j, nt), at, :])
        every[:, at] = total
        return carry

    lax.fori_loop(0, every.shape[1] // step, one, 0)
    stat_ref[...] = jnp.zeros(stat_ref.shape, F32)
    for t in range(trees):
        for x_ref, lo, hi, extra in ((tok, 0, n, gh), (st, n, tall, None)):
            grad = every[t * tall + lo : t * tall + hi, :]
            xhat, scale = norm_stats(x_ref[t].astype(F32))
            back = norm_back(grad, xhat, scale, gain[...])
            if extra is not None:
                back = back + extra[t]
            out_ref[t, lo:hi, :] = back.astype(BF)
            stat_ref[0:1, :] += jnp.sum(grad * xhat, axis=0, keepdims=True)
            stat_ref[1:2, :] += jnp.sum(grad, axis=0, keepdims=True)


def attn_grad_kernel(nt, pos, *refs):
    blocks, grad = refs[:nt], refs[nt]
    far_ref, mid_ref, own_ref, acc, left = refs[nt + 1 :]
    n = own_ref.shape[1]
    rows = grad.shape[0] * grad.shape[1]
    for j in range(nt):
        left[j] = blocks[j][...].reshape(rows, acc.shape[0])

    def one(j, carry):
        acc[...] = mm_tn(left[j], grad[...].reshape(rows, grad.shape[2]))
        for flip, ref in ((0, own_ref), (2, mid_ref), (1, far_ref), (3, far_ref)):
            k = jnp.bitwise_xor(pos[0], flip)
            piece = acc[pl.ds(pl.multiple_of(k * n, n), n), :]
            if flip & 1:
                ref[flip // 2, j] = piece.astype(BF)
            else:
                ref[j] = piece
        return carry

    lax.fori_loop(0, nt, one, 0)


def qkv_grad_kernel(nf, pos, x, gq, gkv, far_ref, mid_ref, own_ref, acc, right):
    t = pl.program_id(0)
    rows, cols = gq.shape[1], gq.shape[2]
    tall = x.shape[1]
    right[:rows, :cols] = gq[0]
    right[rows:, :cols] = jnp.zeros((tall - rows, cols), BF)
    right[:, cols : 2 * cols] = gkv[0, 0]
    right[:, 2 * cols :] = gkv[1, 0]

    @pl.when(t == 0)
    def _():
        acc[...] = jnp.zeros(acc.shape, F32)

    def one(i, carry):
        at = pl.ds(pl.multiple_of(i * cols, cols), cols)
        acc[:, at] += mm_tn(x[0], right[:, at])
        return carry

    lax.fori_loop(0, 3, one, 0)

    @pl.when(t == pl.num_programs(0) - 1)
    def _():
        n = own_ref.shape[1]
        for f in range(nf):
            for flip, ref in ((0, own_ref), (2, mid_ref), (1, far_ref), (3, far_ref)):
                k = jnp.bitwise_xor(pos[0], flip)
                start = pl.multiple_of(f * (acc.shape[0] // nf) + k * n, n)
                piece = acc[pl.ds(start, n), :]
                if flip & 1:
                    ref[flip // 2, f] = piece.astype(BF)
                else:
                    ref[f] = piece


def order_kernel(sizes, places, *refs):
    outs = refs[-len(sizes) :]
    for i, block in enumerate(refs[: -len(sizes)]):
        lo = 0
        for n, out in zip(sizes, outs):
            out[0, pl.ds(pl.multiple_of(places[i] * n, n), n), :] = block[0, lo : lo + n, :]
            lo = lo + n


def finish_ff_kernel(pos, *refs):
    gin, gout = refs[4:]
    depth, fc = gin.shape[0], refs[0].shape[1]
    for flip, b in zip((0, 2, 1, 3), refs[:4]):
        k = jnp.bitwise_xor(pos[0], flip)
        at = pl.ds(pl.multiple_of(k * fc, fc), fc)
        gin[:, at] = b[:depth, :].astype(F32)
        gout[at, :] = b[depth:, :].astype(F32).T


def finish_qkv_kernel(pos, *refs):
    for flip, b in zip((0, 2, 1, 3), refs[:4]):
        n = b.shape[0]
        k = jnp.bitwise_xor(pos[0], flip)
        at = pl.ds(pl.multiple_of(k * n, n), n)
        cols = refs[4].shape[1]
        for i, out in enumerate(refs[4:7]):
            out[at, :] = b[:, i * cols : (i + 1) * cols].astype(F32)
        for out in refs[7:]:
            m = n * (b.shape[1] - 3 * cols) // out.shape[1]
            wide = b.shape[1] - 3 * cols
            at = pl.ds(pl.multiple_of(k * m, m), m)
            for i in range(n // m):
                out[at, i * wide : (i + 1) * wide] = b[
                    i * m : (i + 1) * m, 3 * cols :
                ].astype(F32)


def build(mesh):
    nf, nc, nt = mesh.shape["fsdp"], mesh.shape["context"], mesh.shape["tensor"]
    assert nc == 4

    def px(x):
        return lax.ppermute(x, "fsdp", [(0, 1), (1, 0)])

    def pc(x, k):
        return lax.ppermute(x, "context", [(a, a ^ k) for a in range(nc)])

    def pz(x, j):
        return lax.ppermute(x, "tensor", [(a, (a - j) % nt) for a in range(nt)])

    def ps(x, j):
        return lax.ppermute(x, "tensor", [(a, (a + j) % nt) for a in range(nt)])

    def on_device(
        tokens,
        state,
        parent,
        seg_length,
        cell_gate,
        norm1_gain,
        norm1_shift,
        w_query,
        w_key,
        w_value,
        w_attn_out,
        rel_bias,
        norm2_gain,
        norm2_shift,
        w_in,
        w_out,
        cotangent,
    ):
        trees, rows, width = tokens.shape
        local_segs = seg_length.shape[1]
        seg = rows // local_segs
        all_segs = parent.shape[1]
        heads = rel_bias.shape[0]
        depth, cols = w_query.shape
        head_dim = cols // heads
        each = state.shape[1]
        tall = rows + each
        fi, ci, zi = lax.axis_index("fsdp"), lax.axis_index("context"), lax.axis_index("tensor")
        core = ci & 1
        zr, zs = rows // nt, each // nt
        mine = trees * zr
        pos = jnp.stack([ci, zi, fi]).astype(jnp.int32)
        cell, gain_1, shift_1, gain_2, shift_2 = (
            v.reshape(1, width)
            for v in (cell_gate, norm1_gain, norm1_shift, norm2_gain, norm2_shift)
        )
        sds = jax.ShapeDtypeStruct

        def gate(*xs):
            return lax.optimization_barrier(xs)

        stat = sds((8, width), F32)

        def call(body, grid, ins, outs, out_shape, scratch=(), prefetch=1, vmem=24, name="", us=4, keep=False):
            return hbm_call(
                prefetch,
                body,
                out_shape=out_shape,
                grid_spec=pltpu.PrefetchScalarGridSpec(
                    num_scalar_prefetch=prefetch,
                    grid=grid,
                    in_specs=ins,
                    out_specs=outs,
                    scratch_shapes=scratch,
                ),
                compiler_params=pltpu.CompilerParams(vmem_limit_bytes=vmem << 20),
                cost_estimate=cost(us),
                keep=keep,
                name=name,
            )

        def whole(shape):
            return pl.BlockSpec(shape, lambda *_: (0,) * len(shape))

        row_1 = whole((1, width))
        stat_spec = whole((8, width))

        def place(blocks, starts, axis, total):
            shape = list(blocks[0].shape)
            shape[axis] = total
            out = jnp.zeros(shape, blocks[0].dtype)
            for block, start in zip(blocks, starts):
                out = lax.dynamic_update_slice_in_dim(out, block, start, axis)
            return out

        def half_of(x, k, axis, parts):
            n = x.shape[axis] // parts
            return lax.dynamic_slice_in_dim(x, k * n, n, axis)

        def gather_f(x, axis):
            n = x.shape[axis]
            if nf == 2:
                return place([x, px(x)], [fi * n, (1 - fi) * n], axis, 2 * n)
            return lax.all_gather(x, "fsdp", axis=axis, tiled=True)

        def scatter_f(x, axis):
            if nf == 2:
                sent = half_of(x, 1 - fi, axis, 2).astype(BF)
                return half_of(x, fi, axis, 2) + px(sent).astype(F32)
            return lax.psum_scatter(
                x.astype(BF), "fsdp", scatter_dimension=axis, tiled=True
            ).astype(F32)

        def gather_c(x, axis):
            n = x.shape[axis]
            pair = jnp.stack([x, pc(x, 2)])
            over = pc(pair, 1)
            return place(
                [x, pair[1], over[0], over[1]],
                [ci * n, (ci ^ 2) * n, (ci ^ 1) * n, (ci ^ 3) * n],
                axis,
                nc * n,
            )

        def scatter_c(x, axis):
            cut = lambda k: half_of(x, k, axis, nc)
            sent = jnp.stack([cut(ci ^ 1), cut(ci ^ 3)]).astype(BF)
            got = pc(sent, 1).astype(F32)
            far = (cut(ci ^ 2) + got[1]).astype(BF)
            return cut(ci) + got[0] + pc(far, 2).astype(F32)

        if nf == 2:
            half = depth // 2
            near_send = jnp.concatenate(
                [half_of(w, core, 0, 2) for w in (w_query, w_key, w_value)], axis=1
            )
            near_send, w_in, w_out = gate(near_send, w_in, w_out)
            near_w = px(near_send)
            near_w, w_attn_out = gate(near_w, w_attn_out)
            over_w = pc(near_w, 1)
            weights = (w_query, w_key, w_value, near_w, over_w)
            weight_specs = [whole((depth, cols))] * 3 + [whole((half, 3 * cols))] * 2
            w_scratch = [pltpu.VMEM((2 * depth, 3 * cols), BF)]
        else:
            full_w = lax.all_gather(
                jnp.concatenate([w_query, w_key, w_value], axis=1), "fsdp", axis=0, tiled=True
            )
            weights = (full_w,)
            weight_specs = [whole(full_w.shape)]
            w_scratch = []

        fc = w_in.shape[1] // nc
        pack = jnp.stack([half_of(w_in, ci, 1, nc), half_of(w_out, ci, 0, nc).T])
        packs = lax.all_gather(pack, ("tensor", "fsdp"), axis=0, tiled=False)
        packs = packs.reshape(nt, nf, 2, depth, fc)

        o_blocks = [w_attn_out] + [pz(w_attn_out, j) for j in range(1, nt)]
        o_over = []

        normed = call(
            norm_kernel,
            (trees,),
            [
                row_1,
                row_1,
                pl.BlockSpec((1, rows, width), lambda t: (t, 0, 0)),
                pl.BlockSpec((1, each, width), lambda t: (t, 0, 0)),
            ],
            pl.BlockSpec((1, tall, width), lambda t: (t, 0, 0)),
            sds((trees, tall, width), BF),
            prefetch=0,
            name="norm",
            us=5,
        )(gain_1, shift_1, tokens, state)
        tile = tall // 3
        queries, kv = call(
            project_kernel,
            (trees, 3),
            [pl.BlockSpec((1, tile, width), lambda t, i, *_: (t, i, 0))] + weight_specs,
            (
                pl.BlockSpec((1, tile, cols), lambda t, i, *_: (t, i, 0)),
                pl.BlockSpec((1, tile, 2 * cols), lambda t, i, *_: (t, i, 0)),
            ),
            (sds((trees, tall, cols), BF), sds((trees, tall, 2 * cols), BF)),
            w_scratch,
            name="project",
        )(pos, normed, *weights)
        kv_y = pc(kv, 2)
        kv_c = pc(kv, 1)
        grad_low = half_of(cotangent, zi, 1, nt).reshape(mine, width)
        kv_y, grad_low, *o_blocks = gate(kv_y, grad_low, *o_blocks)
        kv_cy = pc(kv_y, 1)
        if nf == 2:
            o_over = [px(jnp.stack(o_blocks))]
        else:
            full = lax.all_gather(jnp.stack(o_blocks), "fsdp", axis=2, tiled=True)
            o_blocks = [full[j] for j in range(nt)]
        grad_y = pc(grad_low, 2)
        grad_c = pc(grad_low, 1)

        forward, backward = attention_calls(
            trees, heads, local_segs, all_segs, seg, each, head_dim, nt
        )
        tables = (parent, seg_length, pos, rel_bias)
        sources = (queries, kv, kv_c, kv_y, kv_cy, kv, kv_c, kv_y, kv_cy)
        *att_send, log_total = forward(*tables, *sources)
        quarter = jnp.concatenate(
            [half_of(w, ci, 0, nc) for w in (w_query, w_key, w_value)], axis=1
        )
        att_send[0], quarter = gate(att_send[0], quarter)
        all_q = lax.all_gather(quarter, ("tensor", "fsdp"), axis=0, tiled=False)

        att = [att_send[0]] + [pz(att_send[j], j) for j in range(1, nt)]
        att[1], grad_y, *o_over = gate(att[1], grad_y, *o_over)
        grad_rows = [grad_low, grad_y, grad_c, pc(grad_y, 1)]
        chunk = whole((trees, zr, width))
        chunk_z = pl.BlockSpec((trees, zr, width), lambda i, pos: (0, pos[1], 0))
        small = whole((trees, zr, cols))
        o_all = tuple(o_blocks) + tuple(o_over)
        o_specs = [whole(o.shape) for o in o_all]
        o_scratch = [pltpu.VMEM((nt * cols, width), BF)]
        hidden, normed_two, stat_a = call(
            functools.partial(mix_kernel, nt),
            (1,),
            [small] * nt + o_specs + [chunk_z, row_1, row_1, row_1],
            (chunk, chunk, stat_spec),
            (sds((trees, zr, width), F32), sds((trees, zr, width), BF), stat),
            o_scratch
            + [pltpu.VMEM((mine, nt * cols), BF), pltpu.VMEM((mine, width), F32)],
            name="mix",
            keep=True,
        )(pos, *att, *o_all, tokens, cell, gain_2, shift_2)

        rows_two = normed_two.reshape(mine, width)
        rows_y = pc(rows_two, 2)
        rows_c = pc(rows_two, 1)
        block = whole((mine, width))
        units = nt * fc
        half_spec = whole((2, mine, width))
        half_sds, full_sds = sds((2, mine, width), BF), sds((2, mine, units), BF)
        unit_spec = pl.BlockSpec((2, mine, fc), lambda z, *_: (0, 0, z))
        pack_spec = pl.BlockSpec((1,) + packs.shape[1:], lambda z, *_: (z, 0, 0, 0, 0))
        feed = call(
            ff_kernel,
            (nt,),
            [block] * 4 + [pack_spec],
            (block, block, unit_spec, unit_spec),
            (sds((mine, width), BF), sds((mine, width), BF), full_sds, full_sds),
            [pltpu.VMEM((2, mine, width), F32)] + [pltpu.VMEM((2, mine, width), BF)] * 2,
            prefetch=0,
            vmem=32,
            name="feed",
            keep=True,
            us=9,
        )
        gn_own, gn_c, act_a, gup_a = feed(rows_two, rows_c, grad_rows[0], grad_rows[2], packs)
        rows_y, gn_own, gn_c = gate(rows_y, gn_own, gn_c)
        rows_cy = pc(rows_y, 1)
        gn_got = [pc(gn_c, 1)]
        gn_y, gn_cy, act_b, gup_b = feed(rows_y, rows_cy, grad_rows[1], grad_rows[3], packs)
        ff_rows = [rows_two, rows_c, rows_y, rows_cy]
        cot_rows = [grad_rows[0], grad_rows[2], grad_rows[1], grad_rows[3]]
        gn_got.append(pc(gn_cy, 1))
        gn_mid = (gn_y.astype(F32) + gn_got[1].astype(F32)).astype(BF)
        gn_mid, gn_got[0], act_b, gup_b = gate(gn_mid, gn_got[0], act_b, gup_b)
        gn_end = pc(gn_mid, 2)
        ff_sent, ff_near, ff_far = call(
            ff_grad_kernel,
            (nt,),
            [block] * 8 + [unit_spec] * 4 + [pack_spec],
            (
                pl.BlockSpec((nf, 1, 2, depth, fc), lambda z, *_: (0, z, 0, 0, 0)),
                half_spec,
                half_spec,
            ),
            (sds((nf, nt, 2, depth, fc), BF), half_sds, half_sds),
            [
                pltpu.VMEM((2, 4 * mine, width), BF),
                pltpu.VMEM((4 * mine, width), F32),
                pltpu.VMEM((width, fc), BF),
                pltpu.VMEM((2, 4 * mine, fc), BF),
            ],
            prefetch=0,
            vmem=56,
            name="feed_grads",
            keep=True,
            us=16,
        )(*ff_rows, *cot_rows, act_a, gup_a, act_b, gup_b, packs)
        gn_end, ff_sent, ff_near, ff_far, all_q = gate(gn_end, ff_sent, ff_near, ff_far, all_q)
        ff_got = pc(ff_far, 1)

        grad_hidden, grad_branch, *rest = call(
            functools.partial(branch_back_kernel, nt),
            (1,),
            o_specs + [chunk] * 4 + [chunk_z, row_1, row_1],
            (chunk, chunk) + (small,) * nt + (stat_spec,),
            (sds((trees, zr, width), F32), sds((trees, zr, width), BF))
            + (sds((trees, zr, cols), BF),) * nt
            + (stat,),
            o_scratch,
            name="branch_back",
            keep=True,
        )(
            pos,
            *o_all,
            gn_own.reshape(trees, zr, width),
            gn_got[0].reshape(trees, zr, width),
            gn_end.reshape(trees, zr, width),
            hidden,
            cotangent,
            cell,
            gain_2,
        )
        stat_b = rest.pop()
        ff_got, grad_branch, *rest = gate(ff_got, grad_branch, *rest)
        all_q, rest[0] = gate(all_q, rest[0])
        all_y = pc(all_q, 2)
        grad_heads = [rest[0]] + [ps(rest[j], j) for j in range(1, nt)]
        ff_mid = (ff_near[1].astype(F32) + ff_got[1].astype(F32)).astype(BF)
        ff_end = pc(ff_mid, 2)
        o_rows = cols // nc
        att_specs = (whole((2, nt, o_rows, width)),) + (whole((nt, o_rows, width)),) * 2
        attn_far, attn_mid, attn_near = call(
            functools.partial(attn_grad_kernel, nt),
            (1,),
            [whole((trees, zr, cols))] * nt + [whole((trees, zr, width))],
            att_specs,
            (
                sds((2, nt, o_rows, width), BF),
                sds((nt, o_rows, width), F32),
                sds((nt, o_rows, width), F32),
            ),
            [pltpu.VMEM((cols, width), F32), pltpu.VMEM((nt, mine, cols), BF)],
            name="attn_grads",
            us=4,
        )(pos, *att, grad_branch)

        mlp_out = ff_near[0].astype(F32) + ff_got[0].astype(F32) + ff_end.astype(F32)
        result = (hidden.reshape(mine, width) + mlp_out).astype(BF)
        result, attn_near, attn_mid, attn_far, *grad_heads = gate(
            result, attn_near, attn_mid, attn_far, *grad_heads
        )
        result = result.reshape(trees, zr, width)

        def spread_near(x):
            if nt == 4:
                return [
                    lax.ppermute(x, "tensor", [(0, 1), (1, 2), (2, 3)]),
                    lax.ppermute(x, "tensor", [(1, 0), (2, 1), (3, 2)]),
                ]
            return [pz(x, 1), pz(x, nt - 1)]

        def ordered(blocks, places, sizes):
            n = blocks[0].shape[1]
            return call(
                functools.partial(order_kernel, sizes),
                (trees,),
                [pl.BlockSpec((1, n, width), lambda t, *_: (t, 0, 0))] * len(blocks),
                tuple(
                    pl.BlockSpec((1, nt * m, width), lambda t, *_: (t, 0, 0)) for m in sizes
                ),
                tuple(sds((trees, nt * m, width), BF) for m in sizes),
                name="order",
                us=1,
            )(jnp.stack(places).astype(jnp.int32), *blocks)

        def swap(x, pairs):
            return lax.ppermute(x, "tensor", pairs + [(b, a) for a, b in pairs])

        first_at = [jnp.maximum(zi - 1, 0), jnp.minimum(zi + 1, nt - 1), zi]

        out_near = spread_near(result)
        attn_got = pc(attn_far, 1)

        *dq_send, grad_q, kv_near, kv_far, bias_rows = backward(
            *tables, *sources, *grad_heads, log_total
        )
        ff_half = lax.psum_scatter(ff_sent, "fsdp", scatter_dimension=0, tiled=True)[0]
        ff_half = ff_half.reshape(nt, 2 * depth, fc)
        kv_far, kv_near, attn_got, all_y, *out_near = gate(
            kv_far, kv_near, attn_got, all_y, *out_near
        )
        kv_got = pc(kv_far, 1)
        kv_mid = (kv_near[1].astype(F32) + kv_got[1].astype(F32)).astype(BF)
        own = lax.psum_scatter(ff_half, "tensor", scatter_dimension=0, tiled=True)[0]
        kv_mid, result, attn_got, attn_near, attn_mid, all_q, all_y = gate(
            kv_mid, result, attn_got, attn_near, attn_mid, all_q, all_y
        )
        all_w = [all_q, all_y, pc(all_q, 1), pc(all_y, 1)]
        kv_end = pc(kv_mid, 2)
        if nt == 4:
            out_far = [swap(result, [(0, 2), (1, 3)])]
            out_far.append(
                lax.ppermute(out_far[0], "tensor", [(2, 3), (1, 0), (3, 2), (0, 1)])
            )
        else:
            out_far = [pz(result, j) for j in range(2, nt - 1)]
        attn_two = jnp.stack([attn_near, attn_mid]) + attn_got.astype(F32)
        attn_two = scatter_f(attn_two, 3)
        attn_end = pc(attn_two[1].astype(BF), 2)
        kv_end, attn_two, attn_end, all_w, *out_far = gate(
            kv_end, attn_two, attn_end, all_w, *out_far
        )
        attn_sum = (attn_two[0] + attn_end.astype(F32)).astype(BF)
        attn_sum = lax.dynamic_slice_in_dim(
            jnp.concatenate([attn_sum, attn_sum], axis=0), nt - zi, nt, 0
        )
        attn_own = lax.psum_scatter(attn_sum, "tensor", scatter_dimension=0, tiled=True)[0]
        five = pl.BlockSpec((1, 1, 1, tall, cols), lambda t, k, *_: (0, k, t, 0, 0))
        four = pl.BlockSpec((1, 1, tall, cols), lambda t, k, *_: (k, t, 0, 0))
        send = pl.BlockSpec((3, 1, zr + zs, cols), lambda t, k, *_: (0, t, 0, 0))
        grad_kv, *kv_send = call(
            functools.partial(combine_kernel, rows),
            (trees, 2),
            [five, five, four]
            + [pl.BlockSpec((1, zr, cols), lambda t, k, *_: (t, 0, 0))] * nt,
            (four,) + (send,) * nt,
            (sds((2, trees, tall, cols), BF),) + (sds((3, trees, zr + zs, cols), BF),) * nt,
            name="combine",
            keep=True,
        )(pos, kv_near, kv_got, kv_end, *dq_send)
        dqkv = [kv_send[0]] + [pz(kv_send[j], j) for j in range(1, nt)]

        dq_rows = depth // nc
        cut_specs = (whole((2, nf, dq_rows, 3 * cols)),) + (whole((nf, dq_rows, 3 * cols)),) * 2
        qkv_far, qkv_mid, qkv_own = call(
            functools.partial(qkv_grad_kernel, nf),
            (trees,),
            [
                pl.BlockSpec((1, tall, width), lambda t, *_: (t, 0, 0)),
                pl.BlockSpec((1, rows, cols), lambda t, *_: (t, 0, 0)),
                pl.BlockSpec((2, 1, tall, cols), lambda t, *_: (0, t, 0, 0)),
            ],
            cut_specs,
            (
                sds((2, nf, dq_rows, 3 * cols), BF),
                sds((nf, dq_rows, 3 * cols), F32),
                sds((nf, dq_rows, 3 * cols), F32),
            ),
            [pltpu.VMEM((nf * depth, 3 * cols), F32), pltpu.VMEM((tall, 3 * cols), BF)],
            name="qkv_grads",
            keep=True,
            us=8,
        )(pos, normed, grad_q, grad_kv)
        if nt == 4:
            places = first_at + [zi ^ 2, 3 - zi]
            blocks = [out_near[0], out_near[1], result, *out_far]
        else:
            blocks = [result, *out_near, *out_far]
            places = [zi, (zi + 1) % nt, (zi - 1) % nt] + [(zi + j) % nt for j in range(2, nt - 1)]
        (output,) = ordered(blocks, places, (zr,))
        own_y = pc(own, 2)
        qkv_mid, qkv_own, qkv_far, own_y, output, attn_own, *dqkv = gate(
            qkv_mid, qkv_own, qkv_far, own_y, output, attn_own, *dqkv
        )
        qkv_got = pc(qkv_far, 1)
        own_blocks = (own, own_y, pc(own, 1), pc(own_y, 1))

        chunk_sz = pl.BlockSpec((trees, zs, width), lambda i, pos: (0, pos[1], 0))
        grads_own, stat_c = call(
            functools.partial(input_back_kernel, nt),
            (1,),
            [whole((3, trees, zr + zs, cols))] * nt
            + [whole(all_q.shape)] * 4
            + [chunk_z, chunk_sz, chunk, row_1],
            (whole((trees, zr + zs, width)), stat_spec),
            (sds((trees, zr + zs, width), BF), stat),
            [
                pltpu.VMEM((nt, nf * depth, 3 * cols), BF),
                pltpu.VMEM((nt, trees * (zr + zs), 3 * cols), BF),
                pltpu.VMEM((trees * (zr + zs), width), F32),
            ],
            vmem=44,
            name="input_back",
            keep=True,
        )(pos, *dqkv, *all_w, tokens, state, grad_hidden, gain_1)
        grads_own, qkv_got, *own_blocks = gate(grads_own, qkv_got, *own_blocks)
        qkv_got = qkv_got.astype(F32)

        bias_own = jnp.sum(bias_rows, axis=2)
        bias_all = lax.dynamic_update_slice(
            jnp.zeros((heads * nt, BUCKETS), F32), bias_own, (zi * heads, 0)
        )
        squares = jnp.stack([jnp.sum(stat_a[0]), jnp.sum(stat_a[1]), jnp.sum(mlp_out * mlp_out)])
        spare = jnp.zeros((2 * width - bias_all.size - 3,), F32)
        early = jnp.concatenate(
            [
                stat_b[:2],
                jnp.concatenate([bias_all.reshape(-1), squares, spare]).reshape(2, width),
            ],
            axis=0,
        )
        early, grads_own = gate(early, grads_own)
        sums = jnp.concatenate([stat_c[:2], early], axis=0)

        in_near = spread_near(grads_own)
        *in_near, sums, attn_own, qkv_got = gate(*in_near, sums, attn_own, qkv_got)
        qkv_end = pc((qkv_mid + qkv_got[1]).astype(BF), 2)
        if nt == 4:
            c = swap(grads_own, [(0, 2), (1, 3)])
            d = lax.ppermute(c, "tensor", [(2, 3), (1, 0), (3, 2), (0, 1)])
            places = first_at + [zi ^ 2, 3 - zi]
            blocks = [in_near[0], in_near[1], grads_own, c, d]
        else:
            in_far = [pz(grads_own, j) for j in range(2, nt - 1)]
            blocks = [grads_own, *in_near, *in_far]
        tokens_grad, state_grad = ordered(blocks, places, (zr, zs))
        sums = sums + px(sums) if nf == 2 else lax.psum(sums, "fsdp")
        sums = sums + pc(sums, 1)
        sums = sums + pc(sums, 2)
        if nt & (nt - 1):
            sums = lax.psum(sums, "tensor")
        else:
            k = 1
            while k < nt:
                sums = sums + lax.ppermute(sums, "tensor", [(a, a ^ k) for a in range(nt)])
                k = 2 * k

        qkv_sum = scatter_f(qkv_own + qkv_got[0] + qkv_end.astype(F32), 0)[0].astype(BF)
        if depth % o_rows == 0 and depth * o_rows % dq_rows == 0 and nf == 2:
            folded = jnp.concatenate([attn_own[:, :fc], attn_own[:, fc:]], axis=0)
            qkv_sum = jnp.concatenate([qkv_sum, folded], axis=1)
        else:
            attn_full = gather_c(attn_own, 0).astype(F32)
            folded = None
        qkv_y = pc(qkv_sum, 2)
        qkv_blocks = (qkv_sum, qkv_y, pc(qkv_sum, 1), pc(qkv_y, 1))
        last_shapes = ((depth, cols),) * 3
        if folded is not None:
            last_shapes += ((nc * o_rows, depth),)
        *grad_qkv, grad_attn_out = call(
            finish_qkv_kernel,
            (1,),
            [whole(qkv_sum.shape)] * 4,
            tuple(whole(v) for v in last_shapes),
            tuple(sds(v, F32) for v in last_shapes),
            name="finish_qkv",
            us=0,
        )(pos, *qkv_blocks) + (() if folded is not None else (attn_full,))
        grad_in, grad_out = call(
            finish_ff_kernel,
            (1,),
            [whole(own.shape)] * 4,
            (whole((depth, nc * fc)), whole((nc * fc, depth))),
            (sds((depth, nc * fc), F32), sds((nc * fc, depth), F32)),
            name="finish_ff",
            us=0,
        )(pos, *own_blocks)
        last = sums[4:].reshape(-1)
        bias_sum = last[: bias_all.size].reshape(bias_all.shape)
        grad_bias = lax.dynamic_slice_in_dim(bias_sum, zi * heads, heads, 0)
        cell_count = trees * rows * width * nf * nc
        norms = jnp.sqrt(last[bias_all.size : bias_all.size + 3] / cell_count)
        return (
            output,
            tokens_grad,
            state_grad,
            *grad_qkv,
            grad_attn_out,
            grad_bias,
            sums[0],
            sums[1],
            sums[2],
            sums[3],
            grad_in,
            grad_out,
            norms,
        )

    return on_device


def solution(mesh):
    return jax.shard_map(
        build(mesh),
        mesh=mesh,
        in_specs=(
            P("fsdp", "context", None),
            P("fsdp", "context", None),
            P("fsdp", None),
            P("fsdp", "context"),
            P(),
            P(),
            P(),
            P("fsdp", "tensor"),
            P("fsdp", "tensor"),
            P("fsdp", "tensor"),
            P("tensor", "fsdp"),
            P("tensor", None),
            P(),
            P(),
            P("fsdp", "tensor"),
            P("tensor", "fsdp"),
            P("fsdp", "context", None),
        ),
        out_specs=(
            P("fsdp", "context", None),
            P("fsdp", "context", None),
            P("fsdp", "context", None),
            P("fsdp", "tensor"),
            P("fsdp", "tensor"),
            P("fsdp", "tensor"),
            P("tensor", "fsdp"),
            P("tensor", None),
            P(),
            P(),
            P(),
            P(),
            P("fsdp", "tensor"),
            P("tensor", "fsdp"),
            P(),
        ),
        check_vma=False,
    )
```

```python
import functools
import math

import jax
import jax.numpy as jnp
from jax import lax
from jax.experimental import pallas as pl
from jax.experimental.pallas import tpu as pltpu
from jax.sharding import PartitionSpec as P

WINDOW = 512
BUCKETS = 32
REACH = 128
EPSILON = 1e-05
MASKED = -1e30
GELU_C = 0.7978845608028654
GELU_A = 0.044715
BF = jnp.bfloat16
F32 = jnp.float32


def cost(us):
    return pl.CostEstimate(
        flops=int(us * 1e9), transcendentals=0, bytes_accessed=int(us * 3e6)
    )


def bucket_edges(bucket_total, far_reach, window):
    exact_count = bucket_total // 2
    boundaries = []
    current = 0
    for distance in range(window):
        if distance < exact_count:
            bucket = distance
        else:
            bucket = exact_count + int(
                math.log(distance / exact_count)
                / math.log(far_reach / exact_count)
                * (bucket_total - exact_count)
            )
            bucket = min(bucket, bucket_total - 1)
        while current < bucket:
            current = current + 1
            boundaries.append(distance)
    return boundaries


EDGES = bucket_edges(BUCKETS, REACH, WINDOW)


def mm(left, right):
    return lax.dot_general(left, right, (((1,), (0,)), ((), ())), preferred_element_type=F32)


def mm_nt(left, right):
    return lax.dot_general(left, right, (((1,), (1,)), ((), ())), preferred_element_type=F32)


def mm_tn(left, right):
    return lax.dot_general(left, right, (((0,), (0,)), ((), ())), preferred_element_type=F32)


def bias_tables(rb_ref, h, levels, seg, bm_ref):
    key = lax.broadcasted_iota(jnp.int32, (seg, seg), 0)
    query = lax.broadcasted_iota(jnp.int32, (seg, seg), 1)
    for lev in range(levels):
        dist = lev * seg + query - key
        low, high = lev * seg - (seg - 1), lev * seg + seg - 1
        if low >= EDGES[-1]:
            val = jnp.full((seg, seg), rb_ref[h, BUCKETS - 1], F32)
        else:
            val = jnp.full((seg, seg), rb_ref[h, 0], F32)
            for i, edge in enumerate(EDGES):
                if edge <= high:
                    val = jnp.where(dist >= edge, rb_ref[h, i + 1], val)
        if low < 0:
            val = jnp.where(dist >= 0, val, MASKED)
        if high >= WINDOW:
            val = jnp.where(dist < WINDOW, val, MASKED)
        bm_ref[lev * seg : (lev + 1) * seg, :] = val


def chain(par_ref, t, first, levels, all_segs, local_segs, ctx):
    out = []
    anc = first
    for lev in range(levels):
        if lev > 0:
            up = par_ref[t, jnp.maximum(anc, 0)]
            anc = jnp.where(anc >= 0, up, -1)
        safe = jnp.maximum(anc, 0)
        owner = lax.div(safe, local_segs)
        out.append((anc >= 0, jnp.bitwise_xor(owner, ctx), safe - owner * local_segs))
    return out


def window_score(raw, lev, bm_ref, line, length, seg):
    part = raw + bm_ref[lev * seg : (lev + 1) * seg, :]
    if lev == 0:
        key = lax.broadcasted_iota(jnp.int32, (seg, 1), 0)
        return part + jnp.where(key < length, 0.0, MASKED)
    return part + jnp.where(line[lev][0], 0.0, MASKED)


def fold(value, op):
    out = value[0:8]
    for i in range(8, value.shape[0], 8):
        out = op(out, value[i : i + 8])
    return out


def attend_kernel(dims, par_ref, len_ref, pos_ref, rb_ref, q_ref, *refs):
    levels, seg, local_segs, all_segs, factor, nt = dims
    parts_k, parts_v = refs[0:4], refs[4:8]
    att_refs, lse_ref = refs[8 : 8 + nt], refs[8 + nt]
    kall, vall_t, kws, vw_ts, bm, whole, q_t, raws_a, probs_a = refs[9 + nt :]
    t, h = pl.program_id(0), pl.program_id(1)
    ctx, zi = pos_ref[0], pos_ref[1]
    rows, win = local_segs * seg, levels * seg
    each = (kws.shape[1] - win) // 4
    blocks = kws.shape[1] // seg
    bias_tables(rb_ref, h, levels, seg, bm)
    for b in range(4):
        at = slice(win + b * each, win + (b + 1) * each)
        kall[b] = parts_k[b][0, :rows, :]
        turned = parts_v[b][0].T
        vall_t[b] = turned[:, :rows]
        for i in range(2):
            kws[i, at, :] = parts_k[b][0, rows:, :]
            vw_ts[i, :, at] = turned[:, rows:]
    q_t[...] = q_ref[0, :rows, :].T

    def one(s, carry):
        kw, vw_t, raws, probs = (r.at[s % 2] for r in (kws, vw_ts, raws_a, probs_a))
        line = chain(par_ref, t, ctx * local_segs + s, levels, all_segs, local_segs, ctx)
        for lev, (_, part, block) in enumerate(line):
            start = pl.ds(pl.multiple_of(block * seg, seg), seg)
            kw[lev * seg : (lev + 1) * seg, :] = kall[part, start, :]
            vw_t[:, lev * seg : (lev + 1) * seg] = vall_t[part, :, start]
        at = slice(s * seg, (s + 1) * seg)
        turned = q_t[:, at]
        top = None
        for c in range(blocks):
            raw = mm(kw[c * seg : (c + 1) * seg, :], turned) * factor
            if c < levels:
                raw = window_score(raw, c, bm, line, len_ref[t, s], seg)
            raws[c * seg : (c + 1) * seg, :] = raw
            high = fold(raw, jnp.maximum)
            top = high if top is None else jnp.maximum(top, high)
        top = jnp.max(top, axis=0, keepdims=True)
        total = None
        for c in range(blocks):
            prob = jnp.exp(raws[c * seg : (c + 1) * seg, :] - top)
            probs[c * seg : (c + 1) * seg, :] = prob.astype(BF)
            part = fold(prob, jnp.add)
            total = part if total is None else total + part
        total = jnp.sum(total, axis=0, keepdims=True)
        lse_ref[0, 0, 0:1, at] = top + jnp.log(total)
        att = mm(vw_t[...], probs[...]) / total
        whole[at, :] = att.T.astype(BF)
        return carry

    for s in range(local_segs):
        one(s, 0)
    n = rows // nt
    for j in range(nt):
        k = lax.rem(zi - j + nt, nt)
        att_refs[j][0] = whole[pl.ds(pl.multiple_of(k * n, n), n), :]


def attend_back_kernel(dims, par_ref, len_ref, pos_ref, rb_ref, q_ref, *refs):
    levels, seg, local_segs, all_segs, factor, nt = dims
    parts_k, parts_v = refs[0:4], refs[4:8]
    do_refs, lse_ref = refs[8 : 8 + nt], refs[8 + nt]
    dq_refs = refs[9 + nt : 9 + 2 * nt]
    dq_ref, near_ref, far_ref, db_ref = refs[9 + 2 * nt : 13 + 2 * nt]
    kall, vall, kall_t, kw, vw, kw_t, bm, dk, dv, near, far, dos, do_t, q_t, raws, dps, dss, pbs = refs[
        13 + 2 * nt :
    ]
    h, t = pl.program_id(0), pl.program_id(1)
    ctx, zi = pos_ref[0], pos_ref[1]
    rows, win = local_segs * seg, levels * seg
    each = (kw.shape[0] - win) // 4
    blocks = kw.shape[0] // seg
    n = rows // nt
    bias_tables(rb_ref, h, levels, seg, bm)
    for b in range(4):
        at = slice(win + b * each, win + (b + 1) * each)
        kall[b] = parts_k[b][0, :rows, :]
        vall[b] = parts_v[b][0, :rows, :]
        turned = parts_k[b][0].T
        kall_t[b] = turned[:, :rows]
        kw[at, :] = parts_k[b][0, rows:, :]
        vw[at, :] = parts_v[b][0, rows:, :]
        kw_t[:, at] = turned[:, rows:]
    dk[...] = jnp.zeros(dk.shape, F32)
    dv[...] = jnp.zeros(dv.shape, F32)
    for j in range(nt):
        k = lax.rem(zi - j + nt, nt)
        dos[pl.ds(pl.multiple_of(k * n, n), n), :] = do_refs[j][0]
    q_t[...] = q_ref[0, :rows, :].T
    do_t[...] = dos[...].T

    @pl.when(t == 0)
    def _():
        near[...] = jnp.zeros(near.shape, F32)
        far[...] = jnp.zeros(far.shape, F32)

    def one(s, carry):
        line = chain(par_ref, t, ctx * local_segs + s, levels, all_segs, local_segs, ctx)
        for lev, (_, part, block) in enumerate(line):
            start = pl.ds(pl.multiple_of(block * seg, seg), seg)
            at = slice(lev * seg, (lev + 1) * seg)
            kw[at, :] = kall[part, start, :]
            vw[at, :] = vall[part, start, :]
            kw_t[:, at] = kall_t[part, :, start]
        at = pl.ds(pl.multiple_of(s * seg, seg), seg)
        turned, do_turned = q_t[:, at], do_t[:, at]
        lse = lse_ref[0, 0, 0:1, at]
        delta = None
        for c in range(blocks):
            cut = slice(c * seg, (c + 1) * seg)
            raw = mm(kw[cut, :], turned) * factor
            if c < levels:
                raw = window_score(raw, c, bm, line, len_ref[t, s], seg)
            prob = jnp.exp(raw - lse)
            dprob = mm(vw[cut, :], do_turned)
            raws[cut, :] = prob
            dps[cut, :] = dprob
            pbs[cut, :] = prob.astype(BF)
            part = fold(prob * dprob, jnp.add)
            delta = part if delta is None else delta + part
        delta = jnp.sum(delta, axis=0, keepdims=True)
        for c in range(blocks):
            cut = slice(c * seg, (c + 1) * seg)
            dscore = (raws[cut, :] * (dps[cut, :] - delta)).astype(BF)
            dss[cut, :] = dscore
            if c < 2:
                near[cut, :] += dscore.astype(F32)
            elif c < levels:
                far[...] += dscore.astype(F32)
        dq = mm(kw_t[...], dss[...]) * factor
        dq_ref[0, at, :] = dq.T.astype(BF)
        q, do = q_ref[0, at, :], dos[at, :]
        for c in range(blocks):
            cut = slice(c * seg, (c + 1) * seg)
            gk = mm(dss[cut, :], q) * factor
            gv = mm(pbs[cut, :], do)
            if c < levels:
                _, part, block = line[c]
                to = pl.ds(pl.multiple_of(block * seg, seg), seg)
                dk[part, to, :] += gk
                dv[part, to, :] += gv
            else:
                for i in range(0, seg, each):
                    b = ((c - levels) * seg + i) // each
                    dk[b, rows:, :] += gk[i : i + each]
                    dv[b, rows:, :] += gv[i : i + each]
        return carry

    lax.fori_loop(0, local_segs, one, 0)
    for ref, pair in ((near_ref, (0, 2)), (far_ref, (1, 3))):
        for place, b in enumerate(pair):
            ref[place, 0, 0] = dk[b].astype(BF)
            ref[place, 1, 0] = dv[b].astype(BF)
    for j in range(nt):
        k = lax.rem(zi - j + nt, nt)
        dq_refs[j][0] = dq_ref[0, pl.ds(pl.multiple_of(k * n, n), n), :]

    @pl.when(t == pl.num_programs(1) - 1)
    def _():
        key = lax.broadcasted_iota(jnp.int32, (seg, seg), 0)
        query = lax.broadcasted_iota(jnp.int32, (seg, seg), 1)
        edges = [-(10**6)] + list(EDGES) + [10**6]
        for b in range(BUCKETS):
            total = far[...] if b == BUCKETS - 1 else jnp.zeros((seg, seg), F32)
            for lev in range(2):
                dist = lev * seg + query - key
                inside = (dist >= edges[b]) & (dist < edges[b + 1])
                total = total + jnp.where(inside, near[lev * seg : (lev + 1) * seg, :], 0.0)
            db_ref[0, b : b + 1, :] = jnp.sum(total, axis=0, keepdims=True)


def hbm_call(prefetch, body, out_shape, keep=False, **kw):
    if not keep:
        return pl.pallas_call(body, out_shape=out_shape, **kw)
    several = isinstance(out_shape, tuple)
    outs = tuple(
        pltpu.HBM(o.shape, o.dtype) for o in (out_shape if several else (out_shape,))
    )
    kernel = pl.pallas_call(body, out_shape=outs if several else outs[0], **kw)

    def run(*args):
        rest = [pltpu.with_memory_space_constraint(a, pltpu.HBM) for a in args[prefetch:]]
        return kernel(*args[:prefetch], *rest)

    return run


def attention_calls(trees, heads, local_segs, all_segs, seg, each, head_dim, nt):
    levels = WINDOW // seg + 1
    rows = local_segs * seg
    tall = rows + each
    win = levels * seg
    wide = win + 4 * each
    factor = head_dim ** (-0.5)
    dims = (levels, seg, local_segs, all_segs, factor, nt)
    assert EDGES[-1] <= 2 * seg - (seg - 1)
    assert seg == head_dim == 128 and wide % seg == 0 and seg % each == 0
    vm = lambda dt, *shape: pltpu.VMEM(shape, dt)
    forward_scratch = [
        vm(BF, 4, rows, head_dim),
        vm(BF, 4, head_dim, rows),
        vm(BF, 2, wide, head_dim),
        vm(BF, 2, head_dim, wide),
        vm(F32, win, seg),
        vm(BF, rows, head_dim),
        vm(BF, head_dim, rows),
        vm(F32, 2, wide, seg),
        vm(BF, 2, wide, seg),
    ]
    backward_scratch = [
        vm(BF, 4, rows, head_dim),
        vm(BF, 4, rows, head_dim),
        vm(BF, 4, head_dim, rows),
        vm(BF, wide, head_dim),
        vm(BF, wide, head_dim),
        vm(BF, head_dim, wide),
        vm(F32, win, seg),
        vm(F32, 4, tall, head_dim),
        vm(F32, 4, tall, head_dim),
        vm(F32, 2 * seg, seg),
        vm(F32, seg, seg),
        vm(BF, rows, head_dim),
        vm(BF, head_dim, rows),
        vm(BF, head_dim, rows),
        vm(F32, wide, seg),
        vm(F32, wide, seg),
        vm(BF, wide, seg),
        vm(BF, wide, seg),
    ]
    lse_shape = jax.ShapeDtypeStruct((trees, heads, 8, rows), F32)

    def specs(order):
        def at(col):
            return pl.BlockSpec(
                (1, tall, head_dim), lambda a, b, *_: (order(a, b)[0], 0, col(order(a, b)[1]))
            )

        k, v = at(lambda h: h), at(lambda h: heads + h)
        return [k, k, k, k, k, v, v, v, v]

    th = lambda a, b: (a, b)
    ht = lambda a, b: (b, a)
    chunk_shape = jax.ShapeDtypeStruct((trees, rows // nt, heads * head_dim), BF)

    def chunk_spec(order):
        return pl.BlockSpec(
            (1, rows // nt, head_dim), lambda a, b, *_: (order(a, b)[0], 0, order(a, b)[1])
        )

    forward = hbm_call(
        4,
        functools.partial(attend_kernel, dims),
        out_shape=(chunk_shape,) * nt + (lse_shape,),
        grid_spec=pltpu.PrefetchScalarGridSpec(
            num_scalar_prefetch=4,
            grid=(trees, heads),
            in_specs=specs(th),
            out_specs=(chunk_spec(th),) * nt
            + (pl.BlockSpec((1, 1, 8, rows), lambda t, h, *_: (t, h, 0, 0)),),
            scratch_shapes=forward_scratch,
        ),
        compiler_params=pltpu.CompilerParams(vmem_limit_bytes=24 << 20),
        cost_estimate=cost(16),
        keep=True,
        name="attend",
    )
    pair = jax.ShapeDtypeStruct((2, 2, trees, tall, heads * head_dim), BF)
    pair_spec = pl.BlockSpec((2, 2, 1, tall, head_dim), lambda h, t, *_: (0, 0, t, 0, h))
    backward = hbm_call(
        4,
        functools.partial(attend_back_kernel, dims),
        out_shape=(chunk_shape,) * nt
        + (
            jax.ShapeDtypeStruct((trees, rows, heads * head_dim), BF),
            pair,
            pair,
            jax.ShapeDtypeStruct((heads, BUCKETS, 128), F32),
        ),
        grid_spec=pltpu.PrefetchScalarGridSpec(
            num_scalar_prefetch=4,
            grid=(heads, trees),
            in_specs=specs(ht)
            + [chunk_spec(ht)] * nt
            + [pl.BlockSpec((1, 1, 8, rows), lambda h, t, *_: (t, h, 0, 0))],
            out_specs=(chunk_spec(ht),) * nt
            + (
                pl.BlockSpec((1, rows, head_dim), lambda h, t, *_: (t, 0, h)),
                pair_spec,
                pair_spec,
                pl.BlockSpec((1, BUCKETS, 128), lambda h, t, *_: (h, 0, 0)),
            ),
            scratch_shapes=backward_scratch,
        ),
        compiler_params=pltpu.CompilerParams(vmem_limit_bytes=32 << 20),
        cost_estimate=cost(24),
        keep=True,
        name="attend_back",
    )
    return forward, backward


def norm_stats(values):
    mean = jnp.mean(values, axis=-1, keepdims=True)
    centered = values - mean
    scale = lax.rsqrt(jnp.mean(centered * centered, axis=-1, keepdims=True) + EPSILON)
    return centered * scale, scale


def norm_back(grad, xhat, scale, gain):
    scaled = grad * gain
    first = jnp.mean(scaled, axis=-1, keepdims=True)
    second = jnp.mean(scaled * xhat, axis=-1, keepdims=True)
    return scale * (scaled - first - xhat * second)


def gelu_parts(u):
    square = u * u
    th = jnp.tanh(u * (GELU_C + GELU_C * GELU_A * square))
    half = 0.5 * (1.0 + th)
    slope = half + (0.5 * u) * (1.0 - th * th) * (GELU_C + 3.0 * GELU_C * GELU_A * square)
    return u * half, slope


def norm_kernel(gain, shift, tok, st, out):
    each = st.shape[1]
    rows = tok.shape[1]
    for lo in range(0, rows + each, each):
        x = (tok[0, lo : lo + each, :] if lo < rows else st[0]).astype(F32)
        xhat, _ = norm_stats(x)
        out[0, lo : lo + each, :] = (xhat * gain[...] + shift[...]).astype(BF)


def project_kernel(pos, x, *refs):
    if len(refs) == 3:
        w = refs[0]
        q_ref, kv_ref = refs[1:]
    else:
        wq, wk, wv, near, over, q_ref, kv_ref, w = refs

        @pl.when((pl.program_id(0) == 0) & (pl.program_id(1) == 0))
        def _():
            fi, core = pos[2], pos[0] & 1
            depth, cols = wq.shape
            half = depth // 2
            for i, part in enumerate((wq, wk, wv)):
                w[pl.ds(pl.multiple_of(fi * depth, depth), depth), i * cols : (i + 1) * cols] = (
                    part[...]
                )
            base = (1 - fi) * depth
            w[pl.ds(pl.multiple_of(base + core * half, half), half), :] = near[...]
            w[pl.ds(pl.multiple_of(base + (1 - core) * half, half), half), :] = over[...]

    y = mm(x[0], w[...]).astype(BF)
    cols = q_ref.shape[2]
    q_ref[0] = y[:, :cols]
    kv_ref[0] = y[:, cols:]


def load_projection(pos, blocks, w):
    rows, depth = blocks[0].shape
    n = w.shape[0] // rows
    for j in range(n):
        at = slice(j * rows, (j + 1) * rows)
        if n == len(blocks):
            w[at, :] = blocks[j][...]
        else:
            fi = pos[2]
            w[at, pl.ds(pl.multiple_of(fi * depth, depth), depth)] = blocks[j][...]
            w[at, pl.ds(pl.multiple_of((1 - fi) * depth, depth), depth)] = blocks[n][j]


def mix_kernel(n, pos, *refs):
    att, blocks = refs[:n], refs[n:-10]
    tok, cell, gain, shift, hid_ref, n2_ref, stat_ref, w, left, branch = refs[-10:]

    load_projection(pos, blocks, w)
    stat_ref[...] = jnp.zeros(stat_ref.shape, F32)
    cols = att[0].shape[2]
    shape = tok.shape
    mine = shape[0] * shape[1]
    for j in range(n):
        left[:, j * cols : (j + 1) * cols] = att[j][...].reshape(mine, cols)
    branch[...] = mm(left[...], w[...])
    x = tok[...].astype(F32).reshape(mine, shape[2])
    gated = cell[...] * branch[...]
    hidden = x + gated
    hid_ref[...] = hidden.reshape(shape)
    xhat, _ = norm_stats(hidden)
    n2_ref[...] = (xhat * gain[...] + shift[...]).astype(BF).reshape(shape)
    stat_ref[0:1, :] = jnp.sum(x * x, axis=0, keepdims=True)
    stat_ref[1:2, :] = jnp.sum(gated * gated, axis=0, keepdims=True)


def ff_kernel(*refs):
    xs, gs = refs[0:2], refs[2:4]
    pack, first_ref, second_ref, act_ref, gup_ref, acc, xall, gall = refs[4:]
    nf, depth = pack.shape[1], pack.shape[3]
    z = pl.program_id(0)
    mine = xs[0].shape[0]
    cut = [slice(f * depth, (f + 1) * depth) for f in range(nf)]

    @pl.when(z == 0)
    def _():
        for p in range(2):
            xall[p] = xs[p][...]
            gall[p] = gs[p][...]
        acc[...] = jnp.zeros(acc.shape, F32)

    def one(p, carry):
        up = mm(xall[p, :, cut[0]], pack[0, 0, 0])
        back = mm(gall[p, :, cut[0]], pack[0, 0, 1])
        for f in range(1, nf):
            up = up + mm(xall[p, :, cut[f]], pack[0, f, 0])
            back = back + mm(gall[p, :, cut[f]], pack[0, f, 1])
        value, slope = gelu_parts(up)
        act_ref[p] = value.astype(BF)
        gup = (back * slope).astype(BF)
        gup_ref[p] = gup
        for f in range(nf):
            acc[p, :, cut[f]] += mm_nt(gup, pack[0, f, 0])
        return carry

    lax.fori_loop(0, 2, one, 0)

    @pl.when(z == pl.num_programs(0) - 1)
    def _():
        first_ref[...] = acc[0].astype(BF)
        second_ref[...] = acc[1].astype(BF)


def ff_grad_kernel(*refs):
    xs, gs = refs[0:4], refs[4:8]
    act_a, gup_a, act_b, gup_b, pack = refs[8:13]
    sent_ref, near_ref, far_ref, rows, acc, wout, units = refs[13:]
    _, nf, _, depth, fc = pack.shape
    mine = xs[0].shape[0]

    @pl.when(pl.program_id(0) == 0)
    def _():
        for p in range(4):
            rows[0, p * mine : (p + 1) * mine, :] = xs[p][...]
            rows[1, p * mine : (p + 1) * mine, :] = gs[p][...]
        acc[...] = jnp.zeros(acc.shape, F32)

    for f in range(nf):
        wout[f * depth : (f + 1) * depth, :] = pack[0, f, 1]
    for half, (a_ref, u_ref) in enumerate(((act_a, gup_a), (act_b, gup_b))):
        for p in range(2):
            at = slice((2 * half + p) * mine, (2 * half + p + 1) * mine)
            units[1, at, :] = a_ref[p]
            units[0, at, :] = u_ref[p]

    acc[...] += mm_nt(units[1], wout[...])

    def grads(i, carry):
        part = mm_tn(rows[i], units[i])
        for f in range(nf):
            sent_ref[f, 0, i] = part[f * depth : (f + 1) * depth].astype(BF)
        return carry

    lax.fori_loop(0, 2, grads, 0)

    @pl.when(pl.program_id(0) == pl.num_programs(0) - 1)
    def _():
        for i, ref in enumerate((near_ref, far_ref)):
            for p in range(2):
                lo = (2 * p + i) * mine
                ref[p] = acc[lo : lo + mine, :].astype(BF)


def branch_back_kernel(nt, pos, *refs):
    blocks, (own, got, far, hid, cot, cell, gain) = refs[: -(nt + 11)], refs[-(nt + 11) : -(nt + 4)]
    gh_ref, gb_ref = refs[-(nt + 4) : -(nt + 2)]
    ga_refs, stat_ref, w = refs[-(nt + 2) : -2], refs[-2], refs[-1]

    load_projection(pos, blocks, w)
    stat_ref[...] = jnp.zeros(stat_ref.shape, F32)
    shape = cot.shape
    mine = shape[0] * shape[1]
    flat = lambda v: v.astype(F32).reshape(mine, shape[2])
    grad = flat(own[...]) + flat(got[...]) + flat(far[...])
    xhat, scale = norm_stats(flat(hid[...]))
    gh = flat(cot[...]) + norm_back(grad, xhat, scale, gain[...])
    gh_ref[...] = gh.reshape(shape)
    gb = (cell[...] * gh).astype(BF)
    gb_ref[...] = gb.reshape(shape)
    cols = ga_refs[0].shape[2]
    for j, ref in enumerate(ga_refs):
        ref[...] = mm_nt(gb, w[j * cols : (j + 1) * cols, :]).astype(BF).reshape(ref.shape)
    stat_ref[0:1, :] = jnp.sum(grad * xhat, axis=0, keepdims=True)
    stat_ref[1:2, :] = jnp.sum(grad, axis=0, keepdims=True)


def combine_kernel(rows, pos, own, got, far, *refs):
    nt = (len(refs) - 1) // 2
    dq, total_ref, send = refs[:nt], refs[nt], refs[nt + 1 :]
    total = (
        own[0, 0, 0].astype(F32) + got[0, 0, 0].astype(F32) + far[0, 0].astype(F32)
    ).astype(BF)
    total_ref[0, 0] = total
    n = rows // nt
    m = (total_ref.shape[2] - rows) // nt
    kv = pl.program_id(1)
    for j in range(nt):
        k = lax.rem(pos[1] - j + nt, nt)

        @pl.when(kv == 0)
        def _():
            send[j][0, 0, :n, :] = dq[j][0]
            send[j][0, 0, n:, :] = jnp.zeros((m, dq[j].shape[2]), BF)

        send[j][1 + kv, 0, :n, :] = total_ref[0, 0, pl.ds(pl.multiple_of(k * n, n), n), :]
        send[j][1 + kv, 0, n:, :] = total_ref[0, 0, pl.ds(pl.multiple_of(rows + k * m, m), m), :]


def input_back_kernel(nt, pos, *refs):
    blocks = refs[:nt]
    parts, (tok, st, gh, gain, out_ref, stat_ref, w, left, every) = (
        refs[nt : nt + 4],
        refs[nt + 4 :],
    )
    m = parts[0].shape[1]
    nf = parts[0].shape[0] // nt
    cols = blocks[0].shape[3]
    trees, n = tok.shape[0], tok.shape[1]
    tall = blocks[0].shape[2]
    for flip, part in zip((0, 2, 1, 3), parts):

        def put(i, carry, flip=flip, part=part):
            z = lax.div(i, nf)
            at = ((i - z * nf) * 4 + jnp.bitwise_xor(pos[0], flip)) * m
            w[z, pl.ds(pl.multiple_of(at, m), m), :] = part[i]
            return carry

        lax.fori_loop(0, nt * nf, put, 0)
    for j in range(nt):
        for i in range(3):
            left[j, :, i * cols : (i + 1) * cols] = blocks[j][i].reshape(trees * tall, cols)
    step = 256

    def one(i, carry):
        at = pl.ds(pl.multiple_of(i * step, step), step)
        total = mm_nt(left[0], w[pos[1], at, :])
        for j in range(1, nt):
            total = total + mm_nt(left[j], w[lax.rem(pos[1] + j, nt), at, :])
        every[:, at] = total
        return carry

    lax.fori_loop(0, every.shape[1] // step, one, 0)
    stat_ref[...] = jnp.zeros(stat_ref.shape, F32)
    for t in range(trees):
        for x_ref, lo, hi, extra in ((tok, 0, n, gh), (st, n, tall, None)):
            grad = every[t * tall + lo : t * tall + hi, :]
            xhat, scale = norm_stats(x_ref[t].astype(F32))
            back = norm_back(grad, xhat, scale, gain[...])
            if extra is not None:
                back = back + extra[t]
            out_ref[t, lo:hi, :] = back.astype(BF)
            stat_ref[0:1, :] += jnp.sum(grad * xhat, axis=0, keepdims=True)
            stat_ref[1:2, :] += jnp.sum(grad, axis=0, keepdims=True)


def attn_grad_kernel(nt, pos, *refs):
    blocks, grad = refs[:nt], refs[nt]
    far_ref, mid_ref, own_ref, acc, left = refs[nt + 1 :]
    n = own_ref.shape[1]
    rows = grad.shape[0] * grad.shape[1]
    for j in range(nt):
        left[j] = blocks[j][...].reshape(rows, acc.shape[0])

    def one(j, carry):
        acc[...] = mm_tn(left[j], grad[...].reshape(rows, grad.shape[2]))
        for flip, ref in ((0, own_ref), (2, mid_ref), (1, far_ref), (3, far_ref)):
            k = jnp.bitwise_xor(pos[0], flip)
            piece = acc[pl.ds(pl.multiple_of(k * n, n), n), :]
            if flip & 1:
                ref[flip // 2, j] = piece.astype(BF)
            else:
                ref[j] = piece
        return carry

    lax.fori_loop(0, nt, one, 0)


def qkv_grad_kernel(nf, pos, x, gq, gkv, far_ref, mid_ref, own_ref, acc, right):
    t = pl.program_id(0)
    rows, cols = gq.shape[1], gq.shape[2]
    tall = x.shape[1]
    right[:rows, :cols] = gq[0]
    right[rows:, :cols] = jnp.zeros((tall - rows, cols), BF)
    right[:, cols : 2 * cols] = gkv[0, 0]
    right[:, 2 * cols :] = gkv[1, 0]

    @pl.when(t == 0)
    def _():
        acc[...] = jnp.zeros(acc.shape, F32)

    def one(i, carry):
        at = pl.ds(pl.multiple_of(i * cols, cols), cols)
        acc[:, at] += mm_tn(x[0], right[:, at])
        return carry

    lax.fori_loop(0, 3, one, 0)

    @pl.when(t == pl.num_programs(0) - 1)
    def _():
        n = own_ref.shape[1]
        for f in range(nf):
            for flip, ref in ((0, own_ref), (2, mid_ref), (1, far_ref), (3, far_ref)):
                k = jnp.bitwise_xor(pos[0], flip)
                start = pl.multiple_of(f * (acc.shape[0] // nf) + k * n, n)
                piece = acc[pl.ds(start, n), :]
                if flip & 1:
                    ref[flip // 2, f] = piece.astype(BF)
                else:
                    ref[f] = piece


def order_kernel(sizes, places, *refs):
    outs = refs[-len(sizes) :]
    for i, block in enumerate(refs[: -len(sizes)]):
        lo = 0
        for n, out in zip(sizes, outs):
            out[0, pl.ds(pl.multiple_of(places[i] * n, n), n), :] = block[0, lo : lo + n, :]
            lo = lo + n


def finish_ff_kernel(pos, *refs):
    gin, gout = refs[4:]
    depth, fc = gin.shape[0], refs[0].shape[1]
    for flip, b in zip((0, 2, 1, 3), refs[:4]):
        k = jnp.bitwise_xor(pos[0], flip)
        at = pl.ds(pl.multiple_of(k * fc, fc), fc)
        gin[:, at] = b[:depth, :].astype(F32)
        gout[at, :] = b[depth:, :].astype(F32).T


def finish_qkv_kernel(pos, *refs):
    for flip, b in zip((0, 2, 1, 3), refs[:4]):
        n = b.shape[0]
        k = jnp.bitwise_xor(pos[0], flip)
        at = pl.ds(pl.multiple_of(k * n, n), n)
        cols = refs[4].shape[1]
        for i, out in enumerate(refs[4:7]):
            out[at, :] = b[:, i * cols : (i + 1) * cols].astype(F32)
        for out in refs[7:]:
            m = n * (b.shape[1] - 3 * cols) // out.shape[1]
            wide = b.shape[1] - 3 * cols
            at = pl.ds(pl.multiple_of(k * m, m), m)
            for i in range(n // m):
                out[at, i * wide : (i + 1) * wide] = b[
                    i * m : (i + 1) * m, 3 * cols :
                ].astype(F32)


def build(mesh):
    nf, nc, nt = mesh.shape["fsdp"], mesh.shape["context"], mesh.shape["tensor"]
    assert nc == 4

    def px(x):
        return lax.ppermute(x, "fsdp", [(0, 1), (1, 0)])

    def pc(x, k):
        return lax.ppermute(x, "context", [(a, a ^ k) for a in range(nc)])

    def pz(x, j):
        return lax.ppermute(x, "tensor", [(a, (a - j) % nt) for a in range(nt)])

    def ps(x, j):
        return lax.ppermute(x, "tensor", [(a, (a + j) % nt) for a in range(nt)])

    def on_device(
        tokens,
        state,
        parent,
        seg_length,
        cell_gate,
        norm1_gain,
        norm1_shift,
        w_query,
        w_key,
        w_value,
        w_attn_out,
        rel_bias,
        norm2_gain,
        norm2_shift,
        w_in,
        w_out,
        cotangent,
    ):
        trees, rows, width = tokens.shape
        local_segs = seg_length.shape[1]
        seg = rows // local_segs
        all_segs = parent.shape[1]
        heads = rel_bias.shape[0]
        depth, cols = w_query.shape
        head_dim = cols // heads
        each = state.shape[1]
        tall = rows + each
        fi, ci, zi = lax.axis_index("fsdp"), lax.axis_index("context"), lax.axis_index("tensor")
        core = ci & 1
        zr, zs = rows // nt, each // nt
        mine = trees * zr
        pos = jnp.stack([ci, zi, fi]).astype(jnp.int32)
        cell, gain_1, shift_1, gain_2, shift_2 = (
            v.reshape(1, width)
            for v in (cell_gate, norm1_gain, norm1_shift, norm2_gain, norm2_shift)
        )
        sds = jax.ShapeDtypeStruct

        def gate(*xs):
            return lax.optimization_barrier(xs)

        stat = sds((8, width), F32)

        def call(body, grid, ins, outs, out_shape, scratch=(), prefetch=1, vmem=24, name="", us=4, keep=False):
            return hbm_call(
                prefetch,
                body,
                out_shape=out_shape,
                grid_spec=pltpu.PrefetchScalarGridSpec(
                    num_scalar_prefetch=prefetch,
                    grid=grid,
                    in_specs=ins,
                    out_specs=outs,
                    scratch_shapes=scratch,
                ),
                compiler_params=pltpu.CompilerParams(vmem_limit_bytes=vmem << 20),
                cost_estimate=cost(us),
                keep=keep,
                name=name,
            )

        def whole(shape):
            return pl.BlockSpec(shape, lambda *_: (0,) * len(shape))

        row_1 = whole((1, width))
        stat_spec = whole((8, width))

        def place(blocks, starts, axis, total):
            shape = list(blocks[0].shape)
            shape[axis] = total
            out = jnp.zeros(shape, blocks[0].dtype)
            for block, start in zip(blocks, starts):
                out = lax.dynamic_update_slice_in_dim(out, block, start, axis)
            return out

        def half_of(x, k, axis, parts):
            n = x.shape[axis] // parts
            return lax.dynamic_slice_in_dim(x, k * n, n, axis)

        def gather_f(x, axis):
            n = x.shape[axis]
            if nf == 2:
                return place([x, px(x)], [fi * n, (1 - fi) * n], axis, 2 * n)
            return lax.all_gather(x, "fsdp", axis=axis, tiled=True)

        def scatter_f(x, axis):
            if nf == 2:
                sent = half_of(x, 1 - fi, axis, 2).astype(BF)
                return half_of(x, fi, axis, 2) + px(sent).astype(F32)
            return lax.psum_scatter(
                x.astype(BF), "fsdp", scatter_dimension=axis, tiled=True
            ).astype(F32)

        def gather_c(x, axis):
            n = x.shape[axis]
            pair = jnp.stack([x, pc(x, 2)])
            over = pc(pair, 1)
            return place(
                [x, pair[1], over[0], over[1]],
                [ci * n, (ci ^ 2) * n, (ci ^ 1) * n, (ci ^ 3) * n],
                axis,
                nc * n,
            )

        def scatter_c(x, axis):
            cut = lambda k: half_of(x, k, axis, nc)
            sent = jnp.stack([cut(ci ^ 1), cut(ci ^ 3)]).astype(BF)
            got = pc(sent, 1).astype(F32)
            far = (cut(ci ^ 2) + got[1]).astype(BF)
            return cut(ci) + got[0] + pc(far, 2).astype(F32)

        if nf == 2:
            half = depth // 2
            near_send = jnp.concatenate(
                [half_of(w, core, 0, 2) for w in (w_query, w_key, w_value)], axis=1
            )
            near_send, w_in, w_out = gate(near_send, w_in, w_out)
            near_w = px(near_send)
            near_w, w_attn_out = gate(near_w, w_attn_out)
            over_w = pc(near_w, 1)
            weights = (w_query, w_key, w_value, near_w, over_w)
            weight_specs = [whole((depth, cols))] * 3 + [whole((half, 3 * cols))] * 2
            w_scratch = [pltpu.VMEM((2 * depth, 3 * cols), BF)]
        else:
            full_w = lax.all_gather(
                jnp.concatenate([w_query, w_key, w_value], axis=1), "fsdp", axis=0, tiled=True
            )
            weights = (full_w,)
            weight_specs = [whole(full_w.shape)]
            w_scratch = []

        fc = w_in.shape[1] // nc
        pack = jnp.stack([half_of(w_in, ci, 1, nc), half_of(w_out, ci, 0, nc).T])
        packs = lax.all_gather(pack, ("tensor", "fsdp"), axis=0, tiled=False)
        packs = packs.reshape(nt, nf, 2, depth, fc)

        o_blocks = [w_attn_out] + [pz(w_attn_out, j) for j in range(1, nt)]
        o_over = []

        normed = call(
            norm_kernel,
            (trees,),
            [
                row_1,
                row_1,
                pl.BlockSpec((1, rows, width), lambda t: (t, 0, 0)),
                pl.BlockSpec((1, each, width), lambda t: (t, 0, 0)),
            ],
            pl.BlockSpec((1, tall, width), lambda t: (t, 0, 0)),
            sds((trees, tall, width), BF),
            prefetch=0,
            name="norm",
            us=5,
        )(gain_1, shift_1, tokens, state)
        tile = tall // 3
        queries, kv = call(
            project_kernel,
            (trees, 3),
            [pl.BlockSpec((1, tile, width), lambda t, i, *_: (t, i, 0))] + weight_specs,
            (
                pl.BlockSpec((1, tile, cols), lambda t, i, *_: (t, i, 0)),
                pl.BlockSpec((1, tile, 2 * cols), lambda t, i, *_: (t, i, 0)),
            ),
            (sds((trees, tall, cols), BF), sds((trees, tall, 2 * cols), BF)),
            w_scratch,
            name="project",
        )(pos, normed, *weights)
        kv_y = pc(kv, 2)
        kv_c = pc(kv, 1)
        grad_low = half_of(cotangent, zi, 1, nt).reshape(mine, width)
        kv_y, grad_low, *o_blocks = gate(kv_y, grad_low, *o_blocks)
        kv_cy = pc(kv_y, 1)
        if nf == 2:
            o_over = [px(jnp.stack(o_blocks))]
        else:
            full = lax.all_gather(jnp.stack(o_blocks), "fsdp", axis=2, tiled=True)
            o_blocks = [full[j] for j in range(nt)]
        grad_y = pc(grad_low, 2)
        grad_c = pc(grad_low, 1)

        forward, backward = attention_calls(
            trees, heads, local_segs, all_segs, seg, each, head_dim, nt
        )
        tables = (parent, seg_length, pos, rel_bias)
        sources = (queries, kv, kv_c, kv_y, kv_cy, kv, kv_c, kv_y, kv_cy)
        *att_send, log_total = forward(*tables, *sources)
        quarter = jnp.concatenate(
            [half_of(w, ci, 0, nc) for w in (w_query, w_key, w_value)], axis=1
        )
        att_send[0], quarter = gate(att_send[0], quarter)
        all_q = lax.all_gather(quarter, ("tensor", "fsdp"), axis=0, tiled=False)

        att = [att_send[0]] + [pz(att_send[j], j) for j in range(1, nt)]
        att[1], grad_y, *o_over = gate(att[1], grad_y, *o_over)
        grad_rows = [grad_low, grad_y, grad_c, pc(grad_y, 1)]
        chunk = whole((trees, zr, width))
        chunk_z = pl.BlockSpec((trees, zr, width), lambda i, pos: (0, pos[1], 0))
        small = whole((trees, zr, cols))
        o_all = tuple(o_blocks) + tuple(o_over)
        o_specs = [whole(o.shape) for o in o_all]
        o_scratch = [pltpu.VMEM((nt * cols, width), BF)]
        hidden, normed_two, stat_a = call(
            functools.partial(mix_kernel, nt),
            (1,),
            [small] * nt + o_specs + [chunk_z, row_1, row_1, row_1],
            (chunk, chunk, stat_spec),
            (sds((trees, zr, width), F32), sds((trees, zr, width), BF), stat),
            o_scratch
            + [pltpu.VMEM((mine, nt * cols), BF), pltpu.VMEM((mine, width), F32)],
            name="mix",
            keep=True,
        )(pos, *att, *o_all, tokens, cell, gain_2, shift_2)

        rows_two = normed_two.reshape(mine, width)
        rows_y = pc(rows_two, 2)
        rows_c = pc(rows_two, 1)
        block = whole((mine, width))
        units = nt * fc
        half_spec = whole((2, mine, width))
        half_sds, full_sds = sds((2, mine, width), BF), sds((2, mine, units), BF)
        unit_spec = pl.BlockSpec((2, mine, fc), lambda z, *_: (0, 0, z))
        pack_spec = pl.BlockSpec((1,) + packs.shape[1:], lambda z, *_: (z, 0, 0, 0, 0))
        feed = call(
            ff_kernel,
            (nt,),
            [block] * 4 + [pack_spec],
            (block, block, unit_spec, unit_spec),
            (sds((mine, width), BF), sds((mine, width), BF), full_sds, full_sds),
            [pltpu.VMEM((2, mine, width), F32)] + [pltpu.VMEM((2, mine, width), BF)] * 2,
            prefetch=0,
            vmem=32,
            name="feed",
            keep=True,
            us=9,
        )
        gn_own, gn_c, act_a, gup_a = feed(rows_two, rows_c, grad_rows[0], grad_rows[2], packs)
        rows_y, gn_own, gn_c = gate(rows_y, gn_own, gn_c)
        rows_cy = pc(rows_y, 1)
        gn_got = [pc(gn_c, 1)]
        gn_y, gn_cy, act_b, gup_b = feed(rows_y, rows_cy, grad_rows[1], grad_rows[3], packs)
        ff_rows = [rows_two, rows_c, rows_y, rows_cy]
        cot_rows = [grad_rows[0], grad_rows[2], grad_rows[1], grad_rows[3]]
        gn_got.append(pc(gn_cy, 1))
        gn_mid = (gn_y.astype(F32) + gn_got[1].astype(F32)).astype(BF)
        gn_mid, gn_got[0], act_b, gup_b = gate(gn_mid, gn_got[0], act_b, gup_b)
        gn_end = pc(gn_mid, 2)
        ff_sent, ff_near, ff_far = call(
            ff_grad_kernel,
            (nt,),
            [block] * 8 + [unit_spec] * 4 + [pack_spec],
            (
                pl.BlockSpec((nf, 1, 2, depth, fc), lambda z, *_: (0, z, 0, 0, 0)),
                half_spec,
                half_spec,
            ),
            (sds((nf, nt, 2, depth, fc), BF), half_sds, half_sds),
            [
                pltpu.VMEM((2, 4 * mine, width), BF),
                pltpu.VMEM((4 * mine, width), F32),
                pltpu.VMEM((width, fc), BF),
                pltpu.VMEM((2, 4 * mine, fc), BF),
            ],
            prefetch=0,
            vmem=56,
            name="feed_grads",
            keep=True,
            us=16,
        )(*ff_rows, *cot_rows, act_a, gup_a, act_b, gup_b, packs)
        gn_end, ff_sent, ff_near, ff_far, all_q = gate(gn_end, ff_sent, ff_near, ff_far, all_q)
        ff_got = pc(ff_far, 1)

        grad_hidden, grad_branch, *rest = call(
            functools.partial(branch_back_kernel, nt),
            (1,),
            o_specs + [chunk] * 4 + [chunk_z, row_1, row_1],
            (chunk, chunk) + (small,) * nt + (stat_spec,),
            (sds((trees, zr, width), F32), sds((trees, zr, width), BF))
            + (sds((trees, zr, cols), BF),) * nt
            + (stat,),
            o_scratch,
            name="branch_back",
            keep=True,
        )(
            pos,
            *o_all,
            gn_own.reshape(trees, zr, width),
            gn_got[0].reshape(trees, zr, width),
            gn_end.reshape(trees, zr, width),
            hidden,
            cotangent,
            cell,
            gain_2,
        )
        stat_b = rest.pop()
        ff_got, grad_branch, *rest = gate(ff_got, grad_branch, *rest)
        all_q, rest[0] = gate(all_q, rest[0])
        all_y = pc(all_q, 2)
        grad_heads = [rest[0]] + [ps(rest[j], j) for j in range(1, nt)]
        ff_mid = (ff_near[1].astype(F32) + ff_got[1].astype(F32)).astype(BF)
        ff_end = pc(ff_mid, 2)
        o_rows = cols // nc
        att_specs = (whole((2, nt, o_rows, width)),) + (whole((nt, o_rows, width)),) * 2
        attn_far, attn_mid, attn_near = call(
            functools.partial(attn_grad_kernel, nt),
            (1,),
            [whole((trees, zr, cols))] * nt + [whole((trees, zr, width))],
            att_specs,
            (
                sds((2, nt, o_rows, width), BF),
                sds((nt, o_rows, width), F32),
                sds((nt, o_rows, width), F32),
            ),
            [pltpu.VMEM((cols, width), F32), pltpu.VMEM((nt, mine, cols), BF)],
            name="attn_grads",
            us=4,
        )(pos, *att, grad_branch)

        mlp_out = ff_near[0].astype(F32) + ff_got[0].astype(F32) + ff_end.astype(F32)
        result = (hidden.reshape(mine, width) + mlp_out).astype(BF)
        result, attn_near, attn_mid, attn_far, *grad_heads = gate(
            result, attn_near, attn_mid, attn_far, *grad_heads
        )
        result = result.reshape(trees, zr, width)

        def spread_near(x):
            if nt == 4:
                return [
                    lax.ppermute(x, "tensor", [(0, 1), (1, 2), (2, 3)]),
                    lax.ppermute(x, "tensor", [(1, 0), (2, 1), (3, 2)]),
                ]
            return [pz(x, 1), pz(x, nt - 1)]

        def ordered(blocks, places, sizes):
            n = blocks[0].shape[1]
            return call(
                functools.partial(order_kernel, sizes),
                (trees,),
                [pl.BlockSpec((1, n, width), lambda t, *_: (t, 0, 0))] * len(blocks),
                tuple(
                    pl.BlockSpec((1, nt * m, width), lambda t, *_: (t, 0, 0)) for m in sizes
                ),
                tuple(sds((trees, nt * m, width), BF) for m in sizes),
                name="order",
                us=1,
            )(jnp.stack(places).astype(jnp.int32), *blocks)

        def swap(x, pairs):
            return lax.ppermute(x, "tensor", pairs + [(b, a) for a, b in pairs])

        first_at = [jnp.maximum(zi - 1, 0), jnp.minimum(zi + 1, nt - 1), zi]

        out_near = spread_near(result)
        attn_got = pc(attn_far, 1)

        *dq_send, grad_q, kv_near, kv_far, bias_rows = backward(
            *tables, *sources, *grad_heads, log_total
        )
        ff_half = lax.psum_scatter(ff_sent, "fsdp", scatter_dimension=0, tiled=True)[0]
        ff_half = ff_half.reshape(nt, 2 * depth, fc)
        kv_far, kv_near, attn_got, all_y, *out_near = gate(
            kv_far, kv_near, attn_got, all_y, *out_near
        )
        kv_got = pc(kv_far, 1)
        kv_mid = (kv_near[1].astype(F32) + kv_got[1].astype(F32)).astype(BF)
        own = lax.psum_scatter(ff_half, "tensor", scatter_dimension=0, tiled=True)[0]
        kv_mid, result, attn_got, attn_near, attn_mid, all_q, all_y = gate(
            kv_mid, result, attn_got, attn_near, attn_mid, all_q, all_y
        )
        all_w = [all_q, all_y, pc(all_q, 1), pc(all_y, 1)]
        kv_end = pc(kv_mid, 2)
        if nt == 4:
            out_far = [swap(result, [(0, 2), (1, 3)])]
            out_far.append(
                lax.ppermute(out_far[0], "tensor", [(2, 3), (1, 0), (3, 2), (0, 1)])
            )
        else:
            out_far = [pz(result, j) for j in range(2, nt - 1)]
        attn_two = jnp.stack([attn_near, attn_mid]) + attn_got.astype(F32)
        attn_two = scatter_f(attn_two, 3)
        attn_end = pc(attn_two[1].astype(BF), 2)
        kv_end, attn_two, attn_end, all_w, out_far[0] = gate(
            kv_end, attn_two, attn_end, all_w, out_far[0]
        )
        attn_sum = (attn_two[0] + attn_end.astype(F32)).astype(BF)
        attn_sum = lax.dynamic_slice_in_dim(
            jnp.concatenate([attn_sum, attn_sum], axis=0), nt - zi, nt, 0
        )
        attn_own = lax.psum_scatter(attn_sum, "tensor", scatter_dimension=0, tiled=True)[0]
        five = pl.BlockSpec((1, 1, 1, tall, cols), lambda t, k, *_: (0, k, t, 0, 0))
        four = pl.BlockSpec((1, 1, tall, cols), lambda t, k, *_: (k, t, 0, 0))
        send = pl.BlockSpec((3, 1, zr + zs, cols), lambda t, k, *_: (0, t, 0, 0))
        grad_kv, *kv_send = call(
            functools.partial(combine_kernel, rows),
            (trees, 2),
            [five, five, four]
            + [pl.BlockSpec((1, zr, cols), lambda t, k, *_: (t, 0, 0))] * nt,
            (four,) + (send,) * nt,
            (sds((2, trees, tall, cols), BF),) + (sds((3, trees, zr + zs, cols), BF),) * nt,
            name="combine",
            keep=True,
        )(pos, kv_near, kv_got, kv_end, *dq_send)
        dqkv = [kv_send[0]] + [pz(kv_send[j], j) for j in range(1, nt)]

        dq_rows = depth // nc
        cut_specs = (whole((2, nf, dq_rows, 3 * cols)),) + (whole((nf, dq_rows, 3 * cols)),) * 2
        qkv_far, qkv_mid, qkv_own = call(
            functools.partial(qkv_grad_kernel, nf),
            (trees,),
            [
                pl.BlockSpec((1, tall, width), lambda t, *_: (t, 0, 0)),
                pl.BlockSpec((1, rows, cols), lambda t, *_: (t, 0, 0)),
                pl.BlockSpec((2, 1, tall, cols), lambda t, *_: (0, t, 0, 0)),
            ],
            cut_specs,
            (
                sds((2, nf, dq_rows, 3 * cols), BF),
                sds((nf, dq_rows, 3 * cols), F32),
                sds((nf, dq_rows, 3 * cols), F32),
            ),
            [pltpu.VMEM((nf * depth, 3 * cols), F32), pltpu.VMEM((tall, 3 * cols), BF)],
            name="qkv_grads",
            keep=True,
            us=8,
        )(pos, normed, grad_q, grad_kv)
        if nt == 4:
            places = first_at + [zi ^ 2, 3 - zi]
            blocks = [out_near[0], out_near[1], result, *out_far]
        else:
            blocks = [result, *out_near, *out_far]
            places = [zi, (zi + 1) % nt, (zi - 1) % nt] + [(zi + j) % nt for j in range(2, nt - 1)]
        (output,) = ordered(blocks, places, (zr,))
        own_y = pc(own, 2)
        qkv_mid, qkv_own, qkv_far, own_y, output, attn_own, *dqkv = gate(
            qkv_mid, qkv_own, qkv_far, own_y, output, attn_own, *dqkv
        )
        qkv_got = pc(qkv_far, 1)
        own_blocks = (own, own_y, pc(own, 1), pc(own_y, 1))

        chunk_sz = pl.BlockSpec((trees, zs, width), lambda i, pos: (0, pos[1], 0))
        grads_own, stat_c = call(
            functools.partial(input_back_kernel, nt),
            (1,),
            [whole((3, trees, zr + zs, cols))] * nt
            + [whole(all_q.shape)] * 4
            + [chunk_z, chunk_sz, chunk, row_1],
            (whole((trees, zr + zs, width)), stat_spec),
            (sds((trees, zr + zs, width), BF), stat),
            [
                pltpu.VMEM((nt, nf * depth, 3 * cols), BF),
                pltpu.VMEM((nt, trees * (zr + zs), 3 * cols), BF),
                pltpu.VMEM((trees * (zr + zs), width), F32),
            ],
            vmem=44,
            name="input_back",
            keep=True,
        )(pos, *dqkv, *all_w, tokens, state, grad_hidden, gain_1)
        grads_own, qkv_got, *own_blocks = gate(grads_own, qkv_got, *own_blocks)
        qkv_got = qkv_got.astype(F32)

        bias_own = jnp.sum(bias_rows, axis=2)
        bias_all = lax.dynamic_update_slice(
            jnp.zeros((heads * nt, BUCKETS), F32), bias_own, (zi * heads, 0)
        )
        squares = jnp.stack([jnp.sum(stat_a[0]), jnp.sum(stat_a[1]), jnp.sum(mlp_out * mlp_out)])
        spare = jnp.zeros((2 * width - bias_all.size - 3,), F32)
        early = jnp.concatenate(
            [
                stat_b[:2],
                jnp.concatenate([bias_all.reshape(-1), squares, spare]).reshape(2, width),
            ],
            axis=0,
        )
        early, grads_own = gate(early, grads_own)
        sums = jnp.concatenate([stat_c[:2], early], axis=0)

        in_near = spread_near(grads_own)
        *in_near, sums, attn_own, qkv_got = gate(*in_near, sums, attn_own, qkv_got)
        qkv_end = pc((qkv_mid + qkv_got[1]).astype(BF), 2)
        if nt == 4:
            c = swap(grads_own, [(0, 2), (1, 3)])
            d = lax.ppermute(c, "tensor", [(2, 3), (1, 0), (3, 2), (0, 1)])
            places = first_at + [zi ^ 2, 3 - zi]
            blocks = [in_near[0], in_near[1], grads_own, c, d]
        else:
            in_far = [pz(grads_own, j) for j in range(2, nt - 1)]
            blocks = [grads_own, *in_near, *in_far]
        tokens_grad, state_grad = ordered(blocks, places, (zr, zs))
        sums = sums + px(sums) if nf == 2 else lax.psum(sums, "fsdp")
        sums = sums + pc(sums, 1)
        sums = sums + pc(sums, 2)
        if nt & (nt - 1):
            sums = lax.psum(sums, "tensor")
        else:
            k = 1
            while k < nt:
                sums = sums + lax.ppermute(sums, "tensor", [(a, a ^ k) for a in range(nt)])
                k = 2 * k

        qkv_sum = scatter_f(qkv_own + qkv_got[0] + qkv_end.astype(F32), 0)[0].astype(BF)
        if depth % o_rows == 0 and depth * o_rows % dq_rows == 0 and nf == 2:
            folded = jnp.concatenate([attn_own[:, :fc], attn_own[:, fc:]], axis=0)
            qkv_sum = jnp.concatenate([qkv_sum, folded], axis=1)
        else:
            attn_full = gather_c(attn_own, 0).astype(F32)
            folded = None
        qkv_y = pc(qkv_sum, 2)
        qkv_blocks = (qkv_sum, qkv_y, pc(qkv_sum, 1), pc(qkv_y, 1))
        last_shapes = ((depth, cols),) * 3
        if folded is not None:
            last_shapes += ((nc * o_rows, depth),)
        *grad_qkv, grad_attn_out = call(
            finish_qkv_kernel,
            (1,),
            [whole(qkv_sum.shape)] * 4,
            tuple(whole(v) for v in last_shapes),
            tuple(sds(v, F32) for v in last_shapes),
            name="finish_qkv",
            us=0,
        )(pos, *qkv_blocks) + (() if folded is not None else (attn_full,))
        grad_in, grad_out = call(
            finish_ff_kernel,
            (1,),
            [whole(own.shape)] * 4,
            (whole((depth, nc * fc)), whole((nc * fc, depth))),
            (sds((depth, nc * fc), F32), sds((nc * fc, depth), F32)),
            name="finish_ff",
            us=0,
        )(pos, *own_blocks)
        last = sums[4:].reshape(-1)
        bias_sum = last[: bias_all.size].reshape(bias_all.shape)
        grad_bias = lax.dynamic_slice_in_dim(bias_sum, zi * heads, heads, 0)
        cell_count = trees * rows * width * nf * nc
        norms = jnp.sqrt(last[bias_all.size : bias_all.size + 3] / cell_count)
        return (
            output,
            tokens_grad,
            state_grad,
            *grad_qkv,
            grad_attn_out,
            grad_bias,
            sums[0],
            sums[1],
            sums[2],
            sums[3],
            grad_in,
            grad_out,
            norms,
        )

    return on_device


def solution(mesh):
    return jax.shard_map(
        build(mesh),
        mesh=mesh,
        in_specs=(
            P("fsdp", "context", None),
            P("fsdp", "context", None),
            P("fsdp", None),
            P("fsdp", "context"),
            P(),
            P(),
            P(),
            P("fsdp", "tensor"),
            P("fsdp", "tensor"),
            P("fsdp", "tensor"),
            P("tensor", "fsdp"),
            P("tensor", None),
            P(),
            P(),
            P("fsdp", "tensor"),
            P("tensor", "fsdp"),
            P("fsdp", "context", None),
        ),
        out_specs=(
            P("fsdp", "context", None),
            P("fsdp", "context", None),
            P("fsdp", "context", None),
            P("fsdp", "tensor"),
            P("fsdp", "tensor"),
            P("fsdp", "tensor"),
            P("tensor", "fsdp"),
            P("tensor", None),
            P(),
            P(),
            P(),
            P(),
            P("fsdp", "tensor"),
            P("tensor", "fsdp"),
            P(),
        ),
        check_vma=False,
    )
```

```python
import functools
import math

import jax
import jax.numpy as jnp
from jax import lax
from jax.experimental import pallas as pl
from jax.experimental.pallas import tpu as pltpu
from jax.sharding import PartitionSpec as P

WINDOW = 512
BUCKETS = 32
REACH = 128
EPSILON = 1e-05
MASKED = -1e30
GELU_C = 0.7978845608028654
GELU_A = 0.044715
BF = jnp.bfloat16
F32 = jnp.float32


def cost(us):
    return pl.CostEstimate(
        flops=int(us * 1e9), transcendentals=0, bytes_accessed=int(us * 3e6)
    )


def bucket_edges(bucket_total, far_reach, window):
    exact_count = bucket_total // 2
    boundaries = []
    current = 0
    for distance in range(window):
        if distance < exact_count:
            bucket = distance
        else:
            bucket = exact_count + int(
                math.log(distance / exact_count)
                / math.log(far_reach / exact_count)
                * (bucket_total - exact_count)
            )
            bucket = min(bucket, bucket_total - 1)
        while current < bucket:
            current = current + 1
            boundaries.append(distance)
    return boundaries


EDGES = bucket_edges(BUCKETS, REACH, WINDOW)


def mm(left, right):
    return lax.dot_general(left, right, (((1,), (0,)), ((), ())), preferred_element_type=F32)


def mm_nt(left, right):
    return lax.dot_general(left, right, (((1,), (1,)), ((), ())), preferred_element_type=F32)


def mm_tn(left, right):
    return lax.dot_general(left, right, (((0,), (0,)), ((), ())), preferred_element_type=F32)


def bias_tables(rb_ref, h, levels, seg, bm_ref):
    key = lax.broadcasted_iota(jnp.int32, (seg, seg), 0)
    query = lax.broadcasted_iota(jnp.int32, (seg, seg), 1)
    for lev in range(levels):
        dist = lev * seg + query - key
        low, high = lev * seg - (seg - 1), lev * seg + seg - 1
        if low >= EDGES[-1]:
            val = jnp.full((seg, seg), rb_ref[h, BUCKETS - 1], F32)
        else:
            val = jnp.full((seg, seg), rb_ref[h, 0], F32)
            for i, edge in enumerate(EDGES):
                if edge <= high:
                    val = jnp.where(dist >= edge, rb_ref[h, i + 1], val)
        if low < 0:
            val = jnp.where(dist >= 0, val, MASKED)
        if high >= WINDOW:
            val = jnp.where(dist < WINDOW, val, MASKED)
        bm_ref[lev * seg : (lev + 1) * seg, :] = val


def chain(par_ref, t, first, levels, all_segs, local_segs, ctx):
    out = []
    anc = first
    for lev in range(levels):
        if lev > 0:
            up = par_ref[t, jnp.maximum(anc, 0)]
            anc = jnp.where(anc >= 0, up, -1)
        safe = jnp.maximum(anc, 0)
        owner = lax.div(safe, local_segs)
        out.append((anc >= 0, jnp.bitwise_xor(owner, ctx), safe - owner * local_segs))
    return out


def window_score(raw, lev, bm_ref, line, length, seg):
    part = raw + bm_ref[lev * seg : (lev + 1) * seg, :]
    if lev == 0:
        key = lax.broadcasted_iota(jnp.int32, (seg, 1), 0)
        return part + jnp.where(key < length, 0.0, MASKED)
    return part + jnp.where(line[lev][0], 0.0, MASKED)


def fold(value, op):
    out = value[0:8]
    for i in range(8, value.shape[0], 8):
        out = op(out, value[i : i + 8])
    return out


def attend_kernel(dims, par_ref, len_ref, pos_ref, rb_ref, q_ref, *refs):
    levels, seg, local_segs, all_segs, factor, nt = dims
    parts_k, parts_v = refs[0:4], refs[4:8]
    att_refs, lse_ref = refs[8 : 8 + nt], refs[8 + nt]
    kall, vall_t, kws, vw_ts, bm, whole, q_t, raws_a, probs_a = refs[9 + nt :]
    t, h = pl.program_id(0), pl.program_id(1)
    ctx, zi = pos_ref[0], pos_ref[1]
    rows, win = local_segs * seg, levels * seg
    each = (kws.shape[1] - win) // 4
    blocks = kws.shape[1] // seg
    bias_tables(rb_ref, h, levels, seg, bm)
    for b in range(4):
        at = slice(win + b * each, win + (b + 1) * each)
        kall[b] = parts_k[b][0, :rows, :]
        turned = parts_v[b][0].T
        vall_t[b] = turned[:, :rows]
        for i in range(2):
            kws[i, at, :] = parts_k[b][0, rows:, :]
            vw_ts[i, :, at] = turned[:, rows:]
    q_t[...] = q_ref[0, :rows, :].T

    def one(s, carry):
        kw, vw_t, raws, probs = (r.at[s % 2] for r in (kws, vw_ts, raws_a, probs_a))
        line = chain(par_ref, t, ctx * local_segs + s, levels, all_segs, local_segs, ctx)
        for lev, (_, part, block) in enumerate(line):
            start = pl.ds(pl.multiple_of(block * seg, seg), seg)
            kw[lev * seg : (lev + 1) * seg, :] = kall[part, start, :]
            vw_t[:, lev * seg : (lev + 1) * seg] = vall_t[part, :, start]
        at = slice(s * seg, (s + 1) * seg)
        turned = q_t[:, at]
        top = None
        for c in range(blocks):
            raw = mm(kw[c * seg : (c + 1) * seg, :], turned) * factor
            if c < levels:
                raw = window_score(raw, c, bm, line, len_ref[t, s], seg)
            raws[c * seg : (c + 1) * seg, :] = raw
            high = fold(raw, jnp.maximum)
            top = high if top is None else jnp.maximum(top, high)
        top = jnp.max(top, axis=0, keepdims=True)
        total = None
        for c in range(blocks):
            prob = jnp.exp(raws[c * seg : (c + 1) * seg, :] - top)
            probs[c * seg : (c + 1) * seg, :] = prob.astype(BF)
            part = fold(prob, jnp.add)
            total = part if total is None else total + part
        total = jnp.sum(total, axis=0, keepdims=True)
        lse_ref[0, 0, 0:1, at] = top + jnp.log(total)
        att = mm(vw_t[...], probs[...]) / total
        whole[at, :] = att.T.astype(BF)
        return carry

    for s in range(local_segs):
        one(s, 0)
    n = rows // nt
    for j in range(nt):
        k = lax.rem(zi - j + nt, nt)
        att_refs[j][0] = whole[pl.ds(pl.multiple_of(k * n, n), n), :]


def attend_back_kernel(dims, par_ref, len_ref, pos_ref, rb_ref, q_ref, *refs):
    levels, seg, local_segs, all_segs, factor, nt = dims
    parts_k, parts_v = refs[0:4], refs[4:8]
    do_refs, lse_ref = refs[8 : 8 + nt], refs[8 + nt]
    dq_refs = refs[9 + nt : 9 + 2 * nt]
    dq_ref, near_ref, far_ref, db_ref = refs[9 + 2 * nt : 13 + 2 * nt]
    kall, vall, kall_t, kw, vw, kw_t, bm, dk, dv, near, far, dos, do_t, q_t, raws, dps, dss, pbs = refs[
        13 + 2 * nt :
    ]
    h, t = pl.program_id(0), pl.program_id(1)
    ctx, zi = pos_ref[0], pos_ref[1]
    rows, win = local_segs * seg, levels * seg
    each = (kw.shape[0] - win) // 4
    blocks = kw.shape[0] // seg
    n = rows // nt
    bias_tables(rb_ref, h, levels, seg, bm)
    for b in range(4):
        at = slice(win + b * each, win + (b + 1) * each)
        kall[b] = parts_k[b][0, :rows, :]
        vall[b] = parts_v[b][0, :rows, :]
        turned = parts_k[b][0].T
        kall_t[b] = turned[:, :rows]
        kw[at, :] = parts_k[b][0, rows:, :]
        vw[at, :] = parts_v[b][0, rows:, :]
        kw_t[:, at] = turned[:, rows:]
    dk[...] = jnp.zeros(dk.shape, F32)
    dv[...] = jnp.zeros(dv.shape, F32)
    for j in range(nt):
        k = lax.rem(zi - j + nt, nt)
        dos[pl.ds(pl.multiple_of(k * n, n), n), :] = do_refs[j][0]
    q_t[...] = q_ref[0, :rows, :].T
    do_t[...] = dos[...].T

    @pl.when(t == 0)
    def _():
        near[...] = jnp.zeros(near.shape, F32)
        far[...] = jnp.zeros(far.shape, F32)

    def one(s, carry):
        line = chain(par_ref, t, ctx * local_segs + s, levels, all_segs, local_segs, ctx)
        for lev, (_, part, block) in enumerate(line):
            start = pl.ds(pl.multiple_of(block * seg, seg), seg)
            at = slice(lev * seg, (lev + 1) * seg)
            kw[at, :] = kall[part, start, :]
            vw[at, :] = vall[part, start, :]
            kw_t[:, at] = kall_t[part, :, start]
        at = pl.ds(pl.multiple_of(s * seg, seg), seg)
        turned, do_turned = q_t[:, at], do_t[:, at]
        lse = lse_ref[0, 0, 0:1, at]
        delta = None
        for c in range(blocks):
            cut = slice(c * seg, (c + 1) * seg)
            raw = mm(kw[cut, :], turned) * factor
            if c < levels:
                raw = window_score(raw, c, bm, line, len_ref[t, s], seg)
            prob = jnp.exp(raw - lse)
            dprob = mm(vw[cut, :], do_turned)
            raws[cut, :] = prob
            dps[cut, :] = dprob
            pbs[cut, :] = prob.astype(BF)
            part = fold(prob * dprob, jnp.add)
            delta = part if delta is None else delta + part
        delta = jnp.sum(delta, axis=0, keepdims=True)
        for c in range(blocks):
            cut = slice(c * seg, (c + 1) * seg)
            dscore = (raws[cut, :] * (dps[cut, :] - delta)).astype(BF)
            dss[cut, :] = dscore
            if c < 2:
                near[cut, :] += dscore.astype(F32)
            elif c < levels:
                far[...] += dscore.astype(F32)
        dq = mm(kw_t[...], dss[...]) * factor
        dq_ref[0, at, :] = dq.T.astype(BF)
        q, do = q_ref[0, at, :], dos[at, :]
        for c in range(blocks):
            cut = slice(c * seg, (c + 1) * seg)
            gk = mm(dss[cut, :], q) * factor
            gv = mm(pbs[cut, :], do)
            if c < levels:
                _, part, block = line[c]
                to = pl.ds(pl.multiple_of(block * seg, seg), seg)
                dk[part, to, :] += gk
                dv[part, to, :] += gv
            else:
                for i in range(0, seg, each):
                    b = ((c - levels) * seg + i) // each
                    dk[b, rows:, :] += gk[i : i + each]
                    dv[b, rows:, :] += gv[i : i + each]
        return carry

    lax.fori_loop(0, local_segs, one, 0)
    for ref, pair in ((near_ref, (0, 2)), (far_ref, (1, 3))):
        for place, b in enumerate(pair):
            ref[place, 0, 0] = dk[b].astype(BF)
            ref[place, 1, 0] = dv[b].astype(BF)
    for j in range(nt):
        k = lax.rem(zi - j + nt, nt)
        dq_refs[j][0] = dq_ref[0, pl.ds(pl.multiple_of(k * n, n), n), :]

    @pl.when(t == pl.num_programs(1) - 1)
    def _():
        key = lax.broadcasted_iota(jnp.int32, (seg, seg), 0)
        query = lax.broadcasted_iota(jnp.int32, (seg, seg), 1)
        edges = [-(10**6)] + list(EDGES) + [10**6]
        for b in range(BUCKETS):
            total = far[...] if b == BUCKETS - 1 else jnp.zeros((seg, seg), F32)
            for lev in range(2):
                dist = lev * seg + query - key
                inside = (dist >= edges[b]) & (dist < edges[b + 1])
                total = total + jnp.where(inside, near[lev * seg : (lev + 1) * seg, :], 0.0)
            db_ref[0, b : b + 1, :] = jnp.sum(total, axis=0, keepdims=True)


def hbm_call(prefetch, body, out_shape, keep=False, **kw):
    if not keep:
        return pl.pallas_call(body, out_shape=out_shape, **kw)
    several = isinstance(out_shape, tuple)
    outs = tuple(
        pltpu.HBM(o.shape, o.dtype) for o in (out_shape if several else (out_shape,))
    )
    kernel = pl.pallas_call(body, out_shape=outs if several else outs[0], **kw)

    def run(*args):
        rest = [pltpu.with_memory_space_constraint(a, pltpu.HBM) for a in args[prefetch:]]
        return kernel(*args[:prefetch], *rest)

    return run


def attention_calls(trees, heads, local_segs, all_segs, seg, each, head_dim, nt):
    levels = WINDOW // seg + 1
    rows = local_segs * seg
    tall = rows + each
    win = levels * seg
    wide = win + 4 * each
    factor = head_dim ** (-0.5)
    dims = (levels, seg, local_segs, all_segs, factor, nt)
    assert EDGES[-1] <= 2 * seg - (seg - 1)
    assert seg == head_dim == 128 and wide % seg == 0 and seg % each == 0
    vm = lambda dt, *shape: pltpu.VMEM(shape, dt)
    forward_scratch = [
        vm(BF, 4, rows, head_dim),
        vm(BF, 4, head_dim, rows),
        vm(BF, 2, wide, head_dim),
        vm(BF, 2, head_dim, wide),
        vm(F32, win, seg),
        vm(BF, rows, head_dim),
        vm(BF, head_dim, rows),
        vm(F32, 2, wide, seg),
        vm(BF, 2, wide, seg),
    ]
    backward_scratch = [
        vm(BF, 4, rows, head_dim),
        vm(BF, 4, rows, head_dim),
        vm(BF, 4, head_dim, rows),
        vm(BF, wide, head_dim),
        vm(BF, wide, head_dim),
        vm(BF, head_dim, wide),
        vm(F32, win, seg),
        vm(F32, 4, tall, head_dim),
        vm(F32, 4, tall, head_dim),
        vm(F32, 2 * seg, seg),
        vm(F32, seg, seg),
        vm(BF, rows, head_dim),
        vm(BF, head_dim, rows),
        vm(BF, head_dim, rows),
        vm(F32, wide, seg),
        vm(F32, wide, seg),
        vm(BF, wide, seg),
        vm(BF, wide, seg),
    ]
    lse_shape = jax.ShapeDtypeStruct((trees, heads, 8, rows), F32)

    def specs(order):
        def at(col):
            return pl.BlockSpec(
                (1, tall, head_dim), lambda a, b, *_: (order(a, b)[0], 0, col(order(a, b)[1]))
            )

        k, v = at(lambda h: h), at(lambda h: heads + h)
        return [k, k, k, k, k, v, v, v, v]

    th = lambda a, b: (a, b)
    ht = lambda a, b: (b, a)
    chunk_shape = jax.ShapeDtypeStruct((trees, rows // nt, heads * head_dim), BF)

    def chunk_spec(order):
        return pl.BlockSpec(
            (1, rows // nt, head_dim), lambda a, b, *_: (order(a, b)[0], 0, order(a, b)[1])
        )

    forward = hbm_call(
        4,
        functools.partial(attend_kernel, dims),
        out_shape=(chunk_shape,) * nt + (lse_shape,),
        grid_spec=pltpu.PrefetchScalarGridSpec(
            num_scalar_prefetch=4,
            grid=(trees, heads),
            in_specs=specs(th),
            out_specs=(chunk_spec(th),) * nt
            + (pl.BlockSpec((1, 1, 8, rows), lambda t, h, *_: (t, h, 0, 0)),),
            scratch_shapes=forward_scratch,
        ),
        compiler_params=pltpu.CompilerParams(vmem_limit_bytes=24 << 20),
        cost_estimate=cost(16),
        keep=True,
        name="attend",
    )
    pair = jax.ShapeDtypeStruct((2, 2, trees, tall, heads * head_dim), BF)
    pair_spec = pl.BlockSpec((2, 2, 1, tall, head_dim), lambda h, t, *_: (0, 0, t, 0, h))
    backward = hbm_call(
        4,
        functools.partial(attend_back_kernel, dims),
        out_shape=(chunk_shape,) * nt
        + (
            jax.ShapeDtypeStruct((trees, rows, heads * head_dim), BF),
            pair,
            pair,
            jax.ShapeDtypeStruct((heads, BUCKETS, 128), F32),
        ),
        grid_spec=pltpu.PrefetchScalarGridSpec(
            num_scalar_prefetch=4,
            grid=(heads, trees),
            in_specs=specs(ht)
            + [chunk_spec(ht)] * nt
            + [pl.BlockSpec((1, 1, 8, rows), lambda h, t, *_: (t, h, 0, 0))],
            out_specs=(chunk_spec(ht),) * nt
            + (
                pl.BlockSpec((1, rows, head_dim), lambda h, t, *_: (t, 0, h)),
                pair_spec,
                pair_spec,
                pl.BlockSpec((1, BUCKETS, 128), lambda h, t, *_: (h, 0, 0)),
            ),
            scratch_shapes=backward_scratch,
        ),
        compiler_params=pltpu.CompilerParams(vmem_limit_bytes=32 << 20),
        cost_estimate=cost(24),
        keep=True,
        name="attend_back",
    )
    return forward, backward


def norm_stats(values):
    mean = jnp.mean(values, axis=-1, keepdims=True)
    centered = values - mean
    scale = lax.rsqrt(jnp.mean(centered * centered, axis=-1, keepdims=True) + EPSILON)
    return centered * scale, scale


def norm_back(grad, xhat, scale, gain):
    scaled = grad * gain
    first = jnp.mean(scaled, axis=-1, keepdims=True)
    second = jnp.mean(scaled * xhat, axis=-1, keepdims=True)
    return scale * (scaled - first - xhat * second)


def gelu_parts(u):
    square = u * u
    th = jnp.tanh(u * (GELU_C + GELU_C * GELU_A * square))
    half = 0.5 * (1.0 + th)
    slope = half + (0.5 * u) * (1.0 - th * th) * (GELU_C + 3.0 * GELU_C * GELU_A * square)
    return u * half, slope


def norm_kernel(gain, shift, tok, st, out):
    each = st.shape[1]
    rows = tok.shape[1]
    for lo in range(0, rows + each, each):
        x = (tok[0, lo : lo + each, :] if lo < rows else st[0]).astype(F32)
        xhat, _ = norm_stats(x)
        out[0, lo : lo + each, :] = (xhat * gain[...] + shift[...]).astype(BF)


def project_kernel(pos, x, *refs):
    if len(refs) == 3:
        w = refs[0]
        q_ref, kv_ref = refs[1:]
    else:
        wq, wk, wv, near, over, q_ref, kv_ref, w = refs

        @pl.when((pl.program_id(0) == 0) & (pl.program_id(1) == 0))
        def _():
            fi, core = pos[2], pos[0] & 1
            depth, cols = wq.shape
            half = depth // 2
            for i, part in enumerate((wq, wk, wv)):
                w[pl.ds(pl.multiple_of(fi * depth, depth), depth), i * cols : (i + 1) * cols] = (
                    part[...]
                )
            base = (1 - fi) * depth
            w[pl.ds(pl.multiple_of(base + core * half, half), half), :] = near[...]
            w[pl.ds(pl.multiple_of(base + (1 - core) * half, half), half), :] = over[...]

    y = mm(x[0], w[...]).astype(BF)
    cols = q_ref.shape[2]
    q_ref[0] = y[:, :cols]
    kv_ref[0] = y[:, cols:]


def load_projection(pos, blocks, w):
    rows, depth = blocks[0].shape
    n = w.shape[0] // rows
    for j in range(n):
        at = slice(j * rows, (j + 1) * rows)
        if n == len(blocks):
            w[at, :] = blocks[j][...]
        else:
            fi = pos[2]
            w[at, pl.ds(pl.multiple_of(fi * depth, depth), depth)] = blocks[j][...]
            w[at, pl.ds(pl.multiple_of((1 - fi) * depth, depth), depth)] = blocks[n][j]


def mix_kernel(n, pos, *refs):
    att, blocks = refs[:n], refs[n:-10]
    tok, cell, gain, shift, hid_ref, n2_ref, stat_ref, w, left, branch = refs[-10:]

    load_projection(pos, blocks, w)
    stat_ref[...] = jnp.zeros(stat_ref.shape, F32)
    cols = att[0].shape[2]
    shape = tok.shape
    mine = shape[0] * shape[1]
    for j in range(n):
        left[:, j * cols : (j + 1) * cols] = att[j][...].reshape(mine, cols)
    branch[...] = mm(left[...], w[...])
    x = tok[...].astype(F32).reshape(mine, shape[2])
    gated = cell[...] * branch[...]
    hidden = x + gated
    hid_ref[...] = hidden.reshape(shape)
    xhat, _ = norm_stats(hidden)
    n2_ref[...] = (xhat * gain[...] + shift[...]).astype(BF).reshape(shape)
    stat_ref[0:1, :] = jnp.sum(x * x, axis=0, keepdims=True)
    stat_ref[1:2, :] = jnp.sum(gated * gated, axis=0, keepdims=True)


def ff_kernel(*refs):
    xs, gs = refs[0:2], refs[2:4]
    pack, first_ref, second_ref, act_ref, gup_ref, acc, xall, gall = refs[4:]
    nf, depth = pack.shape[1], pack.shape[3]
    z = pl.program_id(0)
    mine = xs[0].shape[0]
    cut = [slice(f * depth, (f + 1) * depth) for f in range(nf)]

    @pl.when(z == 0)
    def _():
        for p in range(2):
            xall[p] = xs[p][...]
            gall[p] = gs[p][...]
        acc[...] = jnp.zeros(acc.shape, F32)

    def one(p, carry):
        up = mm(xall[p, :, cut[0]], pack[0, 0, 0])
        back = mm(gall[p, :, cut[0]], pack[0, 0, 1])
        for f in range(1, nf):
            up = up + mm(xall[p, :, cut[f]], pack[0, f, 0])
            back = back + mm(gall[p, :, cut[f]], pack[0, f, 1])
        value, slope = gelu_parts(up)
        act_ref[p] = value.astype(BF)
        gup = (back * slope).astype(BF)
        gup_ref[p] = gup
        for f in range(nf):
            acc[p, :, cut[f]] += mm_nt(gup, pack[0, f, 0])
        return carry

    lax.fori_loop(0, 2, one, 0)

    @pl.when(z == pl.num_programs(0) - 1)
    def _():
        first_ref[...] = acc[0].astype(BF)
        second_ref[...] = acc[1].astype(BF)


def ff_grad_kernel(*refs):
    xs, gs = refs[0:4], refs[4:8]
    act_a, gup_a, act_b, gup_b, pack = refs[8:13]
    sent_ref, near_ref, far_ref, rows, acc, wout, units = refs[13:]
    _, nf, _, depth, fc = pack.shape
    mine = xs[0].shape[0]

    @pl.when(pl.program_id(0) == 0)
    def _():
        for p in range(4):
            rows[0, p * mine : (p + 1) * mine, :] = xs[p][...]
            rows[1, p * mine : (p + 1) * mine, :] = gs[p][...]
        acc[...] = jnp.zeros(acc.shape, F32)

    for f in range(nf):
        wout[f * depth : (f + 1) * depth, :] = pack[0, f, 1]
    for half, (a_ref, u_ref) in enumerate(((act_a, gup_a), (act_b, gup_b))):
        for p in range(2):
            at = slice((2 * half + p) * mine, (2 * half + p + 1) * mine)
            units[1, at, :] = a_ref[p]
            units[0, at, :] = u_ref[p]

    acc[...] += mm_nt(units[1], wout[...])

    def grads(i, carry):
        part = mm_tn(rows[i], units[i])
        for f in range(nf):
            sent_ref[f, 0, i] = part[f * depth : (f + 1) * depth].astype(BF)
        return carry

    lax.fori_loop(0, 2, grads, 0)

    @pl.when(pl.program_id(0) == pl.num_programs(0) - 1)
    def _():
        for i, ref in enumerate((near_ref, far_ref)):
            for p in range(2):
                lo = (2 * p + i) * mine
                ref[p] = acc[lo : lo + mine, :].astype(BF)


def branch_back_kernel(nt, pos, *refs):
    blocks, (own, got, far, hid, cot, cell, gain) = refs[: -(nt + 11)], refs[-(nt + 11) : -(nt + 4)]
    gh_ref, gb_ref = refs[-(nt + 4) : -(nt + 2)]
    ga_refs, stat_ref, w = refs[-(nt + 2) : -2], refs[-2], refs[-1]

    load_projection(pos, blocks, w)
    stat_ref[...] = jnp.zeros(stat_ref.shape, F32)
    shape = cot.shape
    mine = shape[0] * shape[1]
    flat = lambda v: v.astype(F32).reshape(mine, shape[2])
    grad = flat(own[...]) + flat(got[...]) + flat(far[...])
    xhat, scale = norm_stats(flat(hid[...]))
    gh = flat(cot[...]) + norm_back(grad, xhat, scale, gain[...])
    gh_ref[...] = gh.reshape(shape)
    gb = (cell[...] * gh).astype(BF)
    gb_ref[...] = gb.reshape(shape)
    cols = ga_refs[0].shape[2]
    for j, ref in enumerate(ga_refs):
        ref[...] = mm_nt(gb, w[j * cols : (j + 1) * cols, :]).astype(BF).reshape(ref.shape)
    stat_ref[0:1, :] = jnp.sum(grad * xhat, axis=0, keepdims=True)
    stat_ref[1:2, :] = jnp.sum(grad, axis=0, keepdims=True)


def combine_kernel(rows, pos, own, got, far, *refs):
    nt = (len(refs) - 1) // 2
    dq, total_ref, send = refs[:nt], refs[nt], refs[nt + 1 :]
    total = (
        own[0, 0, 0].astype(F32) + got[0, 0, 0].astype(F32) + far[0, 0].astype(F32)
    ).astype(BF)
    total_ref[0, 0] = total
    n = rows // nt
    m = (total_ref.shape[2] - rows) // nt
    kv = pl.program_id(1)
    for j in range(nt):
        k = lax.rem(pos[1] - j + nt, nt)

        @pl.when(kv == 0)
        def _():
            send[j][0, 0, :n, :] = dq[j][0]
            send[j][0, 0, n:, :] = jnp.zeros((m, dq[j].shape[2]), BF)

        send[j][1 + kv, 0, :n, :] = total_ref[0, 0, pl.ds(pl.multiple_of(k * n, n), n), :]
        send[j][1 + kv, 0, n:, :] = total_ref[0, 0, pl.ds(pl.multiple_of(rows + k * m, m), m), :]


def input_back_kernel(nt, pos, *refs):
    blocks = refs[:nt]
    parts, (tok, st, gh, gain, out_ref, stat_ref, w, left, every) = (
        refs[nt : nt + 4],
        refs[nt + 4 :],
    )
    m = parts[0].shape[1]
    nf = parts[0].shape[0] // nt
    cols = blocks[0].shape[3]
    trees, n = tok.shape[0], tok.shape[1]
    tall = blocks[0].shape[2]
    for flip, part in zip((0, 2, 1, 3), parts):

        def put(i, carry, flip=flip, part=part):
            z = lax.div(i, nf)
            at = ((i - z * nf) * 4 + jnp.bitwise_xor(pos[0], flip)) * m
            w[z, pl.ds(pl.multiple_of(at, m), m), :] = part[i]
            return carry

        lax.fori_loop(0, nt * nf, put, 0)
    for j in range(nt):
        for i in range(3):
            left[j, :, i * cols : (i + 1) * cols] = blocks[j][i].reshape(trees * tall, cols)
    step = 256

    def one(i, carry):
        at = pl.ds(pl.multiple_of(i * step, step), step)
        total = mm_nt(left[0], w[pos[1], at, :])
        for j in range(1, nt):
            total = total + mm_nt(left[j], w[lax.rem(pos[1] + j, nt), at, :])
        every[:, at] = total
        return carry

    lax.fori_loop(0, every.shape[1] // step, one, 0)
    stat_ref[...] = jnp.zeros(stat_ref.shape, F32)
    for t in range(trees):
        for x_ref, lo, hi, extra in ((tok, 0, n, gh), (st, n, tall, None)):
            grad = every[t * tall + lo : t * tall + hi, :]
            xhat, scale = norm_stats(x_ref[t].astype(F32))
            back = norm_back(grad, xhat, scale, gain[...])
            if extra is not None:
                back = back + extra[t]
            out_ref[t, lo:hi, :] = back.astype(BF)
            stat_ref[0:1, :] += jnp.sum(grad * xhat, axis=0, keepdims=True)
            stat_ref[1:2, :] += jnp.sum(grad, axis=0, keepdims=True)


def attn_grad_kernel(nt, pos, *refs):
    blocks, grad = refs[:nt], refs[nt]
    far_ref, mid_ref, own_ref, acc, left = refs[nt + 1 :]
    n = own_ref.shape[1]
    rows = grad.shape[0] * grad.shape[1]
    for j in range(nt):
        left[j] = blocks[j][...].reshape(rows, acc.shape[0])

    def one(j, carry):
        acc[...] = mm_tn(left[j], grad[...].reshape(rows, grad.shape[2]))
        for flip, ref in ((0, own_ref), (2, mid_ref), (1, far_ref), (3, far_ref)):
            k = jnp.bitwise_xor(pos[0], flip)
            piece = acc[pl.ds(pl.multiple_of(k * n, n), n), :]
            if flip & 1:
                ref[flip // 2, j] = piece.astype(BF)
            else:
                ref[j] = piece
        return carry

    lax.fori_loop(0, nt, one, 0)


def qkv_grad_kernel(nf, pos, x, gq, gkv, far_ref, mid_ref, own_ref, acc, right):
    t = pl.program_id(0)
    rows, cols = gq.shape[1], gq.shape[2]
    tall = x.shape[1]
    right[:rows, :cols] = gq[0]
    right[rows:, :cols] = jnp.zeros((tall - rows, cols), BF)
    right[:, cols : 2 * cols] = gkv[0, 0]
    right[:, 2 * cols :] = gkv[1, 0]

    @pl.when(t == 0)
    def _():
        acc[...] = jnp.zeros(acc.shape, F32)

    def one(i, carry):
        at = pl.ds(pl.multiple_of(i * cols, cols), cols)
        acc[:, at] += mm_tn(x[0], right[:, at])
        return carry

    lax.fori_loop(0, 3, one, 0)

    @pl.when(t == pl.num_programs(0) - 1)
    def _():
        n = own_ref.shape[1]
        for f in range(nf):
            for flip, ref in ((0, own_ref), (2, mid_ref), (1, far_ref), (3, far_ref)):
                k = jnp.bitwise_xor(pos[0], flip)
                start = pl.multiple_of(f * (acc.shape[0] // nf) + k * n, n)
                piece = acc[pl.ds(start, n), :]
                if flip & 1:
                    ref[flip // 2, f] = piece.astype(BF)
                else:
                    ref[f] = piece


def order_kernel(sizes, places, *refs):
    outs = refs[-len(sizes) :]
    for i, block in enumerate(refs[: -len(sizes)]):
        lo = 0
        for n, out in zip(sizes, outs):
            out[0, pl.ds(pl.multiple_of(places[i] * n, n), n), :] = block[0, lo : lo + n, :]
            lo = lo + n


def finish_ff_kernel(pos, *refs):
    gin, gout = refs[4:]
    depth, fc = gin.shape[0], refs[0].shape[1]
    for flip, b in zip((0, 2, 1, 3), refs[:4]):
        k = jnp.bitwise_xor(pos[0], flip)
        at = pl.ds(pl.multiple_of(k * fc, fc), fc)
        gin[:, at] = b[:depth, :].astype(F32)
        gout[at, :] = b[depth:, :].astype(F32).T


def finish_qkv_kernel(pos, *refs):
    for flip, b in zip((0, 2, 1, 3), refs[:4]):
        n = b.shape[0]
        k = jnp.bitwise_xor(pos[0], flip)
        at = pl.ds(pl.multiple_of(k * n, n), n)
        cols = refs[4].shape[1]
        for i, out in enumerate(refs[4:7]):
            out[at, :] = b[:, i * cols : (i + 1) * cols].astype(F32)
        for out in refs[7:]:
            m = n * (b.shape[1] - 3 * cols) // out.shape[1]
            wide = b.shape[1] - 3 * cols
            at = pl.ds(pl.multiple_of(k * m, m), m)
            for i in range(n // m):
                out[at, i * wide : (i + 1) * wide] = b[
                    i * m : (i + 1) * m, 3 * cols :
                ].astype(F32)


def build(mesh):
    nf, nc, nt = mesh.shape["fsdp"], mesh.shape["context"], mesh.shape["tensor"]
    assert nc == 4

    def px(x):
        return lax.ppermute(x, "fsdp", [(0, 1), (1, 0)])

    def pc(x, k):
        return lax.ppermute(x, "context", [(a, a ^ k) for a in range(nc)])

    def pz(x, j):
        return lax.ppermute(x, "tensor", [(a, (a - j) % nt) for a in range(nt)])

    def ps(x, j):
        return lax.ppermute(x, "tensor", [(a, (a + j) % nt) for a in range(nt)])

    def on_device(
        tokens,
        state,
        parent,
        seg_length,
        cell_gate,
        norm1_gain,
        norm1_shift,
        w_query,
        w_key,
        w_value,
        w_attn_out,
        rel_bias,
        norm2_gain,
        norm2_shift,
        w_in,
        w_out,
        cotangent,
    ):
        trees, rows, width = tokens.shape
        local_segs = seg_length.shape[1]
        seg = rows // local_segs
        all_segs = parent.shape[1]
        heads = rel_bias.shape[0]
        depth, cols = w_query.shape
        head_dim = cols // heads
        each = state.shape[1]
        tall = rows + each
        fi, ci, zi = lax.axis_index("fsdp"), lax.axis_index("context"), lax.axis_index("tensor")
        core = ci & 1
        zr, zs = rows // nt, each // nt
        mine = trees * zr
        pos = jnp.stack([ci, zi, fi]).astype(jnp.int32)
        cell, gain_1, shift_1, gain_2, shift_2 = (
            v.reshape(1, width)
            for v in (cell_gate, norm1_gain, norm1_shift, norm2_gain, norm2_shift)
        )
        sds = jax.ShapeDtypeStruct

        def gate(*xs):
            return lax.optimization_barrier(xs)

        stat = sds((8, width), F32)

        def call(body, grid, ins, outs, out_shape, scratch=(), prefetch=1, vmem=24, name="", us=4, keep=False):
            return hbm_call(
                prefetch,
                body,
                out_shape=out_shape,
                grid_spec=pltpu.PrefetchScalarGridSpec(
                    num_scalar_prefetch=prefetch,
                    grid=grid,
                    in_specs=ins,
                    out_specs=outs,
                    scratch_shapes=scratch,
                ),
                compiler_params=pltpu.CompilerParams(vmem_limit_bytes=vmem << 20),
                cost_estimate=cost(us),
                keep=keep,
                name=name,
            )

        def whole(shape):
            return pl.BlockSpec(shape, lambda *_: (0,) * len(shape))

        row_1 = whole((1, width))
        stat_spec = whole((8, width))

        def place(blocks, starts, axis, total):
            shape = list(blocks[0].shape)
            shape[axis] = total
            out = jnp.zeros(shape, blocks[0].dtype)
            for block, start in zip(blocks, starts):
                out = lax.dynamic_update_slice_in_dim(out, block, start, axis)
            return out

        def half_of(x, k, axis, parts):
            n = x.shape[axis] // parts
            return lax.dynamic_slice_in_dim(x, k * n, n, axis)

        def gather_f(x, axis):
            n = x.shape[axis]
            if nf == 2:
                return place([x, px(x)], [fi * n, (1 - fi) * n], axis, 2 * n)
            return lax.all_gather(x, "fsdp", axis=axis, tiled=True)

        def scatter_f(x, axis):
            if nf == 2:
                sent = half_of(x, 1 - fi, axis, 2).astype(BF)
                return half_of(x, fi, axis, 2) + px(sent).astype(F32)
            return lax.psum_scatter(
                x.astype(BF), "fsdp", scatter_dimension=axis, tiled=True
            ).astype(F32)

        def gather_c(x, axis):
            n = x.shape[axis]
            pair = jnp.stack([x, pc(x, 2)])
            over = pc(pair, 1)
            return place(
                [x, pair[1], over[0], over[1]],
                [ci * n, (ci ^ 2) * n, (ci ^ 1) * n, (ci ^ 3) * n],
                axis,
                nc * n,
            )

        def scatter_c(x, axis):
            cut = lambda k: half_of(x, k, axis, nc)
            sent = jnp.stack([cut(ci ^ 1), cut(ci ^ 3)]).astype(BF)
            got = pc(sent, 1).astype(F32)
            far = (cut(ci ^ 2) + got[1]).astype(BF)
            return cut(ci) + got[0] + pc(far, 2).astype(F32)

        if nf == 2:
            half = depth // 2
            near_send = jnp.concatenate(
                [half_of(w, core, 0, 2) for w in (w_query, w_key, w_value)], axis=1
            )
            near_send, w_in, w_out = gate(near_send, w_in, w_out)
            near_w = px(near_send)
            near_w, w_attn_out = gate(near_w, w_attn_out)
            over_w = pc(near_w, 1)
            weights = (w_query, w_key, w_value, near_w, over_w)
            weight_specs = [whole((depth, cols))] * 3 + [whole((half, 3 * cols))] * 2
            w_scratch = [pltpu.VMEM((2 * depth, 3 * cols), BF)]
        else:
            full_w = lax.all_gather(
                jnp.concatenate([w_query, w_key, w_value], axis=1), "fsdp", axis=0, tiled=True
            )
            weights = (full_w,)
            weight_specs = [whole(full_w.shape)]
            w_scratch = []

        fc = w_in.shape[1] // nc
        pack = jnp.stack([half_of(w_in, ci, 1, nc), half_of(w_out, ci, 0, nc).T])
        packs = lax.all_gather(pack, ("tensor", "fsdp"), axis=0, tiled=False)
        packs = packs.reshape(nt, nf, 2, depth, fc)

        o_blocks = [w_attn_out] + [pz(w_attn_out, j) for j in range(1, nt)]
        o_over = []

        normed = call(
            norm_kernel,
            (trees,),
            [
                row_1,
                row_1,
                pl.BlockSpec((1, rows, width), lambda t: (t, 0, 0)),
                pl.BlockSpec((1, each, width), lambda t: (t, 0, 0)),
            ],
            pl.BlockSpec((1, tall, width), lambda t: (t, 0, 0)),
            sds((trees, tall, width), BF),
            prefetch=0,
            name="norm",
            us=5,
        )(gain_1, shift_1, tokens, state)
        tile = tall // 3
        queries, kv = call(
            project_kernel,
            (trees, 3),
            [pl.BlockSpec((1, tile, width), lambda t, i, *_: (t, i, 0))] + weight_specs,
            (
                pl.BlockSpec((1, tile, cols), lambda t, i, *_: (t, i, 0)),
                pl.BlockSpec((1, tile, 2 * cols), lambda t, i, *_: (t, i, 0)),
            ),
            (sds((trees, tall, cols), BF), sds((trees, tall, 2 * cols), BF)),
            w_scratch,
            name="project",
        )(pos, normed, *weights)
        kv_y = pc(kv, 2)
        kv_c = pc(kv, 1)
        grad_low = half_of(cotangent, zi, 1, nt).reshape(mine, width)
        kv_y, grad_low, *o_blocks = gate(kv_y, grad_low, *o_blocks)
        kv_cy = pc(kv_y, 1)
        if nf == 2:
            o_over = [px(jnp.stack(o_blocks))]
        else:
            full = lax.all_gather(jnp.stack(o_blocks), "fsdp", axis=2, tiled=True)
            o_blocks = [full[j] for j in range(nt)]
        grad_y = pc(grad_low, 2)
        grad_c = pc(grad_low, 1)

        forward, backward = attention_calls(
            trees, heads, local_segs, all_segs, seg, each, head_dim, nt
        )
        tables = (parent, seg_length, pos, rel_bias)
        sources = (queries, kv, kv_c, kv_y, kv_cy, kv, kv_c, kv_y, kv_cy)
        *att_send, log_total = forward(*tables, *sources)
        quarter = jnp.concatenate(
            [half_of(w, ci, 0, nc) for w in (w_query, w_key, w_value)], axis=1
        )
        att_send[0], quarter = gate(att_send[0], quarter)
        all_q = lax.all_gather(quarter, ("tensor", "fsdp"), axis=0, tiled=False)

        att = [att_send[0]] + [pz(att_send[j], j) for j in range(1, nt)]
        att[1], grad_y, *o_over = gate(att[1], grad_y, *o_over)
        grad_rows = [grad_low, grad_y, grad_c, pc(grad_y, 1)]
        chunk = whole((trees, zr, width))
        chunk_z = pl.BlockSpec((trees, zr, width), lambda i, pos: (0, pos[1], 0))
        small = whole((trees, zr, cols))
        o_all = tuple(o_blocks) + tuple(o_over)
        o_specs = [whole(o.shape) for o in o_all]
        o_scratch = [pltpu.VMEM((nt * cols, width), BF)]
        hidden, normed_two, stat_a = call(
            functools.partial(mix_kernel, nt),
            (1,),
            [small] * nt + o_specs + [chunk_z, row_1, row_1, row_1],
            (chunk, chunk, stat_spec),
            (sds((trees, zr, width), F32), sds((trees, zr, width), BF), stat),
            o_scratch
            + [pltpu.VMEM((mine, nt * cols), BF), pltpu.VMEM((mine, width), F32)],
            name="mix",
            keep=True,
        )(pos, *att, *o_all, tokens, cell, gain_2, shift_2)

        rows_two = normed_two.reshape(mine, width)
        rows_y = pc(rows_two, 2)
        rows_c = pc(rows_two, 1)
        block = whole((mine, width))
        units = nt * fc
        half_spec = whole((2, mine, width))
        half_sds, full_sds = sds((2, mine, width), BF), sds((2, mine, units), BF)
        unit_spec = pl.BlockSpec((2, mine, fc), lambda z, *_: (0, 0, z))
        pack_spec = pl.BlockSpec((1,) + packs.shape[1:], lambda z, *_: (z, 0, 0, 0, 0))
        feed = call(
            ff_kernel,
            (nt,),
            [block] * 4 + [pack_spec],
            (block, block, unit_spec, unit_spec),
            (sds((mine, width), BF), sds((mine, width), BF), full_sds, full_sds),
            [pltpu.VMEM((2, mine, width), F32)] + [pltpu.VMEM((2, mine, width), BF)] * 2,
            prefetch=0,
            vmem=32,
            name="feed",
            keep=True,
            us=9,
        )
        gn_own, gn_c, act_a, gup_a = feed(rows_two, rows_c, grad_rows[0], grad_rows[2], packs)
        rows_y, gn_own, gn_c = gate(rows_y, gn_own, gn_c)
        rows_cy = pc(rows_y, 1)
        gn_got = [pc(gn_c, 1)]
        gn_y, gn_cy, act_b, gup_b = feed(rows_y, rows_cy, grad_rows[1], grad_rows[3], packs)
        ff_rows = [rows_two, rows_c, rows_y, rows_cy]
        cot_rows = [grad_rows[0], grad_rows[2], grad_rows[1], grad_rows[3]]
        gn_got.append(pc(gn_cy, 1))
        gn_mid = (gn_y.astype(F32) + gn_got[1].astype(F32)).astype(BF)
        gn_mid, gn_got[0], act_b, gup_b = gate(gn_mid, gn_got[0], act_b, gup_b)
        gn_end = pc(gn_mid, 2)
        ff_sent, ff_near, ff_far = call(
            ff_grad_kernel,
            (nt,),
            [block] * 8 + [unit_spec] * 4 + [pack_spec],
            (
                pl.BlockSpec((nf, 1, 2, depth, fc), lambda z, *_: (0, z, 0, 0, 0)),
                half_spec,
                half_spec,
            ),
            (sds((nf, nt, 2, depth, fc), BF), half_sds, half_sds),
            [
                pltpu.VMEM((2, 4 * mine, width), BF),
                pltpu.VMEM((4 * mine, width), F32),
                pltpu.VMEM((width, fc), BF),
                pltpu.VMEM((2, 4 * mine, fc), BF),
            ],
            prefetch=0,
            vmem=56,
            name="feed_grads",
            keep=True,
            us=16,
        )(*ff_rows, *cot_rows, act_a, gup_a, act_b, gup_b, packs)
        gn_end, ff_sent, ff_near, ff_far, all_q = gate(gn_end, ff_sent, ff_near, ff_far, all_q)
        ff_got = pc(ff_far, 1)

        grad_hidden, grad_branch, *rest = call(
            functools.partial(branch_back_kernel, nt),
            (1,),
            o_specs + [chunk] * 4 + [chunk_z, row_1, row_1],
            (chunk, chunk) + (small,) * nt + (stat_spec,),
            (sds((trees, zr, width), F32), sds((trees, zr, width), BF))
            + (sds((trees, zr, cols), BF),) * nt
            + (stat,),
            o_scratch,
            name="branch_back",
            keep=True,
        )(
            pos,
            *o_all,
            gn_own.reshape(trees, zr, width),
            gn_got[0].reshape(trees, zr, width),
            gn_end.reshape(trees, zr, width),
            hidden,
            cotangent,
            cell,
            gain_2,
        )
        stat_b = rest.pop()
        ff_got, grad_branch, *rest = gate(ff_got, grad_branch, *rest)
        all_q, rest[0] = gate(all_q, rest[0])
        all_y = pc(all_q, 2)
        grad_heads = [rest[0]] + [ps(rest[j], j) for j in range(1, nt)]
        ff_mid = (ff_near[1].astype(F32) + ff_got[1].astype(F32)).astype(BF)
        ff_end = pc(ff_mid, 2)
        o_rows = cols // nc
        att_specs = (whole((2, nt, o_rows, width)),) + (whole((nt, o_rows, width)),) * 2
        attn_far, attn_mid, attn_near = call(
            functools.partial(attn_grad_kernel, nt),
            (1,),
            [whole((trees, zr, cols))] * nt + [whole((trees, zr, width))],
            att_specs,
            (
                sds((2, nt, o_rows, width), BF),
                sds((nt, o_rows, width), F32),
                sds((nt, o_rows, width), F32),
            ),
            [pltpu.VMEM((cols, width), F32), pltpu.VMEM((nt, mine, cols), BF)],
            name="attn_grads",
            us=4,
        )(pos, *att, grad_branch)

        mlp_out = ff_near[0].astype(F32) + ff_got[0].astype(F32) + ff_end.astype(F32)
        result = (hidden.reshape(mine, width) + mlp_out).astype(BF)
        result, attn_near, attn_mid, attn_far, *grad_heads = gate(
            result, attn_near, attn_mid, attn_far, *grad_heads
        )
        result = result.reshape(trees, zr, width)

        def spread_near(x):
            if nt == 4:
                return [
                    lax.ppermute(x, "tensor", [(0, 1), (1, 2), (2, 3)]),
                    lax.ppermute(x, "tensor", [(1, 0), (2, 1), (3, 2)]),
                ]
            return [pz(x, 1), pz(x, nt - 1)]

        def ordered(blocks, places, sizes):
            n = blocks[0].shape[1]
            return call(
                functools.partial(order_kernel, sizes),
                (trees,),
                [pl.BlockSpec((1, n, width), lambda t, *_: (t, 0, 0))] * len(blocks),
                tuple(
                    pl.BlockSpec((1, nt * m, width), lambda t, *_: (t, 0, 0)) for m in sizes
                ),
                tuple(sds((trees, nt * m, width), BF) for m in sizes),
                name="order",
                us=1,
            )(jnp.stack(places).astype(jnp.int32), *blocks)

        def swap(x, pairs):
            return lax.ppermute(x, "tensor", pairs + [(b, a) for a, b in pairs])

        first_at = [jnp.maximum(zi - 1, 0), jnp.minimum(zi + 1, nt - 1), zi]

        out_near = spread_near(result)
        attn_got = pc(attn_far, 1)

        *dq_send, grad_q, kv_near, kv_far, bias_rows = backward(
            *tables, *sources, *grad_heads, log_total
        )
        ff_half = lax.psum_scatter(ff_sent, "fsdp", scatter_dimension=0, tiled=True)[0]
        ff_half = ff_half.reshape(nt, 2 * depth, fc)
        kv_far, kv_near, attn_got, all_y, *out_near = gate(
            kv_far, kv_near, attn_got, all_y, *out_near
        )
        kv_got = pc(kv_far, 1)
        kv_mid = (kv_near[1].astype(F32) + kv_got[1].astype(F32)).astype(BF)
        own = lax.psum_scatter(ff_half, "tensor", scatter_dimension=0, tiled=True)[0]
        kv_mid, result, attn_got, attn_near, attn_mid, all_q, all_y = gate(
            kv_mid, result, attn_got, attn_near, attn_mid, all_q, all_y
        )
        all_w = [all_q, all_y, pc(all_q, 1), pc(all_y, 1)]
        kv_end = pc(kv_mid, 2)
        if nt == 4:
            out_far = [swap(result, [(0, 2), (1, 3)])]
            out_far.append(
                lax.ppermute(out_far[0], "tensor", [(2, 3), (1, 0), (3, 2), (0, 1)])
            )
        else:
            out_far = [pz(result, j) for j in range(2, nt - 1)]
        attn_two = jnp.stack([attn_near, attn_mid]) + attn_got.astype(F32)
        attn_two = scatter_f(attn_two, 3)
        attn_end = pc(attn_two[1].astype(BF), 2)
        kv_end, attn_two, attn_end, all_w, out_far[0] = gate(
            kv_end, attn_two, attn_end, all_w, out_far[0]
        )
        attn_sum = (attn_two[0] + attn_end.astype(F32)).astype(BF)
        attn_sum = lax.dynamic_slice_in_dim(
            jnp.concatenate([attn_sum, attn_sum], axis=0), nt - zi, nt, 0
        )
        attn_own = lax.psum_scatter(attn_sum, "tensor", scatter_dimension=0, tiled=True)[0]
        five = pl.BlockSpec((1, 1, 1, tall, cols), lambda t, k, *_: (0, k, t, 0, 0))
        four = pl.BlockSpec((1, 1, tall, cols), lambda t, k, *_: (k, t, 0, 0))
        send = pl.BlockSpec((3, 1, zr + zs, cols), lambda t, k, *_: (0, t, 0, 0))
        grad_kv, *kv_send = call(
            functools.partial(combine_kernel, rows),
            (trees, 2),
            [five, five, four]
            + [pl.BlockSpec((1, zr, cols), lambda t, k, *_: (t, 0, 0))] * nt,
            (four,) + (send,) * nt,
            (sds((2, trees, tall, cols), BF),) + (sds((3, trees, zr + zs, cols), BF),) * nt,
            name="combine",
            keep=True,
        )(pos, kv_near, kv_got, kv_end, *dq_send)
        dqkv = [kv_send[0]] + [pz(kv_send[j], j) for j in range(1, nt)]

        dq_rows = depth // nc
        cut_specs = (whole((2, nf, dq_rows, 3 * cols)),) + (whole((nf, dq_rows, 3 * cols)),) * 2
        qkv_far, qkv_mid, qkv_own = call(
            functools.partial(qkv_grad_kernel, nf),
            (trees,),
            [
                pl.BlockSpec((1, tall, width), lambda t, *_: (t, 0, 0)),
                pl.BlockSpec((1, rows, cols), lambda t, *_: (t, 0, 0)),
                pl.BlockSpec((2, 1, tall, cols), lambda t, *_: (0, t, 0, 0)),
            ],
            cut_specs,
            (
                sds((2, nf, dq_rows, 3 * cols), BF),
                sds((nf, dq_rows, 3 * cols), F32),
                sds((nf, dq_rows, 3 * cols), F32),
            ),
            [pltpu.VMEM((nf * depth, 3 * cols), F32), pltpu.VMEM((tall, 3 * cols), BF)],
            name="qkv_grads",
            keep=True,
            us=8,
        )(pos, normed, grad_q, grad_kv)
        if nt == 4:
            places = first_at + [zi ^ 2, 3 - zi]
            blocks = [out_near[0], out_near[1], result, *out_far]
        else:
            blocks = [result, *out_near, *out_far]
            places = [zi, (zi + 1) % nt, (zi - 1) % nt] + [(zi + j) % nt for j in range(2, nt - 1)]
        (output,) = ordered(blocks, places, (zr,))
        own_y = pc(own, 2)
        qkv_mid, qkv_own, qkv_far, own_y, output, *dqkv = gate(
            qkv_mid, qkv_own, qkv_far, own_y, output, *dqkv
        )
        qkv_got = pc(qkv_far, 1)
        own_blocks = (own, own_y, pc(own, 1), pc(own_y, 1))

        chunk_sz = pl.BlockSpec((trees, zs, width), lambda i, pos: (0, pos[1], 0))
        grads_own, stat_c = call(
            functools.partial(input_back_kernel, nt),
            (1,),
            [whole((3, trees, zr + zs, cols))] * nt
            + [whole(all_q.shape)] * 4
            + [chunk_z, chunk_sz, chunk, row_1],
            (whole((trees, zr + zs, width)), stat_spec),
            (sds((trees, zr + zs, width), BF), stat),
            [
                pltpu.VMEM((nt, nf * depth, 3 * cols), BF),
                pltpu.VMEM((nt, trees * (zr + zs), 3 * cols), BF),
                pltpu.VMEM((trees * (zr + zs), width), F32),
            ],
            vmem=44,
            name="input_back",
            keep=True,
        )(pos, *dqkv, *all_w, tokens, state, grad_hidden, gain_1)
        grads_own, qkv_got, *own_blocks = gate(grads_own, qkv_got, *own_blocks)
        qkv_got = qkv_got.astype(F32)

        bias_own = jnp.sum(bias_rows, axis=2)
        bias_all = lax.dynamic_update_slice(
            jnp.zeros((heads * nt, BUCKETS), F32), bias_own, (zi * heads, 0)
        )
        squares = jnp.stack([jnp.sum(stat_a[0]), jnp.sum(stat_a[1]), jnp.sum(mlp_out * mlp_out)])
        spare = jnp.zeros((2 * width - bias_all.size - 3,), F32)
        early = jnp.concatenate(
            [
                stat_b[:2],
                jnp.concatenate([bias_all.reshape(-1), squares, spare]).reshape(2, width),
            ],
            axis=0,
        )
        early, grads_own = gate(early, grads_own)
        sums = jnp.concatenate([stat_c[:2], early], axis=0)

        in_near = spread_near(grads_own)
        *in_near, sums, attn_own, qkv_got = gate(*in_near, sums, attn_own, qkv_got)
        qkv_end = pc((qkv_mid + qkv_got[1]).astype(BF), 2)
        if nt == 4:
            c = swap(grads_own, [(0, 2), (1, 3)])
            d = lax.ppermute(c, "tensor", [(2, 3), (1, 0), (3, 2), (0, 1)])
            places = first_at + [zi ^ 2, 3 - zi]
            blocks = [in_near[0], in_near[1], grads_own, c, d]
        else:
            in_far = [pz(grads_own, j) for j in range(2, nt - 1)]
            blocks = [grads_own, *in_near, *in_far]
        tokens_grad, state_grad = ordered(blocks, places, (zr, zs))
        sums = sums + px(sums) if nf == 2 else lax.psum(sums, "fsdp")
        sums = sums + pc(sums, 1)
        sums = sums + pc(sums, 2)
        if nt & (nt - 1):
            sums = lax.psum(sums, "tensor")
        else:
            k = 1
            while k < nt:
                sums = sums + lax.ppermute(sums, "tensor", [(a, a ^ k) for a in range(nt)])
                k = 2 * k

        qkv_sum = scatter_f(qkv_own + qkv_got[0] + qkv_end.astype(F32), 0)[0].astype(BF)
        if depth % o_rows == 0 and depth * o_rows % dq_rows == 0 and nf == 2:
            folded = jnp.concatenate([attn_own[:, :fc], attn_own[:, fc:]], axis=0)
            qkv_sum = jnp.concatenate([qkv_sum, folded], axis=1)
        else:
            attn_full = gather_c(attn_own, 0).astype(F32)
            folded = None
        qkv_y = pc(qkv_sum, 2)
        qkv_blocks = (qkv_sum, qkv_y, pc(qkv_sum, 1), pc(qkv_y, 1))
        last_shapes = ((depth, cols),) * 3
        if folded is not None:
            last_shapes += ((nc * o_rows, depth),)
        *grad_qkv, grad_attn_out = call(
            finish_qkv_kernel,
            (1,),
            [whole(qkv_sum.shape)] * 4,
            tuple(whole(v) for v in last_shapes),
            tuple(sds(v, F32) for v in last_shapes),
            name="finish_qkv",
            us=0,
        )(pos, *qkv_blocks) + (() if folded is not None else (attn_full,))
        grad_in, grad_out = call(
            finish_ff_kernel,
            (1,),
            [whole(own.shape)] * 4,
            (whole((depth, nc * fc)), whole((nc * fc, depth))),
            (sds((depth, nc * fc), F32), sds((nc * fc, depth), F32)),
            name="finish_ff",
            us=0,
        )(pos, *own_blocks)
        last = sums[4:].reshape(-1)
        bias_sum = last[: bias_all.size].reshape(bias_all.shape)
        grad_bias = lax.dynamic_slice_in_dim(bias_sum, zi * heads, heads, 0)
        cell_count = trees * rows * width * nf * nc
        norms = jnp.sqrt(last[bias_all.size : bias_all.size + 3] / cell_count)
        return (
            output,
            tokens_grad,
            state_grad,
            *grad_qkv,
            grad_attn_out,
            grad_bias,
            sums[0],
            sums[1],
            sums[2],
            sums[3],
            grad_in,
            grad_out,
            norms,
        )

    return on_device


def solution(mesh):
    return jax.shard_map(
        build(mesh),
        mesh=mesh,
        in_specs=(
            P("fsdp", "context", None),
            P("fsdp", "context", None),
            P("fsdp", None),
            P("fsdp", "context"),
            P(),
            P(),
            P(),
            P("fsdp", "tensor"),
            P("fsdp", "tensor"),
            P("fsdp", "tensor"),
            P("tensor", "fsdp"),
            P("tensor", None),
            P(),
            P(),
            P("fsdp", "tensor"),
            P("tensor", "fsdp"),
            P("fsdp", "context", None),
        ),
        out_specs=(
            P("fsdp", "context", None),
            P("fsdp", "context", None),
            P("fsdp", "context", None),
            P("fsdp", "tensor"),
            P("fsdp", "tensor"),
            P("fsdp", "tensor"),
            P("tensor", "fsdp"),
            P("tensor", None),
            P(),
            P(),
            P(),
            P(),
            P("fsdp", "tensor"),
            P("tensor", "fsdp"),
            P(),
        ),
        check_vma=False,
    )
```
